32 devices in a mesh: dp: 16 (over z, x, core), head: 2 (over y).
Axes of the slice: x: 2, y: 2, z: 4, core: 2. Of those that a mesh axis runs over, the one named last changes fastest.
Arguments:
- tokens: bfloat16 [4, 8192, 768], P(None, 'dp'), may hold values from -6 to 6
- live: int32 [4, 8192], P(None, 'dp'), may hold values from 0 to 1, as said below
- bucket: int32 [4], replicated, may hold values from 64 to 512, as said below
- query_weight: bfloat16 [768, 768], P('dp', 'head'), may hold values from -0.21875 to 0.21875
- key_weight: bfloat16 [768, 768], P('dp', 'head'), may hold values from -0.21875 to 0.21875
- value_weight: bfloat16 [768, 768], P('dp', 'head'), may hold values from -0.21875 to 0.21875
- output_weight: bfloat16 [768, 768], P('head', 'dp'), may hold values from -0.875 to 0.875
- inner_weight: bfloat16 [768, 3072], P('dp', 'head'), may hold values from -0.21875 to 0.21875
- outer_weight: bfloat16 [3072, 768], P('head', 'dp'), may hold values from -0.109375 to 0.109375
- query_bias_vector: bfloat16 [768], P('head'), may hold values from -3 to 3
- value_bias_vector: bfloat16 [768], P('head'), may hold values from -3 to 3
- output_bias_vector: bfloat16 [768], replicated, may hold values from -3 to 3
- inner_bias_vector: bfloat16 [3072], P('head'), may hold values from -3 to 3
- outer_bias_vector: bfloat16 [768], replicated, may hold values from -3 to 3
- first_norm_scale: bfloat16 [768], replicated, may hold values from 0.099609375 to 1.8984375
- first_norm_bias: bfloat16 [768], replicated, may hold values from -2 to 2
- second_norm_scale: bfloat16 [768], replicated, may hold values from 0.099609375 to 1.8984375
- second_norm_bias: bfloat16 [768], replicated, may hold values from -2 to 2
- query_down_matrix: bfloat16 [768, 8], replicated, may hold values from -0.21875 to 0.21875
- value_down_matrix: bfloat16 [768, 8], replicated, may hold values from -0.21875 to 0.21875
- query_up_matrix: float32 [8, 768], P(None, 'head'), may hold values from -1.2 to 1.2
- value_up_matrix: float32 [8, 768], P(None, 'head'), may hold values from -1.2 to 1.2
- cotangent: bfloat16 [4, 8192, 768], P(None, 'dp'), may hold values from -6 to 6
Outputs:
- activations: bfloat16 [4, 8192, 768], P(None, 'dp')
- input_grad: bfloat16 [4, 8192, 768], P(None, 'dp')
- lora_query_grad: float32 [8, 768], P(None, 'head')
- lora_value_grad: float32 [8, 768], P(None, 'head')
The draws below stay inside these ranges and needn't reach their ends.
Inputs may be any that keep to these rules, and one draw needn't show every extreme that they name: The four micro-batches take the bucket lengths 512, 256, 128 and 64, each once. The slots of micro-batch m form aligned items of bucket[m] slots; live is 1 on a prefix of each item longer than half of it and 0 after.
All inputs are finite; a program needn't handle non-finite values.
Results may differ from the reference program's by a relative error of at most 0.02.
Values may be sent and summed in bfloat16 or wider, within the bound.
No kernel may reach another device: no remote copies, remote signals or barrier semaphores. Data moves between devices by JAX's collectives and lax.ppermute only.
A program may use at most 192 MiB of HBM per device.

```python
import math
import jax
import jax.numpy as jnp
from jax import lax

MODEL_DIMENSION = 768
HEADS = 12
HEAD_DIM = 64
FF = 3072
ADAPTER_RANK = 8
ALPHA = 16
MICRO = 4
BUCKET_TOP = 512
TOKENS = 8192
N_HEAD = 2


def bucket_order(key):
    return jax.random.permutation(jax.random.fold_in(key, 11), 4).astype(jnp.int32)


def draw_bucket(key, part):
    return (BUCKET_TOP // jnp.left_shift(jnp.int32(1), bucket_order(key))).astype(jnp.int32)


def draw_live(key, part):
    spans = draw_bucket(key, part)[:, None]
    positions = jnp.arange(TOKENS, dtype=jnp.int32)[None, :]
    within = positions % spans
    starts = jnp.broadcast_to(positions - within, (MICRO, TOKENS))
    raw_draw = jax.random.randint(jax.random.fold_in(key, 23), (MICRO, TOKENS), 0, 1 << 20, dtype=jnp.int32)
    picked = jnp.take_along_axis(raw_draw, starts, axis=1)
    lengths = spans // 2 + 1 + picked % (spans // 2)
    return (within < lengths).astype(jnp.int32)


def block_scale(stream_key, shape, pieces, least, largest):
    level, own = 1.0, jax.random.fold_in(stream_key, 6)
    for dim, blocks in pieces:
        draws = jnp.exp(jax.random.uniform(jax.random.fold_in(own, dim), (blocks,), jnp.float32, least / len(pieces), largest / len(pieces)))
        level = level * jnp.repeat(draws, shape[dim] // blocks).reshape([-1 if axis == dim else 1 for axis in range(len(shape))])
    return level


def noise(key, dims, scale, reach, split=(), kind=jnp.bfloat16):
    entries = scale * jax.random.normal(key, dims, jnp.float32)
    if split:
        entries = entries * block_scale(key, dims, split, -0.22, 0.18)
    return jnp.clip(entries, -reach, reach).astype(kind)


def setup_inputs(seed: int = 0) -> dict:
    key_of = jax.random.split(jax.random.key(seed), 24)
    tokens = noise(key_of[0], (MICRO, TOKENS, MODEL_DIMENSION), 1.0, 6.0, ((1, 16),))
    live = draw_live(jax.random.fold_in(key_of[23], 71), 0)
    bucket = draw_bucket(jax.random.fold_in(key_of[23], 71), 0)
    query_weight = noise(key_of[3], (MODEL_DIMENSION, MODEL_DIMENSION), MODEL_DIMENSION ** -0.5, 0.21875, ((0, 16), (1, 2)))
    key_weight = noise(key_of[4], (MODEL_DIMENSION, MODEL_DIMENSION), MODEL_DIMENSION ** -0.5, 0.21875, ((0, 16), (1, 2)))
    value_weight = noise(key_of[5], (MODEL_DIMENSION, MODEL_DIMENSION), MODEL_DIMENSION ** -0.5, 0.21875, ((0, 16), (1, 2)))
    output_weight = noise(key_of[6], (MODEL_DIMENSION, MODEL_DIMENSION), (MODEL_DIMENSION // 16) ** -0.5, 0.875, ((0, 2), (1, 16)))
    inner_weight = noise(key_of[7], (MODEL_DIMENSION, FF), MODEL_DIMENSION ** -0.5, 0.21875, ((0, 16), (1, 2)))
    outer_weight = noise(key_of[8], (FF, MODEL_DIMENSION), FF ** -0.5, 0.109375, ((0, 2), (1, 16)))
    query_bias_vector = noise(key_of[9], (MODEL_DIMENSION,), 0.5, 3.0, ((0, 2),))
    value_bias_vector = noise(key_of[10], (MODEL_DIMENSION,), 0.5, 3.0, ((0, 2),))
    output_bias_vector = noise(key_of[11], (MODEL_DIMENSION,), 0.5, 3.0)
    inner_bias_vector = noise(key_of[12], (FF,), 0.5, 3.0, ((0, 2),))
    outer_bias_vector = noise(key_of[13], (MODEL_DIMENSION,), 0.5, 3.0)
    first_norm_scale = jnp.clip(1.0 + 0.18 * jax.random.normal(key_of[14], (MODEL_DIMENSION,), jnp.float32), 0.099609375, 1.8984375).astype(jnp.bfloat16)
    first_norm_bias = noise(key_of[15], (MODEL_DIMENSION,), 0.3, 2.0)
    second_norm_scale = jnp.clip(1.0 + 0.18 * jax.random.normal(key_of[16], (MODEL_DIMENSION,), jnp.float32), 0.099609375, 1.8984375).astype(jnp.bfloat16)
    second_norm_bias = noise(key_of[17], (MODEL_DIMENSION,), 0.3, 2.0)
    query_down_matrix = noise(key_of[18], (MODEL_DIMENSION, ADAPTER_RANK), MODEL_DIMENSION ** -0.5, 0.21875)
    value_down_matrix = noise(key_of[19], (MODEL_DIMENSION, ADAPTER_RANK), MODEL_DIMENSION ** -0.5, 0.21875)
    query_up_matrix = noise(key_of[20], (ADAPTER_RANK, MODEL_DIMENSION), 0.2, 1.2, ((1, 2),), jnp.float32)
    value_up_matrix = noise(key_of[21], (ADAPTER_RANK, MODEL_DIMENSION), 0.2, 1.2, ((1, 2),), jnp.float32)
    cotangent = noise(key_of[22], (MICRO, TOKENS, MODEL_DIMENSION), 1.0, 6.0, ((1, 16),))
    return {"tokens": tokens, "live": live, "bucket": bucket, "query_weight": query_weight, "key_weight": key_weight, "value_weight": value_weight, "output_weight": output_weight, "inner_weight": inner_weight, "outer_weight": outer_weight, "query_bias_vector": query_bias_vector, "value_bias_vector": value_bias_vector, "output_bias_vector": output_bias_vector, "inner_bias_vector": inner_bias_vector, "outer_bias_vector": outer_bias_vector, "first_norm_scale": first_norm_scale, "first_norm_bias": first_norm_bias, "second_norm_scale": second_norm_scale, "second_norm_bias": second_norm_bias, "query_down_matrix": query_down_matrix, "value_down_matrix": value_down_matrix, "query_up_matrix": query_up_matrix, "value_up_matrix": value_up_matrix, "cotangent": cotangent}


@jax.custom_vjp
def low(v):
    return lax.optimization_barrier(v.astype(jnp.bfloat16)).astype(jnp.float32)

@jax.custom_vjp
def low_back(v):
    return v

def low_keep(v):
    return (low(v), None)

def low_pass(kept, grad):
    return (grad,)

def back_keep(v):
    return (v, None)

def back_low(kept, grad):
    return (low(grad),)
low.defvjp(low_keep, low_pass)
low_back.defvjp(back_keep, back_low)
eps_norm = 1e-05
masked_score = -1000000000.0
highest = lax.Precision.HIGHEST

def precise_product(left, right):
    return jnp.dot(left, right, precision=highest, preferred_element_type=jnp.float32)

def norm_rows(rows_in, gain, shift):
    center = rows_in - lax.optimization_barrier(jnp.mean(rows_in, axis=-1, keepdims=True))
    spread = lax.optimization_barrier(jnp.mean(center * center, axis=-1, keepdims=True))
    return center * lax.rsqrt(spread + eps_norm) * gain + shift

def layer_forward_pass(block_token_rows, query_adapter_rows, value_adapter_rows, permitted_mask, fixed_parameters):
    query_weight, key_weight, value_weight, output_weight, inner_weight, outer_weight, query_bias_vector, value_bias_vector, output_bias_vector, inner_bias_vector, outer_bias_vector, first_norm_scale, first_norm_bias, second_norm_scale, second_norm_bias, query_down_matrix, value_down_matrix = fixed_parameters
    rows_count = block_token_rows.shape[0]
    group = HEADS // N_HEAD
    width = MODEL_DIMENSION // N_HEAD
    hidden = FF // N_HEAD
    adapter_multiplier = ALPHA / ADAPTER_RANK
    inverse = 1.0 / math.sqrt(HEAD_DIM)
    attended = jnp.zeros((rows_count, MODEL_DIMENSION), jnp.float32)
    for index in range(N_HEAD):
        column_count_total = slice(index * width, (index + 1) * width)
        token_group_rows = low_back(block_token_rows)
        query_down_rows = low(precise_product(token_group_rows, query_down_matrix))
        value_down_rows = low(precise_product(token_group_rows, value_down_matrix))
        query_matrix = precise_product(token_group_rows, query_weight[:, column_count_total]) + query_bias_vector[column_count_total] + adapter_multiplier * precise_product(query_down_rows, query_adapter_rows[:, column_count_total])
        query_matrix = low(low_back(query_matrix))
        keys = low(low_back(precise_product(token_group_rows, key_weight[:, column_count_total])))
        value_matrix = precise_product(token_group_rows, value_weight[:, column_count_total]) + value_bias_vector[column_count_total] + adapter_multiplier * precise_product(value_down_rows, value_adapter_rows[:, column_count_total])
        value_matrix = low(low_back(value_matrix))
        query_heads = query_matrix.reshape(rows_count, group, HEAD_DIM)
        key_heads = keys.reshape(rows_count, group, HEAD_DIM)
        value_heads = value_matrix.reshape(rows_count, group, HEAD_DIM)
        scores = jnp.einsum('qhd,khd->hqk', query_heads, key_heads, precision=highest) * inverse
        scores = low_back(scores)
        scores = jnp.where(permitted_mask[None], scores, masked_score)
        probs = low(jax.nn.softmax(scores, axis=-1))
        context = jnp.einsum('hqk,khd->qhd', probs, value_heads, precision=highest).reshape(rows_count, width)
        context = low(low_back(context))
        attended = attended + low(low_back(precise_product(context, output_weight[column_count_total, :])))
    normed = norm_rows(block_token_rows + attended + output_bias_vector, first_norm_scale, first_norm_bias)
    fed = jnp.zeros((rows_count, MODEL_DIMENSION), jnp.float32)
    for index in range(N_HEAD):
        units = slice(index * hidden, (index + 1) * hidden)
        normed_group = low(low_back(normed))
        pre_act = low_back(precise_product(normed_group, inner_weight[:, units]) + inner_bias_vector[units])
        activated = low(jax.nn.gelu(pre_act, approximate=False))
        fed = fed + low(low_back(precise_product(activated, outer_weight[units, :])))
    return norm_rows(normed + fed + outer_bias_vector, second_norm_scale, second_norm_bias)

def reference(tokens, live, bucket, query_weight, key_weight, value_weight, output_weight, inner_weight, outer_weight, query_bias_vector, value_bias_vector, output_bias_vector, inner_bias_vector, outer_bias_vector, first_norm_scale, first_norm_bias, second_norm_scale, second_norm_bias, query_down_matrix, value_down_matrix, query_up_matrix, value_up_matrix, cotangent):
    fixed_parameters = tuple((item.astype(jnp.float32) for item in (query_weight, key_weight, value_weight, output_weight, inner_weight, outer_weight, query_bias_vector, value_bias_vector, output_bias_vector, inner_bias_vector, outer_bias_vector, first_norm_scale, first_norm_bias, second_norm_scale, second_norm_bias, query_down_matrix, value_down_matrix)))
    query_adapter_rows = query_up_matrix.astype(jnp.float32)
    value_adapter_rows = value_up_matrix.astype(jnp.float32)
    per_batch = TOKENS // BUCKET_TOP
    count = MICRO * per_batch
    token_blocks = tokens.astype(jnp.float32).reshape(count, BUCKET_TOP, MODEL_DIMENSION)
    grad_blocks = (cotangent.astype(jnp.float32) * live[:, :, None].astype(jnp.float32)).reshape(count, BUCKET_TOP, MODEL_DIMENSION)
    live_blocks = live.reshape(count, BUCKET_TOP)
    bucket_blocks = jnp.repeat(bucket, per_batch)
    positions = jnp.arange(BUCKET_TOP, dtype=jnp.int32)

    def step(carry, item):
        block_token_rows, block_grad, block_live, block_bucket = item
        segment = positions // block_bucket
        permitted_mask = (segment[:, None] == segment[None, :]) & (block_live[None, :] == 1)

        def forward_pass(first, second, third):
            return layer_forward_pass(first, second, third, permitted_mask, fixed_parameters)
        layer_result, backward_pass = jax.vjp(forward_pass, block_token_rows, query_adapter_rows, value_adapter_rows)
        grad_tokens, query_gradient, value_gradient = backward_pass(block_grad)
        return ((carry[0] + query_gradient, carry[1] + value_gradient), (layer_result.astype(jnp.bfloat16), grad_tokens.astype(jnp.bfloat16)))
    start = (jnp.zeros((ADAPTER_RANK, MODEL_DIMENSION), jnp.float32), jnp.zeros((ADAPTER_RANK, MODEL_DIMENSION), jnp.float32))
    (query_total_sum, value_total_sum), (outputs, grads) = lax.scan(step, start, (token_blocks, grad_blocks, live_blocks, bucket_blocks))
    return (outputs.reshape(MICRO, TOKENS, MODEL_DIMENSION), grads.reshape(MICRO, TOKENS, MODEL_DIMENSION), query_total_sum, value_total_sum)
```

```python
import functools
import math
import jax
import jax.numpy as jnp
from jax import lax
from jax.experimental import pallas as pl
from jax.experimental.pallas import tpu as pltpu
from jax.sharding import PartitionSpec as P

F32, BF16 = jnp.float32, jnp.bfloat16
ALPHA = 16
EPS = 1e-5
MASKED = -1e9
NT = (((1,), (1,)), ((), ()))
TN = (((0,), (0,)), ((), ()))
NN = (((1,), (0,)), ((), ()))


def mm(a, b, dims=NN):
    return lax.dot_general(a, b, dims, preferred_element_type=F32)


def lane_masks():
    lane = lax.broadcasted_iota(jnp.int32, (1, 128), 1)
    one, zero = jnp.ones((1, 128), F32), jnp.zeros((1, 128), F32)
    low = jnp.where(lane < 64, one, zero)
    return low.astype(BF16), (one - low).astype(BF16)


def fwd_kernel(ids, bucket, x_ref, w_ref, addq_ref, addv_ref, live_ref, qkv_ref, p_ref, ctx_ref, bias):
    slots, width = x_ref.shape[1], ctx_ref.shape[2]
    span = bucket[ids[pl.program_id(0)]]

    @pl.when(pl.program_id(1) == 0)
    def _():
        t = lax.broadcasted_iota(jnp.int32, (slots, slots), 0)
        s = lax.broadcasted_iota(jnp.int32, (slots, slots), 1)
        ok = ((t ^ s) < span) & (live_ref[0] == 1)
        bias[...] = jnp.where(ok, 0.0, MASKED)

    x = x_ref[0]
    qkv_ref[0, 0, :, :width] = (mm(x, w_ref[0, :, :width]) + addq_ref[0, 0]).astype(BF16)
    qkv_ref[0, 0, :, width : 2 * width] = mm(x, w_ref[0, :, width : 2 * width]).astype(BF16)
    qkv_ref[0, 0, :, 2 * width :] = (mm(x, w_ref[0, :, 2 * width :]) + addv_ref[0, 0]).astype(BF16)
    masks = lane_masks()

    def attend(size):
        def pair(j, _):
            col = pl.multiple_of(j * 128, 128)
            for b in range(slots // size):
                rows = slice(b * size, (b + 1) * size)
                q2 = qkv_ref[0, 0, rows, pl.ds(col, 128)]
                k2 = qkv_ref[0, 0, rows, pl.ds(width + col, 128)] * jnp.asarray(0.125, BF16)
                v2 = qkv_ref[0, 0, rows, pl.ds(2 * width + col, 128)]
                acc = None
                for e in range(2):
                    s = mm(q2, k2 * masks[e], NT) + bias[rows, rows]
                    s = jnp.exp(s - jnp.max(s, axis=1, keepdims=True))
                    probs = (s * (1.0 / jnp.sum(s, axis=1, keepdims=True))).astype(BF16)
                    p_ref[0, 0, 2 * j + e, rows, :size] = probs
                    part = mm(probs, v2 * masks[e])
                    acc = part if acc is None else acc + part
                ctx_ref[0, rows, pl.ds(col, 128)] = acc.astype(BF16)
            return 0

        lax.fori_loop(0, width // 128, pair, 0)

    @pl.when(span == slots)
    def _():
        attend(slots)

    @pl.when(span != slots)
    def _():
        attend(slots // 2)


def run_fwd(ids, bucket, tokens, wqkv, addq, addv, live):
    n = ids.shape[0]
    _, slots, model = tokens.shape
    half = wqkv.shape[2] // 3
    heads = half // 64
    return pl.pallas_call(
        fwd_kernel,
        out_shape=(
            jax.ShapeDtypeStruct((n, 2, slots, 3 * half), BF16),
            jax.ShapeDtypeStruct((n, 2, heads, slots, slots), BF16),
            jax.ShapeDtypeStruct((n, slots, 2 * half), BF16),
        ),
        grid_spec=pltpu.PrefetchScalarGridSpec(
            num_scalar_prefetch=2,
            grid=(n, 2),
            in_specs=[
                pl.BlockSpec((1, slots, model), lambda i, h, ids, b: (ids[i], 0, 0)),
                pl.BlockSpec((1, model, 3 * half), lambda i, h, ids, b: (h, 0, 0)),
                pl.BlockSpec((1, 1, slots, half), lambda i, h, ids, b: (ids[i], h, 0, 0)),
                pl.BlockSpec((1, 1, slots, half), lambda i, h, ids, b: (ids[i], h, 0, 0)),
                pl.BlockSpec((1, 1, slots), lambda i, h, ids, b: (ids[i], 0, 0)),
            ],
            out_specs=[
                pl.BlockSpec((1, 1, slots, 3 * half), lambda i, h, ids, b: (i, h, 0, 0)),
                pl.BlockSpec((1, 1, heads, slots, slots), lambda i, h, ids, b: (i, h, 0, 0, 0)),
                pl.BlockSpec((1, slots, half), lambda i, h, ids, b: (i, 0, h)),
            ],
            scratch_shapes=[pltpu.VMEM((slots, slots), F32)],
        ),
        compiler_params=pltpu.CompilerParams(vmem_limit_bytes=50 << 20),
        name="attention_forward",
    )(ids, bucket, tokens, wqkv, addq, addv, live.reshape(live.shape[0], 1, slots))


RSQRT2 = 1.0 / math.sqrt(2.0)
PHI0 = 1.0 / math.sqrt(2.0 * math.pi)


def gelu_parts(u):
    cdf = 0.5 * (1.0 + lax.erf(u * RSQRT2))
    pdf = jnp.exp(-0.5 * u * u) * PHI0
    return u * cdf, cdf + u * pdf


def norm(rows):
    c = rows - jnp.mean(rows, axis=1, keepdims=True)
    rstd = lax.rsqrt(jnp.mean(c * c, axis=1, keepdims=True) + EPS)
    return c * rstd, rstd


def norm_back(e, xhat, rstd):
    return rstd * (
        e - jnp.mean(e, axis=1, keepdims=True) - xhat * jnp.mean(e * xhat, axis=1, keepdims=True)
    )


def mid_kernel(
    ids, x_ref, ctx_ref, cot_ref, live_ref, wo_ref, wi_ref, wt_ref, bi_ref, vec_ref,
    act_ref, g1_ref, gctx_ref, slope, xhat, acc, low,
):
    slots, model = x_ref.shape[1], x_ref.shape[2]
    half, hid = wo_ref.shape[2], wi_ref.shape[2]
    step = 512
    bo, b2 = vec_ref[0:1], vec_ref[1:2]
    s1, t1, s2, t2 = vec_ref[2:3], vec_ref[3:4], vec_ref[4:5], vec_ref[5:6]
    r1 = x_ref[0].astype(F32) + bo
    for h in range(2):
        r1 = r1 + mm(ctx_ref[0, :, h * half : (h + 1) * half], wo_ref[h], NT)
    xh, rstd1 = norm(r1)
    xhat[...] = xh
    normed = xh * s1 + t1
    low[...] = normed.astype(BF16)
    acc[...] = normed + b2
    for h in range(2):

        def up(j, _):
            cols = pl.ds(pl.multiple_of(j * step, step), step)
            u = mm(low[...], wi_ref[h, :, cols]) + bi_ref[h, :, cols]
            a, d = gelu_parts(u)
            slope[h, :, cols] = d
            acc[...] += mm(a.astype(BF16), wt_ref[h, :, cols], NT)
            return 0

        lax.fori_loop(0, hid // step, up, 0)
    xh2, rstd2 = norm(acc[...])
    act_ref[0] = (xh2 * s2 + t2).astype(BF16)
    e = cot_ref[0].astype(F32) * live_ref[0].astype(F32) * s2
    g2 = norm_back(e, xh2, rstd2)
    low[...] = g2.astype(BF16)
    acc[...] = g2
    for h in range(2):

        def down(j, _):
            cols = pl.ds(pl.multiple_of(j * step, step), step)
            g = mm(low[...], wt_ref[h, :, cols]) * slope[h, :, cols]
            acc[...] += mm(g.astype(BF16), wi_ref[h, :, cols], NT)
            return 0

        lax.fori_loop(0, hid // step, down, 0)
    g1 = norm_back(acc[...] * s1, xhat[...], rstd1)
    g1_ref[0] = g1
    g1 = g1.astype(BF16)
    for h in range(2):
        gctx_ref[0, :, h * half : (h + 1) * half] = mm(g1, wo_ref[h]).astype(BF16)


def run_mid(ids, tokens, ctx, cot, live, wo, wi, wt, bi, vec):
    n = ids.shape[0]
    _, slots, model = tokens.shape
    half, hid = wo.shape[2], wi.shape[2]
    one = pl.Buffered(1)
    return pl.pallas_call(
        mid_kernel,
        out_shape=(
            jax.ShapeDtypeStruct((n, slots, model), BF16),
            jax.ShapeDtypeStruct((n, slots, model), F32),
            jax.ShapeDtypeStruct((n, slots, model), BF16),
        ),
        grid_spec=pltpu.PrefetchScalarGridSpec(
            num_scalar_prefetch=1,
            grid=(n,),
            in_specs=[
                pl.BlockSpec((1, slots, model), lambda i, ids: (ids[i], 0, 0)),
                pl.BlockSpec((1, slots, model), lambda i, ids: (i, 0, 0)),
                pl.BlockSpec((1, slots, model), lambda i, ids: (ids[i], 0, 0)),
                pl.BlockSpec((1, slots, 1), lambda i, ids: (ids[i], 0, 0)),
                pl.BlockSpec((2, model, half), lambda i, ids: (0, 0, 0), pipeline_mode=one),
                pl.BlockSpec((2, model, hid), lambda i, ids: (0, 0, 0), pipeline_mode=one),
                pl.BlockSpec((2, model, hid), lambda i, ids: (0, 0, 0), pipeline_mode=one),
                pl.BlockSpec((2, 1, hid), lambda i, ids: (0, 0, 0), pipeline_mode=one),
                pl.BlockSpec((8, model), lambda i, ids: (0, 0), pipeline_mode=one),
            ],
            out_specs=[
                pl.BlockSpec((1, slots, model), lambda i, ids: (i, 0, 0)),
                pl.BlockSpec((1, slots, model), lambda i, ids: (i, 0, 0)),
                pl.BlockSpec((1, slots, model), lambda i, ids: (i, 0, 0)),
            ],
            scratch_shapes=[
                pltpu.VMEM((2, slots, hid), F32),
                pltpu.VMEM((slots, model), F32),
                pltpu.VMEM((slots, model), F32),
                pltpu.VMEM((slots, model), BF16),
            ],
        ),
        compiler_params=pltpu.CompilerParams(vmem_limit_bytes=58 << 20),
        name="feed_forward",
    )(ids, tokens, ctx, cot, live.reshape(live.shape[0], slots, 1), wo, wi, wt, bi, vec)


def bwd_kernel(
    ids, bucket, qkv_ref, p_ref, gctx_ref, g1_ref, w_ref, zt_ref, u_ref, d_ref,
    grad_ref, lora_ref, dqkv, total, tlo,
):
    slots, width = gctx_ref.shape[1], gctx_ref.shape[2]
    i, h = pl.program_id(0), pl.program_id(1)
    span = bucket[ids[i]]
    masks = lane_masks()

    def attend(size):
        def pair(j, _):
            col = pl.multiple_of(j * 128, 128)
            for b in range(slots // size):
                rows = slice(b * size, (b + 1) * size)
                q2 = qkv_ref[0, 0, rows, pl.ds(col, 128)] * jnp.asarray(0.125, BF16)
                k2 = qkv_ref[0, 0, rows, pl.ds(width + col, 128)] * jnp.asarray(0.125, BF16)
                v2 = qkv_ref[0, 0, rows, pl.ds(2 * width + col, 128)]
                g2 = gctx_ref[0, rows, pl.ds(col, 128)]
                dq = dk = dv = jnp.zeros((size, 128), F32)
                for e in range(2):
                    probs = p_ref[0, 0, 2 * j + e, rows, :size]
                    dp = mm(g2, v2 * masks[e], NT)
                    dv = dv + mm(probs, g2 * masks[e], TN)
                    p32 = probs.astype(F32)
                    pd = p32 * dp
                    ds = (pd - p32 * jnp.sum(pd, axis=1, keepdims=True)).astype(BF16)
                    dq = dq + mm(ds, k2 * masks[e])
                    dk = dk + mm(ds, q2 * masks[e], TN)
                dqkv[rows, pl.ds(col, 128)] = dq.astype(BF16)
                dqkv[rows, pl.ds(width + col, 128)] = dk.astype(BF16)
                dqkv[rows, pl.ds(2 * width + col, 128)] = dv.astype(BF16)
            return 0

        lax.fori_loop(0, width // 128, pair, 0)

    @pl.when(span == slots)
    def _():
        attend(slots)

    @pl.when(span != slots)
    def _():
        attend(slots // 2)

    part = mm(dqkv[...], w_ref[0], NT)
    tq = mm(dqkv[:, :width], u_ref[0, :16], NT)
    tv = mm(dqkv[:, 2 * width :], u_ref[0, 16:], NT)
    t = jnp.concatenate([tq[:, :8] + tq[:, 8:], tv[:, :8] + tv[:, 8:]], axis=1)
    t_high = t.astype(BF16)
    t_low = (t - t_high.astype(F32)).astype(BF16)
    part = part + mm(jnp.concatenate([t_high, t_low], axis=1), d_ref[...])
    lora_ref[0, 0] = 2.0 * mm(zt_ref[0], dqkv[...])

    @pl.when(h == 0)
    def _():
        total[...] = g1_ref[0] + part

    @pl.when(h == 1)
    def _():
        grad_ref[0] = (total[...] + part).astype(BF16)


def run_bwd(ids, bucket, qkv, probs, gctx, g1, wqkv, zt, up, down):
    n, _, slots, width3 = qkv.shape
    half, model = width3 // 3, g1.shape[2]
    heads = half // 64
    return pl.pallas_call(
        bwd_kernel,
        out_shape=(
            jax.ShapeDtypeStruct((n, slots, model), BF16),
            jax.ShapeDtypeStruct((n, 2, 16, width3), F32),
        ),
        grid_spec=pltpu.PrefetchScalarGridSpec(
            num_scalar_prefetch=2,
            grid=(n, 2),
            in_specs=[
                pl.BlockSpec((1, 1, slots, width3), lambda i, h, ids, b: (i, h, 0, 0)),
                pl.BlockSpec((1, 1, heads, slots, slots), lambda i, h, ids, b: (i, h, 0, 0, 0)),
                pl.BlockSpec((1, slots, half), lambda i, h, ids, b: (i, 0, h)),
                pl.BlockSpec((1, slots, model), lambda i, h, ids, b: (i, 0, 0)),
                pl.BlockSpec((1, model, width3), lambda i, h, ids, b: (h, 0, 0)),
                pl.BlockSpec((1, 16, slots), lambda i, h, ids, b: (ids[i], 0, 0)),
                pl.BlockSpec((1, 32, half), lambda i, h, ids, b: (h, 0, 0)),
                pl.BlockSpec((32, model), lambda i, h, ids, b: (0, 0)),
            ],
            out_specs=[
                pl.BlockSpec((1, slots, model), lambda i, h, ids, b: (i, 0, 0)),
                pl.BlockSpec((1, 1, 16, width3), lambda i, h, ids, b: (i, h, 0, 0)),
            ],
            scratch_shapes=[
                pltpu.VMEM((slots, width3), BF16),
                pltpu.VMEM((slots, model), F32),
                pltpu.VMEM((8, 128), F32),
            ],
        ),
        compiler_params=pltpu.CompilerParams(vmem_limit_bytes=50 << 20),
        name="attention_backward",
    )(ids, bucket, qkv, probs, gctx, g1, wqkv, zt, up, down)


def place_kernel(ids, own_ref, peer_ref, out_ref, sems):
    count = own_ref.shape[0]
    copies = [
        pltpu.make_async_copy(ref.at[i], out_ref.at[ids[k * count + i]], sems.at[k * count + i])
        for k, ref in enumerate((own_ref, peer_ref))
        for i in range(count)
    ]
    for copy in copies:
        copy.start()
    for copy in copies:
        copy.wait()


def place(ids, own, peer):
    count, slots, model = own.shape
    return pl.pallas_call(
        place_kernel,
        out_shape=jax.ShapeDtypeStruct((2 * count, slots, model), own.dtype),
        grid_spec=pltpu.PrefetchScalarGridSpec(
            num_scalar_prefetch=1,
            grid=(),
            in_specs=[pl.BlockSpec(memory_space=pl.ANY)] * 2,
            out_specs=pl.BlockSpec(memory_space=pl.ANY),
            scratch_shapes=[pltpu.SemaphoreType.DMA((2 * count,))],
        ),
        name="place",
    )(ids, own, peer)


SWAP = [(0, 1), (1, 0)]


def shards(
    tokens, live, bucket, query_weight, key_weight, value_weight, output_weight, inner_weight,
    outer_weight, query_bias, value_bias, output_bias, inner_bias, outer_bias, first_scale,
    first_bias, second_scale, second_bias, query_down, value_down, query_up, value_up, cotangent,
):
    micro, slots, model = tokens.shape
    half, hid = query_weight.shape[1], inner_weight.shape[1]
    rank = query_up.shape[0]
    scale = ALPHA / rank
    me = lax.axis_index("head")

    packed = jnp.concatenate(
        [query_weight, key_weight, value_weight, output_weight.T, inner_weight, outer_weight.T], axis=1
    )
    weights = lax.all_gather(packed, ("head", "dp"), axis=0, tiled=True).reshape(2, model, -1)
    wqkv = weights[:, :, : 3 * half]
    wo = weights[:, :, 3 * half : 4 * half]
    wi = weights[:, :, 4 * half : 4 * half + hid]
    wt = weights[:, :, 4 * half + hid :]

    small = jnp.concatenate(
        [query_up, value_up]
        + [b.astype(F32).reshape(-1, half) for b in (query_bias, value_bias, inner_bias)],
        axis=0,
    )
    other = lax.ppermute(small, "head", SWAP)
    both = jnp.where(me == 0, jnp.stack([small, other]), jnp.stack([other, small]))
    uq, uv = both[:, :rank], both[:, rank : 2 * rank]
    bq, bv = both[:, 2 * rank], both[:, 2 * rank + 1]
    bi = both[:, 2 * rank + 2 :].reshape(2, 1, hid)

    down = jnp.concatenate([query_down, value_down], axis=1)
    z = mm(tokens.reshape(-1, model), down).astype(BF16)
    zf = z.astype(F32).reshape(micro, slots, 2 * rank)
    exact = functools.partial(
        jnp.einsum, "mtr,hrc->mhtc", precision=lax.Precision.HIGHEST, preferred_element_type=F32
    )
    addq = scale * exact(zf[..., :rank], uq) + bq[None, :, None, :]
    addv = scale * exact(zf[..., rank:], uv) + bv[None, :, None, :]
    zt = z.reshape(micro, slots, 2 * rank).transpose(0, 2, 1)

    def split(a):
        high = a.astype(BF16)
        return high, (a - high.astype(F32)).astype(BF16)

    up = jnp.concatenate([*split(scale * uq), *split(scale * uv)], axis=1)
    down_t = jnp.concatenate([down.T, down.T], axis=0)
    zero = jnp.zeros((model,), F32)
    vec = jnp.stack(
        [
            a.astype(F32)
            for a in (output_bias, outer_bias, first_scale, first_bias, second_scale, second_bias, zero, zero)
        ]
    )

    order = jnp.argsort(-bucket)
    pairs = jnp.stack([order[jnp.array([0, 3])], order[jnp.array([1, 2])]]).astype(jnp.int32)
    ids, peer_ids = pairs[me], pairs[1 - me]
    where = jnp.concatenate([ids, peer_ids])

    qkv, probs, ctx = run_fwd(ids, bucket, tokens, wqkv, addq, addv, live)
    act, g1, gctx = run_mid(ids, tokens, ctx, cotangent, live, wo, wi, wt, bi, vec)
    peer_act = lax.ppermute(act, "head", SWAP)
    grad, lora = run_bwd(ids, bucket, qkv, probs, gctx, g1, wqkv, zt, up, down_t)
    peer_grad = lax.ppermute(grad, "head", SWAP)
    lora = jnp.sum(lora, axis=0)
    lora = jnp.concatenate([lora[:, :rank, :half], lora[:, rank:, 2 * half :]], axis=2)
    lora = jnp.where(me == 0, lora[0], lora[1]) + lax.ppermute(jnp.where(me == 0, lora[1], lora[0]), "head", SWAP)
    lora = lax.psum(lora, "dp")
    return place(where, act, peer_act), place(where, grad, peer_grad), lora[:, :half], lora[:, half:]


def solution(mesh):
    return jax.shard_map(
        shards,
        mesh=mesh,
        in_specs=(
            P(None, "dp", None), P(None, "dp"), P(),
            P("dp", "head"), P("dp", "head"), P("dp", "head"), P("head", "dp"), P("dp", "head"), P("head", "dp"),
            P("head"), P("head"), P(), P("head"), P(), P(), P(), P(), P(),
            P(), P(), P(None, "head"), P(None, "head"), P(None, "dp", None),
        ),
        out_specs=(P(None, "dp", None), P(None, "dp", None), P(None, "head"), P(None, "head")),
        check_vma=False,
    )
```

```python
import functools
import math

import jax
import jax.numpy as jnp
from jax import lax
from jax.experimental import pallas as pl
from jax.experimental.pallas import tpu as pltpu
from jax.sharding import PartitionSpec as P

F32, BF16 = jnp.float32, jnp.bfloat16
ALPHA = 16
EPS = 1e-5
MASKED = -1e9
NT = (((1,), (1,)), ((), ()))
TN = (((0,), (0,)), ((), ()))
NN = (((1,), (0,)), ((), ()))
SWAP = [(0, 1), (1, 0)]
RSQRT2 = 1.0 / math.sqrt(2.0)
PHI0 = 1.0 / math.sqrt(2.0 * math.pi)
ONCE = pl.Buffered(1)

def mm(a, b, dims=NN):
    return lax.dot_general(a, b, dims, preferred_element_type=F32)


def lane_masks():
    lane = lax.broadcasted_iota(jnp.int32, (1, 128), 1)
    one, zero = jnp.ones((1, 128), F32), jnp.zeros((1, 128), F32)
    low = jnp.where(lane < 64, one, zero)
    return low.astype(BF16), (one - low).astype(BF16)


def fwd_kernel(ids, bucket, x_ref, w_ref, addq_ref, addv_ref, live_ref, qkv_ref, p_ref, ctx_ref, bias):
    slots, width = x_ref.shape[1], ctx_ref.shape[2]
    span = bucket[ids[pl.program_id(0)]]

    @pl.when(pl.program_id(1) == 0)
    def _():
        t = lax.broadcasted_iota(jnp.int32, (slots, slots), 0)
        s = lax.broadcasted_iota(jnp.int32, (slots, slots), 1)
        ok = ((t ^ s) < span) & (live_ref[0] == 1)
        bias[...] = jnp.where(ok, 0.0, MASKED)

    x = x_ref[0]
    qkv_ref[0, 0, :, :width] = (mm(x, w_ref[0, :, :width]) + addq_ref[0, 0]).astype(BF16)
    qkv_ref[0, 0, :, width : 2 * width] = mm(x, w_ref[0, :, width : 2 * width]).astype(BF16)
    qkv_ref[0, 0, :, 2 * width :] = (mm(x, w_ref[0, :, 2 * width :]) + addv_ref[0, 0]).astype(BF16)
    masks = lane_masks()

    def attend(size):
        def pair(j, _):
            col = pl.multiple_of(j * 128, 128)
            for b in range(slots // size):
                rows = slice(b * size, (b + 1) * size)
                q2 = qkv_ref[0, 0, rows, pl.ds(col, 128)]
                k2 = qkv_ref[0, 0, rows, pl.ds(width + col, 128)] * jnp.asarray(0.125, BF16)
                v2 = qkv_ref[0, 0, rows, pl.ds(2 * width + col, 128)]
                acc = None
                for e in range(2):
                    s = mm(q2, k2 * masks[e], NT) + bias[rows, rows]
                    s = jnp.exp(s - jnp.max(s, axis=1, keepdims=True))
                    probs = (s * (1.0 / jnp.sum(s, axis=1, keepdims=True))).astype(BF16)
                    p_ref[0, 0, 2 * j + e, rows, :size] = probs
                    part = mm(probs, v2 * masks[e])
                    acc = part if acc is None else acc + part
                ctx_ref[0, rows, pl.ds(col, 128)] = acc.astype(BF16)
            return 0

        lax.fori_loop(0, width // 128, pair, 0)

    @pl.when(span == slots)
    def _():
        attend(slots)

    @pl.when(span != slots)
    def _():
        attend(slots // 2)


def run_fwd(ids, bucket, tokens, weights, addq, addv, live):
    n = ids.shape[0]
    _, slots, model = tokens.shape
    half = addq.shape[3]
    heads = half // 64
    return pl.pallas_call(
        fwd_kernel,
        out_shape=(
            jax.ShapeDtypeStruct((n, 2, slots, 3 * half), BF16),
            jax.ShapeDtypeStruct((n, 2, heads, slots, slots), BF16),
            jax.ShapeDtypeStruct((n, slots, 2 * half), BF16),
        ),
        grid_spec=pltpu.PrefetchScalarGridSpec(
            num_scalar_prefetch=2,
            grid=(n, 2),
            in_specs=[
                pl.BlockSpec((1, slots, model), lambda i, h, ids, b: (ids[i], 0, 0)),
                pl.BlockSpec((1, model, 3 * half), lambda i, h, ids, b: (h, 0, 0)),
                pl.BlockSpec((1, 1, slots, half), lambda i, h, ids, b: (ids[i], h, 0, 0)),
                pl.BlockSpec((1, 1, slots, half), lambda i, h, ids, b: (ids[i], h, 0, 0)),
                pl.BlockSpec((1, 1, slots), lambda i, h, ids, b: (ids[i], 0, 0)),
            ],
            out_specs=[
                pl.BlockSpec((1, 1, slots, 3 * half), lambda i, h, ids, b: (i, h, 0, 0)),
                pl.BlockSpec((1, 1, heads, slots, slots), lambda i, h, ids, b: (i, h, 0, 0, 0)),
                pl.BlockSpec((1, slots, half), lambda i, h, ids, b: (i, 0, h)),
            ],
            scratch_shapes=[pltpu.VMEM((slots, slots), F32)],
        ),
        compiler_params=pltpu.CompilerParams(vmem_limit_bytes=50 << 20),
        name="attention_forward",
    )(ids, bucket, tokens, weights, addq, addv, live.reshape(live.shape[0], 1, slots))


def gelu_parts(u):
    cdf = 0.5 * (1.0 + lax.erf(u * RSQRT2))
    pdf = jnp.exp(-0.5 * u * u) * PHI0
    return u * cdf, cdf + u * pdf


def norm(rows):
    c = rows - jnp.mean(rows, axis=1, keepdims=True)
    rstd = lax.rsqrt(jnp.mean(c * c, axis=1, keepdims=True) + EPS)
    return c * rstd, rstd


def norm_back(e, xhat, rstd):
    return rstd * (
        e - jnp.mean(e, axis=1, keepdims=True) - xhat * jnp.mean(e * xhat, axis=1, keepdims=True)
    )


def mid_kernel(ids, x_ref, ctx_ref, cot_ref, live_ref, w_hbm, bi_ref, vec_ref, *rest):
    act_ref, full_ref, g1_ref, gctx_ref, wo, wi, wt, slope, xhat, acc, low, hidden, sems = rest[-13:]
    model = x_ref.shape[2]
    half, units = model // 2, wi.shape[1]
    hid, step = units // 2, 768
    copies = []
    for k, (buf, start, cols) in enumerate(
        ((wo, 3 * half, half), (wi, 4 * half, hid), (wt, 4 * half + hid, hid))
    ):
        for h in range(2):
            copies.append(
                pltpu.make_async_copy(
                    w_hbm.at[h, :, start : start + cols],
                    buf.at[:, h * cols : (h + 1) * cols],
                    sems.at[2 * k + h],
                )
            )
    for copy in copies:
        copy.start()
    bo, b2 = vec_ref[0:1], vec_ref[1:2]
    s1, t1, s2, t2 = vec_ref[2:3], vec_ref[3:4], vec_ref[4:5], vec_ref[5:6]
    for copy in copies[:2]:
        copy.wait()
    xh, rstd1 = norm(x_ref[0].astype(F32) + bo + mm(ctx_ref[0], wo[...], NT))
    xhat[...] = xh
    low[...] = (xh * s1 + t1).astype(BF16)
    for copy in copies[2:]:
        copy.wait()

    def up(j, _):
        cols = pl.ds(pl.multiple_of(j * step, step), step)
        a, d = gelu_parts(mm(low[...], wi[:, cols]) + bi_ref[:, cols])
        slope[:, cols] = d
        hidden[:, cols] = a.astype(BF16)
        return 0

    lax.fori_loop(0, units // step, up, 0)
    xh2, rstd2 = norm(mm(hidden[...], wt[...], NT) + (xhat[...] * s1 + t1) + b2)
    act_ref[0] = (xh2 * s2 + t2).astype(BF16)
    full_ref[0] = act_ref[0]
    g2 = norm_back(cot_ref[0].astype(F32) * live_ref[0].astype(F32) * s2, xh2, rstd2)
    low[...] = g2.astype(BF16)
    acc[...] = g2

    def down(j, _):
        cols = pl.ds(pl.multiple_of(j * step, step), step)
        hidden[:, cols] = (mm(low[...], wt[:, cols]) * slope[:, cols]).astype(BF16)
        return 0

    lax.fori_loop(0, units // step, down, 0)
    g1 = norm_back((acc[...] + mm(hidden[...], wi[...], NT)) * s1, xhat[...], rstd1)
    g1_ref[0] = g1
    gctx_ref[0] = mm(g1.astype(BF16), wo[...]).astype(BF16)


def run_mid(pos, ids, tokens, ctx, cot, live, weights, bi, vec, full):
    micro, slots, model = tokens.shape
    units = bi.shape[1]
    own = lambda i, ids: (ids[pos], 0, 0)
    same = lambda i, ids: (0, 0)
    in_specs = [
        pl.BlockSpec((1, slots, model), own),
        pl.BlockSpec((1, slots, model), lambda i, ids: (pos, 0, 0)),
        pl.BlockSpec((1, slots, model), own),
        pl.BlockSpec((1, slots, 1), own),
        pl.BlockSpec(memory_space=pl.ANY),
        pl.BlockSpec((1, units), same, pipeline_mode=ONCE),
        pl.BlockSpec((8, model), same, pipeline_mode=ONCE),
    ]
    args = [ids, tokens, ctx, cot, live.reshape(micro, slots, 1), weights, bi, vec]
    aliases = {}
    if full is not None:
        in_specs.append(pl.BlockSpec(memory_space=pl.ANY))
        args.append(full)
        aliases = {8: 1}
    first = pl.BlockSpec((1, slots, model), lambda i, ids: (0, 0, 0))
    return pl.pallas_call(
        mid_kernel,
        out_shape=(
            jax.ShapeDtypeStruct((1, slots, model), BF16),
            jax.ShapeDtypeStruct(tokens.shape, BF16),
            jax.ShapeDtypeStruct((1, slots, model), F32),
            jax.ShapeDtypeStruct((1, slots, model), BF16),
        ),
        grid_spec=pltpu.PrefetchScalarGridSpec(
            num_scalar_prefetch=1,
            grid=(1,),
            in_specs=in_specs,
            out_specs=[first, pl.BlockSpec((1, slots, model), own), first, first],
            scratch_shapes=[
                pltpu.VMEM((model, model), BF16),
                pltpu.VMEM((model, units), BF16),
                pltpu.VMEM((model, units), BF16),
                pltpu.VMEM((slots, units), F32),
                pltpu.VMEM((slots, model), F32),
                pltpu.VMEM((slots, model), F32),
                pltpu.VMEM((slots, model), BF16),
                pltpu.VMEM((slots, units), BF16),
                pltpu.SemaphoreType.DMA((6,)),
            ],
        ),
        input_output_aliases=aliases,
        compiler_params=pltpu.CompilerParams(vmem_limit_bytes=58 << 20),
        name="feed_forward",
    )(*args)


def bwd_kernel(
    pos, ids, bucket, qkv_ref, p_ref, gctx_ref, g1_ref, w_ref, zt_ref, u_ref, d_ref, *rest
):
    grad_ref, full_ref, lora_ref, dqkv, total = rest[-5:]
    slots, width = gctx_ref.shape[1], gctx_ref.shape[2]
    h = pl.program_id(1)
    span = bucket[ids[pos]]
    masks = lane_masks()

    def attend(size):
        def pair(j, _):
            col = pl.multiple_of(j * 128, 128)
            for b in range(slots // size):
                rows = slice(b * size, (b + 1) * size)
                q2 = qkv_ref[0, 0, rows, pl.ds(col, 128)] * jnp.asarray(0.125, BF16)
                k2 = qkv_ref[0, 0, rows, pl.ds(width + col, 128)] * jnp.asarray(0.125, BF16)
                v2 = qkv_ref[0, 0, rows, pl.ds(2 * width + col, 128)]
                g2 = gctx_ref[0, rows, pl.ds(col, 128)]
                dq = dk = dv = jnp.zeros((size, 128), F32)
                for e in range(2):
                    probs = p_ref[0, 0, 2 * j + e, rows, :size]
                    dp = mm(g2, v2 * masks[e], NT)
                    dv = dv + mm(probs, g2 * masks[e], TN)
                    p32 = probs.astype(F32)
                    pd = p32 * dp
                    ds = (pd - p32 * jnp.sum(pd, axis=1, keepdims=True)).astype(BF16)
                    dq = dq + mm(ds, k2 * masks[e])
                    dk = dk + mm(ds, q2 * masks[e], TN)
                dqkv[rows, pl.ds(col, 128)] = dq.astype(BF16)
                dqkv[rows, pl.ds(width + col, 128)] = dk.astype(BF16)
                dqkv[rows, pl.ds(2 * width + col, 128)] = dv.astype(BF16)
            return 0

        lax.fori_loop(0, width // 128, pair, 0)

    @pl.when(span == slots)
    def _():
        attend(slots)

    @pl.when(span != slots)
    def _():
        attend(slots // 2)

    part = mm(dqkv[...], w_ref[0], NT)
    tq = mm(dqkv[:, :width], u_ref[0, :16], NT)
    tv = mm(dqkv[:, 2 * width :], u_ref[0, 16:], NT)
    t = jnp.concatenate([tq[:, :8] + tq[:, 8:], tv[:, :8] + tv[:, 8:]], axis=1)
    t_high = t.astype(BF16)
    t_low = (t - t_high.astype(F32)).astype(BF16)
    part = part + mm(jnp.concatenate([t_high, t_low], axis=1), d_ref[...])
    lora_ref[0, 0] = 2.0 * mm(zt_ref[0], dqkv[...])

    @pl.when(h == 0)
    def _():
        total[...] = g1_ref[0] + part

    @pl.when(h == 1)
    def _():
        grad_ref[0] = (total[...] + part).astype(BF16)
        full_ref[0] = grad_ref[0]


def run_bwd(pos, ids, bucket, qkv, probs, gctx, g1, weights, zt, up, down, full):
    _, _, slots, width3 = qkv.shape
    micro = zt.shape[0]
    half, model = width3 // 3, g1.shape[2]
    heads = half // 64
    in_specs = [
        pl.BlockSpec((1, 1, slots, width3), lambda i, h, ids, b: (pos, h, 0, 0)),
        pl.BlockSpec((1, 1, heads, slots, slots), lambda i, h, ids, b: (pos, h, 0, 0, 0)),
        pl.BlockSpec((1, slots, half), lambda i, h, ids, b: (0, 0, h)),
        pl.BlockSpec((1, slots, model), lambda i, h, ids, b: (0, 0, 0)),
        pl.BlockSpec((1, model, width3), lambda i, h, ids, b: (h, 0, 0)),
        pl.BlockSpec((1, 16, slots), lambda i, h, ids, b: (ids[pos], 0, 0)),
        pl.BlockSpec((1, 32, half), lambda i, h, ids, b: (h, 0, 0)),
        pl.BlockSpec((32, model), lambda i, h, ids, b: (0, 0)),
    ]
    args = [ids, bucket, qkv, probs, gctx, g1, weights, zt, up, down]
    aliases = {}
    if full is not None:
        in_specs.append(pl.BlockSpec(memory_space=pl.ANY))
        args.append(full)
        aliases = {10: 1}
    return pl.pallas_call(
        functools.partial(bwd_kernel, pos),
        out_shape=(
            jax.ShapeDtypeStruct((1, slots, model), BF16),
            jax.ShapeDtypeStruct((micro, slots, model), BF16),
            jax.ShapeDtypeStruct((1, 2, 16, width3), F32),
        ),
        grid_spec=pltpu.PrefetchScalarGridSpec(
            num_scalar_prefetch=2,
            grid=(1, 2),
            in_specs=in_specs,
            out_specs=[
                pl.BlockSpec((1, slots, model), lambda i, h, ids, b: (0, 0, 0)),
                pl.BlockSpec((1, slots, model), lambda i, h, ids, b: (ids[pos], 0, 0)),
                pl.BlockSpec((1, 1, 16, width3), lambda i, h, ids, b: (0, h, 0, 0)),
            ],
            scratch_shapes=[pltpu.VMEM((slots, width3), BF16), pltpu.VMEM((slots, model), F32)],
        ),
        input_output_aliases=aliases,
        compiler_params=pltpu.CompilerParams(vmem_limit_bytes=50 << 20),
        name="attention_backward",
    )(*args)


def place_kernel(ids, full_ref, piece_ref, out_ref):
    out_ref[...] = piece_ref[...]


def place(pos, ids, full, piece):
    _, slots, model = full.shape
    return pl.pallas_call(
        place_kernel,
        out_shape=jax.ShapeDtypeStruct(full.shape, full.dtype),
        grid_spec=pltpu.PrefetchScalarGridSpec(
            num_scalar_prefetch=1,
            grid=(2,),
            in_specs=[
                pl.BlockSpec(memory_space=pl.ANY),
                pl.BlockSpec((1, slots // 2, model), lambda i, ids: (0, i, 0)),
            ],
            out_specs=pl.BlockSpec((1, slots // 2, model), lambda i, ids: (ids[pos], i, 0)),
        ),
        input_output_aliases={1: 0},
        name="place",
    )(ids, full, piece)


def sum_over_dp(a):
    size = lax.axis_size("dp")
    if size & (size - 1):
        return lax.psum(a, "dp")
    bit = 1
    while bit < size:
        a = a + lax.ppermute(a, "dp", [(i, i ^ bit) for i in range(size)])
        bit *= 2
    return a


def shards(
    tokens, live, bucket, query_weight, key_weight, value_weight, output_weight, inner_weight,
    outer_weight, query_bias, value_bias, output_bias, inner_bias, outer_bias, first_scale,
    first_bias, second_scale, second_bias, query_down, value_down, query_up, value_up, cotangent,
):
    micro, slots, model = tokens.shape
    half, hid = query_weight.shape[1], inner_weight.shape[1]
    rank = query_up.shape[0]
    scale = ALPHA / rank
    me = lax.axis_index("head")

    packed = jnp.concatenate(
        [query_weight, key_weight, value_weight, output_weight.T, inner_weight, outer_weight.T], axis=1
    )
    weights = lax.all_gather(packed, ("head", "dp"), axis=0, tiled=True).reshape(2, model, -1)

    small = jnp.concatenate(
        [query_up, value_up]
        + [b.astype(F32).reshape(-1, half) for b in (query_bias, value_bias, inner_bias)],
        axis=0,
    )
    other = lax.ppermute(small, "head", SWAP)
    both = jnp.where(me == 0, jnp.stack([small, other]), jnp.stack([other, small]))
    uq, uv = both[:, :rank], both[:, rank : 2 * rank]
    bq, bv = both[:, 2 * rank], both[:, 2 * rank + 1]
    bi = both[:, 2 * rank + 2 :].reshape(1, 2 * hid)

    down = jnp.concatenate([query_down, value_down], axis=1)
    z = mm(tokens.reshape(-1, model), down).astype(BF16)
    zf = z.astype(F32).reshape(micro, slots, 2 * rank)
    exact = functools.partial(
        jnp.einsum, "mtr,hrc->mhtc", precision=lax.Precision.HIGHEST, preferred_element_type=F32
    )
    addq = scale * exact(zf[..., :rank], uq) + bq[None, :, None, :]
    addv = scale * exact(zf[..., rank:], uv) + bv[None, :, None, :]
    zt = z.reshape(micro, slots, 2 * rank).transpose(0, 2, 1)

    def split(a):
        high = a.astype(BF16)
        return high, (a - high.astype(F32)).astype(BF16)

    up = jnp.concatenate([*split(scale * uq), *split(scale * uv)], axis=1)
    down_t = jnp.concatenate([down.T, down.T], axis=0)
    zero = jnp.zeros((model,), F32)
    vec = jnp.stack(
        [
            a.astype(F32)
            for a in (output_bias, outer_bias, first_scale, first_bias, second_scale, second_bias, zero, zero)
        ]
    )

    order = jnp.argsort(-bucket)
    pairs = jnp.stack([order[jnp.array([0, 3])], order[jnp.array([1, 2])]]).astype(jnp.int32)
    ids, peer_ids = pairs[me], pairs[1 - me]

    qkv, probs, ctx = run_fwd(ids, bucket, tokens, weights, addq, addv, live)
    acts = grads = lora = None
    from_peer = []
    for pos in range(2):
        act, acts, g1, gctx = run_mid(pos, ids, tokens, ctx, cotangent, live, weights, bi, vec, acts)
        peer_act = lax.ppermute(act, "head", SWAP)
        grad, grads, part = run_bwd(pos, ids, bucket, qkv, probs, gctx, g1, weights, zt, up, down_t, grads)
        peer_grad = lax.ppermute(grad, "head", SWAP)
        lora = part[0] if lora is None else lora + part[0]
        from_peer.append((peer_act, peer_grad))
    lora = jnp.concatenate([lora[:, :rank, :half], lora[:, rank:, 2 * half :]], axis=2)
    mine, other = jnp.where(me == 0, lora, lora[::-1])
    lora = sum_over_dp(mine + lax.ppermute(other, "head", SWAP))
    for pos, (peer_act, peer_grad) in enumerate(from_peer):
        acts, grads = place(pos, peer_ids, acts, peer_act), place(pos, peer_ids, grads, peer_grad)
    return acts, grads, lora[:, :half], lora[:, half:]


def solution(mesh):
    return jax.shard_map(
        shards,
        mesh=mesh,
        in_specs=(
            P(None, "dp", None), P(None, "dp"), P(),
            P("dp", "head"), P("dp", "head"), P("dp", "head"), P("head", "dp"), P("dp", "head"), P("head", "dp"),
            P("head"), P("head"), P(), P("head"), P(), P(), P(), P(), P(),
            P(), P(), P(None, "head"), P(None, "head"), P(None, "dp", None),
        ),
        out_specs=(P(None, "dp", None), P(None, "dp", None), P(None, "head"), P(None, "head")),
        check_vma=False,
    )
```

```python
import functools
import math

import jax
import jax.numpy as jnp
from jax import lax
from jax.experimental import pallas as pl
from jax.experimental.pallas import tpu as pltpu
from jax.sharding import PartitionSpec as P

F32, BF16 = jnp.float32, jnp.bfloat16
ALPHA = 16
EPS = 1e-5
MASKED = -1e9
NT = (((1,), (1,)), ((), ()))
TN = (((0,), (0,)), ((), ()))
NN = (((1,), (0,)), ((), ()))
SWAP = [(0, 1), (1, 0)]
RSQRT2 = 1.0 / math.sqrt(2.0)
PHI0 = 1.0 / math.sqrt(2.0 * math.pi)
ONCE = pl.Buffered(1)
VMEM = 60 << 20


def work(flops):
    return pl.CostEstimate(flops=int(flops), bytes_accessed=8 << 20, transcendentals=0)


def chip_table(size, move):
    deep = size // 4

    def index(z, x, c, y):
        return ((z % deep) * 4 + x * 2 + c) * 2 + y

    return [
        (index(z, x, c, y), index(*move(z, x, c, y)))
        for z in range(deep)
        for x in range(2)
        for c in range(2)
        for y in range(2)
    ]


def by_permutes(size):
    return size == 16


def permuter(size):
    tables = {
        "first": chip_table(size, lambda z, x, c, y: (z, x, c, 1 - y) if c else (z, 1 - x, c, y)),
        "second": chip_table(size, lambda z, x, c, y: (z, 1 - x, c, y) if c else (z, x, c, 1 - y)),
        "ring": chip_table(size, lambda z, x, c, y: (z + 1, x, c, y)),
        "core": chip_table(size, lambda z, x, c, y: (z, x, 1 - c, y)),
    }
    return lambda a, which: lax.ppermute(a, ("dp", "head"), tables[which])


def then(value, done):
    return lax.optimization_barrier((value, done))[0]


def spread_ring(shard, size):
    go, blocks = permuter(size), [shard]
    for _ in range(3):
        blocks.append(go(blocks[-1], "ring"))
    return blocks


def spread_first(blocks, size):
    pair = jnp.stack(blocks)
    return jnp.concatenate([pair, permuter(size)(pair, "first")])


def spread_core(four, far, size):
    eight = jnp.concatenate([four, far])
    return [eight, permuter(size)(eight, "core")]


def gather_whole(shard):
    whole = lax.all_gather(shard, ("head", "dp"), axis=0, tiled=True)
    return [whole.reshape(2, -1, shard.shape[1])]


def sub_pieces(refs, info):
    dp, y = info[8], info[9]
    if len(refs) == 1:
        return [(refs[0].at[h], h, 0) for h in range(2)]
    rows = refs[0].shape[1]
    z, x, core = dp >> 2, (dp >> 1) & 1, dp & 1
    out = []
    for k in range(4):
        deep = ((z + 4 - k) & 3) << 2
        for side in range(2):
            c = core ^ side
            for j in range(4):
                dx, dy = ((0, 0), (1 - c, c), (c, 1 - c), (1, 1))[j]
                row = (deep + ((x ^ dx) << 1) + c) * rows
                view = refs[(k // 2) * 2 + side].at[j * 2 + k % 2]
                out.append((view, y ^ dy, pl.multiple_of(row, rows)))
    return out


def fetch(refs, info, parts, sems):
    subs = sub_pieces(refs, info)
    result = []
    for p, (start, count, dest) in enumerate(parts):
        result.append(
            [
                pltpu.make_async_copy(
                    ref.at[:, pl.ds(start, count)], dest(h, row, ref.shape[0]), sems.at[p * len(subs) + n]
                )
                for n, (ref, h, row) in enumerate(subs)
            ]
        )
    return result


def side_by_side(buf, count):
    return lambda h, row, rows: buf.at[pl.ds(row, rows), pl.ds(pl.multiple_of(h * count, 128), count)]


def stacked(buf):
    return lambda h, row, rows: buf.at[h, pl.ds(row, rows)]


def mm(a, b, dims=NN):
    return lax.dot_general(a, b, dims, preferred_element_type=F32)


def lane_masks():
    lane = lax.broadcasted_iota(jnp.int32, (1, 128), 1)
    one, zero = jnp.ones((1, 128), F32), jnp.zeros((1, 128), F32)
    low = jnp.where(lane < 64, one, zero)
    return low.astype(BF16), (one - low).astype(BF16)


def split(a):
    high = a.astype(BF16)
    return high, (a - high.astype(F32)).astype(BF16)


def fwd_kernel(pos, count, info, x_ref, small_ref, qd_ref, vd_ref, live_ref, *rest):
    pieces, (qkv_ref, p_ref, ctx_ref, z_ref, w, bias, sems) = rest[:count], rest[count:]
    slots, width = x_ref.shape[1], ctx_ref.shape[2]
    span, half = info[4 + info[pos]], pl.program_id(1)

    @pl.when(half == 0)
    def _():
        (copies,) = fetch(pieces, info, [(0, 3 * width, stacked(w))], sems)
        for copy in copies:
            copy.start()
        t = lax.broadcasted_iota(jnp.int32, (slots, slots), 0)
        s = lax.broadcasted_iota(jnp.int32, (slots, slots), 1)
        ok = ((t ^ s) < span) & (live_ref[0] == 1)
        bias[...] = jnp.where(ok, 0.0, MASKED)
        down = jnp.concatenate([qd_ref[...], vd_ref[...]], axis=1)
        z_ref[0] = mm(x_ref[0], down).astype(BF16)
        for copy in copies:
            copy.wait()

    x, z, r = x_ref[0], z_ref[0], small_ref.shape[1] // 2 - 3
    uq, uv = split(2.0 * small_ref[0, :r]), split(2.0 * small_ref[0, r : 2 * r])
    addq = mm(z[:, :r], uq[0]) + mm(z[:, :r], uq[1]) + small_ref[0, 2 * r : 2 * r + 1]
    addv = mm(z[:, r:], uv[0]) + mm(z[:, r:], uv[1]) + small_ref[0, 2 * r + 1 : 2 * r + 2]
    qkv_ref[0, :, :width] = (mm(x, w[half, :, :width]) + addq).astype(BF16)
    qkv_ref[0, :, width : 2 * width] = mm(x, w[half, :, width : 2 * width]).astype(BF16)
    qkv_ref[0, :, 2 * width :] = (mm(x, w[half, :, 2 * width :]) + addv).astype(BF16)
    masks = lane_masks()

    def attend(size):
        def pair(j, _):
            col = pl.multiple_of(j * 128, 128)
            for b in range(slots // size):
                rows = slice(b * size, (b + 1) * size)
                q2 = qkv_ref[0, rows, pl.ds(col, 128)]
                k2 = qkv_ref[0, rows, pl.ds(width + col, 128)] * jnp.asarray(0.125, BF16)
                v2 = qkv_ref[0, rows, pl.ds(2 * width + col, 128)]
                acc = None
                for e in range(2):
                    s = mm(q2, k2 * masks[e], NT) + bias[rows, rows]
                    s = jnp.exp(s - jnp.max(s, axis=1, keepdims=True))
                    probs = (s * (1.0 / jnp.sum(s, axis=1, keepdims=True))).astype(BF16)
                    p_ref[0, 2 * j + e, rows, :size] = probs
                    part = mm(probs, v2 * masks[e])
                    acc = part if acc is None else acc + part
                ctx_ref[0, rows, pl.ds(col, 128)] = acc.astype(BF16)
            return 0

        lax.fori_loop(0, width // 128, pair, 0)

    by_span(pos, span, slots, attend)


def by_span(pos, span, slots, attend):
    if pos == 0:
        pl.when(span == slots)(lambda: attend(slots))
        pl.when(span != slots)(lambda: attend(slots // 2))
    else:
        attend(slots // 2)


def any_spec():
    return pl.BlockSpec(memory_space=pl.ANY)


def sub_count(pieces):
    return sum(p.shape[0] for p in pieces)


def run_fwd(pos, info, tokens, pieces, small, query_down, value_down, live):
    micro, slots, model = tokens.shape
    half = small.shape[2]
    heads, wide = half // 64, slots if pos == 0 else slots // 2
    return pl.pallas_call(
        functools.partial(fwd_kernel, pos, len(pieces)),
        out_shape=(
            jax.ShapeDtypeStruct((2, slots, 3 * half), BF16),
            jax.ShapeDtypeStruct((2, heads, slots, wide), BF16),
            jax.ShapeDtypeStruct((1, slots, model), BF16),
            jax.ShapeDtypeStruct((1, slots, 2 * query_down.shape[1]), BF16),
        ),
        grid_spec=pltpu.PrefetchScalarGridSpec(
            num_scalar_prefetch=1,
            grid=(1, 2),
            in_specs=[
                pl.BlockSpec((1, slots, model), lambda i, h, info: (info[pos], 0, 0)),
                pl.BlockSpec((1, small.shape[1], half), lambda i, h, info: (h, 0, 0)),
                pl.BlockSpec(query_down.shape, lambda i, h, info: (0, 0)),
                pl.BlockSpec(value_down.shape, lambda i, h, info: (0, 0)),
                pl.BlockSpec((1, 1, slots), lambda i, h, info: (info[pos], 0, 0)),
            ]
            + [any_spec() for _ in pieces],
            out_specs=[
                pl.BlockSpec((1, slots, 3 * half), lambda i, h, info: (h, 0, 0)),
                pl.BlockSpec((1, heads, slots, wide), lambda i, h, info: (h, 0, 0, 0)),
                pl.BlockSpec((1, slots, half), lambda i, h, info: (0, 0, h)),
                pl.BlockSpec((1, slots, 2 * query_down.shape[1]), lambda i, h, info: (0, 0, 0)),
            ],
            scratch_shapes=[
                pltpu.VMEM((2, model, 3 * half), BF16),
                pltpu.VMEM((slots, slots), F32),
                pltpu.SemaphoreType.DMA((sub_count(pieces),)),
            ],
        ),
        compiler_params=pltpu.CompilerParams(vmem_limit_bytes=VMEM),
        cost_estimate=work(12e9),
        name="attention_forward",
    )(info, tokens, small, query_down, value_down, live, *pieces)


def gelu_parts(u):
    cdf = 0.5 * (1.0 + lax.erf(u * RSQRT2))
    pdf = jnp.exp(-0.5 * u * u) * PHI0
    return u * cdf, cdf + u * pdf


def norm(rows):
    c = rows - jnp.mean(rows, axis=1, keepdims=True)
    rstd = lax.rsqrt(jnp.mean(c * c, axis=1, keepdims=True) + EPS)
    return c * rstd, rstd


def norm_back(e, xhat, rstd):
    return rstd * (
        e - jnp.mean(e, axis=1, keepdims=True) - xhat * jnp.mean(e * xhat, axis=1, keepdims=True)
    )


def mid_kernel(count, info, x_ref, ctx_ref, cot_ref, live_ref, bi_ref, vec_ref, *rest):
    pieces = rest[:count]
    full_ref, act_ref, g1_ref, gctx_ref, wo, wi, wt, slope, xhat, acc, low, hidden, sems = rest[-13:]
    model = x_ref.shape[2]
    half, units = model // 2, wi.shape[1]
    hid, step = units // 2, 768
    parts = [
        (0, half, side_by_side(wo, half)),
        (half, hid, side_by_side(wi, hid)),
        (half + hid, hid, side_by_side(wt, hid)),
    ]
    copies = fetch(pieces, info, parts, sems)
    for copy in copies[0] + copies[1] + copies[2]:
        copy.start()
    bo, b2 = vec_ref[0:1], vec_ref[1:2]
    s1, t1, s2, t2 = vec_ref[2:3], vec_ref[3:4], vec_ref[4:5], vec_ref[5:6]
    for copy in copies[0]:
        copy.wait()
    xh, rstd1 = norm(x_ref[0].astype(F32) + bo + mm(ctx_ref[0], wo[...], NT))
    xhat[...] = xh
    low[...] = (xh * s1 + t1).astype(BF16)
    for copy in copies[1]:
        copy.wait()

    def up(j, _):
        cols = pl.ds(pl.multiple_of(j * step, step), step)
        a, d = gelu_parts(mm(low[...], wi[:, cols]) + bi_ref[:, cols])
        slope[:, cols] = d
        hidden[:, cols] = a.astype(BF16)
        return 0

    lax.fori_loop(0, units // step, up, 0)
    for copy in copies[2]:
        copy.wait()
    xh2, rstd2 = norm(mm(hidden[...], wt[...], NT) + (xhat[...] * s1 + t1) + b2)
    act_ref[0] = (xh2 * s2 + t2).astype(BF16)
    full_ref[0] = act_ref[0]
    live = jnp.broadcast_to(live_ref[0].astype(F32), (8, live_ref.shape[2])).T[:, :1]
    g2 = norm_back(cot_ref[0].astype(F32) * live * s2, xh2, rstd2)
    low[...] = g2.astype(BF16)
    acc[...] = g2

    def down(j, _):
        cols = pl.ds(pl.multiple_of(j * step, step), step)
        hidden[:, cols] = (mm(low[...], wt[:, cols]) * slope[:, cols]).astype(BF16)
        return 0

    lax.fori_loop(0, units // step, down, 0)
    g1 = norm_back((acc[...] + mm(hidden[...], wi[...], NT)) * s1, xhat[...], rstd1)
    g1_ref[0] = g1
    gctx_ref[0] = mm(g1.astype(BF16), wo[...]).astype(BF16)


def run_mid(pos, info, tokens, ctx, cot, live, pieces, bi, vec, full):
    micro, slots, model = tokens.shape
    units = bi.shape[1]
    own = lambda i, info: (info[pos], 0, 0)
    same = lambda i, info: (0, 0)
    in_specs = [
        pl.BlockSpec((1, slots, model), own),
        pl.BlockSpec((1, slots, model), lambda i, info: (0, 0, 0)),
        pl.BlockSpec((1, slots, model), own),
        pl.BlockSpec((1, 1, slots), own),
        pl.BlockSpec((1, units), same, pipeline_mode=ONCE),
        pl.BlockSpec((8, model), same, pipeline_mode=ONCE),
    ] + [any_spec() for _ in pieces]
    args = [info, tokens, ctx, cot, live, bi, vec, *pieces]
    aliases = {}
    if full is not None:
        in_specs.append(any_spec())
        args.append(full)
        aliases = {len(args) - 1: 0}
    first = pl.BlockSpec((1, slots, model), lambda i, info: (0, 0, 0))
    return pl.pallas_call(
        functools.partial(mid_kernel, len(pieces)),
        out_shape=(
            jax.ShapeDtypeStruct(tokens.shape, BF16),
            jax.ShapeDtypeStruct((1, slots, model), BF16),
            jax.ShapeDtypeStruct((1, slots, model), F32),
            jax.ShapeDtypeStruct((1, slots, model), BF16),
        ),
        grid_spec=pltpu.PrefetchScalarGridSpec(
            num_scalar_prefetch=1,
            grid=(1,),
            in_specs=in_specs,
            out_specs=[pl.BlockSpec((1, slots, model), own), first, first, first],
            scratch_shapes=[
                pltpu.VMEM((model, model), BF16),
                pltpu.VMEM((model, units), BF16),
                pltpu.VMEM((model, units), BF16),
                pltpu.VMEM((slots, units), F32),
                pltpu.VMEM((slots, model), F32),
                pltpu.VMEM((slots, model), F32),
                pltpu.VMEM((slots, model), BF16),
                pltpu.VMEM((slots, units), BF16),
                pltpu.SemaphoreType.DMA((3 * sub_count(pieces),)),
            ],
        ),
        input_output_aliases=aliases,
        compiler_params=pltpu.CompilerParams(vmem_limit_bytes=VMEM),
        cost_estimate=work(24e9),
        name="feed_forward",
    )(*args)


def bwd_kernel(pos, count, info, qkv_ref, p_ref, z_ref, gctx_ref, g1_ref, small_ref, qd_ref, vd_ref, *rest):
    pieces = rest[:count]
    full_ref, grad_ref, lora_ref, w, dqkv, total, sems = rest[-7:]
    slots, width = gctx_ref.shape[1], gctx_ref.shape[2]
    span, half = info[4 + info[pos]], pl.program_id(1)
    masks = lane_masks()
    (copies,) = fetch(pieces, info, [(0, 3 * width, stacked(w))], sems)

    @pl.when(half == 0)
    def _():
        for copy in copies:
            copy.start()

    def attend(size):
        def pair(j, _):
            col = pl.multiple_of(j * 128, 128)
            for b in range(slots // size):
                rows = slice(b * size, (b + 1) * size)
                q2 = qkv_ref[0, rows, pl.ds(col, 128)] * jnp.asarray(0.125, BF16)
                k2 = qkv_ref[0, rows, pl.ds(width + col, 128)] * jnp.asarray(0.125, BF16)
                v2 = qkv_ref[0, rows, pl.ds(2 * width + col, 128)]
                g2 = gctx_ref[0, rows, pl.ds(col, 128)]
                dq = dk = dv = jnp.zeros((size, 128), F32)
                for e in range(2):
                    probs = p_ref[0, 2 * j + e, rows, :size]
                    dp = mm(g2, v2 * masks[e], NT)
                    dv = dv + mm(probs, g2 * masks[e], TN)
                    p32 = probs.astype(F32)
                    pd = p32 * dp
                    ds = (pd - p32 * jnp.sum(pd, axis=1, keepdims=True)).astype(BF16)
                    dq = dq + mm(ds, k2 * masks[e])
                    dk = dk + mm(ds, q2 * masks[e], TN)
                dqkv[rows, pl.ds(col, 128)] = dq.astype(BF16)
                dqkv[rows, pl.ds(width + col, 128)] = dk.astype(BF16)
                dqkv[rows, pl.ds(2 * width + col, 128)] = dv.astype(BF16)
            return 0

        lax.fori_loop(0, width // 128, pair, 0)

    by_span(pos, span, slots, attend)

    @pl.when(half == 0)
    def _():
        for copy in copies:
            copy.wait()

    part = mm(dqkv[...], w[half], NT)
    r = small_ref.shape[1] // 2 - 3
    uq, uv = split(2.0 * small_ref[0, :r]), split(2.0 * small_ref[0, r : 2 * r])
    dq, dv = dqkv[:, :width], dqkv[:, 2 * width :]
    tq = split(mm(dq, uq[0], NT) + mm(dq, uq[1], NT))
    tv = split(mm(dv, uv[0], NT) + mm(dv, uv[1], NT))
    down = jnp.concatenate([qd_ref[...], vd_ref[...]] * 2, axis=1)
    part = part + mm(jnp.concatenate([tq[0], tv[0], tq[1], tv[1]], axis=1), down, NT)
    lora_ref[0] = 2.0 * mm(z_ref[0], dqkv[...], TN)

    @pl.when(half == 0)
    def _():
        total[...] = g1_ref[0] + part

    @pl.when(half == 1)
    def _():
        grad_ref[0] = (total[...] + part).astype(BF16)
        full_ref[0] = grad_ref[0]


def run_bwd(pos, info, qkv, probs, ctx, z, gctx, g1, pieces, small, query_down, value_down, full):
    _, slots, width3 = qkv.shape
    half, model = width3 // 3, g1.shape[2]
    heads, wide = probs.shape[1], probs.shape[3]
    in_specs = [
        pl.BlockSpec((1, slots, width3), lambda i, h, info: (h, 0, 0)),
        pl.BlockSpec((1, heads, slots, wide), lambda i, h, info: (h, 0, 0, 0)),
        pl.BlockSpec(z.shape, lambda i, h, info: (0, 0, 0)),
        pl.BlockSpec((1, slots, half), lambda i, h, info: (0, 0, h)),
        pl.BlockSpec((1, slots, model), lambda i, h, info: (0, 0, 0)),
        pl.BlockSpec((1, small.shape[1], half), lambda i, h, info: (h, 0, 0)),
        pl.BlockSpec(query_down.shape, lambda i, h, info: (0, 0)),
        pl.BlockSpec(value_down.shape, lambda i, h, info: (0, 0)),
    ] + [any_spec() for _ in pieces]
    args = [info, qkv, probs, z, gctx, g1, small, query_down, value_down, *pieces]
    aliases = {}
    if full is not None:
        in_specs.append(any_spec())
        args.append(full)
        aliases = {len(args) - 1: 0}
    return pl.pallas_call(
        functools.partial(bwd_kernel, pos, len(pieces)),
        out_shape=(
            jax.ShapeDtypeStruct((4, slots, model), BF16),
            jax.ShapeDtypeStruct((1, slots, model), BF16),
            jax.ShapeDtypeStruct((2, 16, width3), F32),
        ),
        grid_spec=pltpu.PrefetchScalarGridSpec(
            num_scalar_prefetch=1,
            grid=(1, 2),
            in_specs=in_specs,
            out_specs=[
                pl.BlockSpec((1, slots, model), lambda i, h, info: (info[pos], 0, 0)),
                pl.BlockSpec((1, slots, model), lambda i, h, info: (0, 0, 0)),
                pl.BlockSpec((1, 16, width3), lambda i, h, info: (h, 0, 0)),
            ],
            scratch_shapes=[
                pltpu.VMEM((2, model, width3), BF16),
                pltpu.VMEM((slots, width3), BF16),
                pltpu.VMEM((slots, model), F32),
                pltpu.SemaphoreType.DMA((sub_count(pieces),)),
            ],
        ),
        input_output_aliases=aliases,
        compiler_params=pltpu.CompilerParams(vmem_limit_bytes=VMEM),
        cost_estimate=work(16e9),
        name="attention_backward",
    )(*args)


def place_kernel(pos, info, full_ref, *rest):
    count = len(rest) - 4
    pieces, (out_ref, buf, into, out_of) = rest[:count], rest[count:]
    parts = buf.shape[1]
    rows = buf.shape[2]
    reads, writes = [], []
    for n, piece in enumerate(pieces):
        for c in range(parts):
            part = pl.ds(c * rows, rows)
            dest = out_ref.at[info[2 + pos + n], part]
            reads.append(pltpu.make_async_copy(piece.at[0, part], buf.at[n, c], into.at[n * parts + c]))
            writes.append(pltpu.make_async_copy(buf.at[n, c], dest, out_of.at[n * parts + c]))
    for read in reads:
        read.start()
    for read, write in zip(reads, writes):
        read.wait()
        write.start()
    for write in writes:
        write.wait()


def place(pos, info, full, pieces):
    _, slots, model = full.shape
    parts = 4
    return pl.pallas_call(
        functools.partial(place_kernel, pos),
        out_shape=jax.ShapeDtypeStruct(full.shape, full.dtype),
        grid_spec=pltpu.PrefetchScalarGridSpec(
            num_scalar_prefetch=1,
            grid=(),
            in_specs=[any_spec() for _ in range(1 + len(pieces))],
            out_specs=any_spec(),
            scratch_shapes=[
                pltpu.VMEM((len(pieces), parts, slots // parts, model), full.dtype),
                pltpu.SemaphoreType.DMA((len(pieces) * parts,)),
                pltpu.SemaphoreType.DMA((len(pieces) * parts,)),
            ],
        ),
        input_output_aliases={1: 0},
        compiler_params=pltpu.CompilerParams(vmem_limit_bytes=VMEM),
        name="place",
    )(info, full, *pieces)


def sum_over_dp(a):
    size = lax.axis_size("dp")
    if size & (size - 1):
        return lax.psum(a, "dp")
    bit = 1
    while bit < size:
        a = a + lax.ppermute(a, "dp", [(i, i ^ bit) for i in range(size)])
        bit *= 2
    return a


def shards(
    tokens, live, bucket, query_weight, key_weight, value_weight, output_weight, inner_weight,
    outer_weight, query_bias, value_bias, output_bias, inner_bias, outer_bias, first_scale,
    first_bias, second_scale, second_bias, query_down, value_down, query_up, value_up, cotangent,
):
    micro, slots, model = tokens.shape
    half, hid = query_weight.shape[1], inner_weight.shape[1]
    rank = query_up.shape[0]
    scale = ALPHA / rank
    me = lax.axis_index("head")

    early = jnp.concatenate([query_weight, key_weight, value_weight], axis=1)
    size = lax.axis_size("dp")
    if by_permutes(size):
        go = permuter(size)
        ring = spread_ring(early, size)
        fours = [spread_first(ring[k : k + 2], size) for k in (0, 2)]
        wqkv = [p for four in fours for p in spread_core(four, go(four, "second"), size)]
        output_weight, inner_weight, outer_weight = then((output_weight, inner_weight, outer_weight), ring[1])
        query_up, value_up, query_bias, value_bias, inner_bias = then(
            (query_up, value_up, query_bias, value_bias, inner_bias), ring[2]
        )
        query_down, value_down, bucket, live, output_bias = then(
            (query_down, value_down, bucket, live, output_bias), ring[3]
        )
    late = jnp.concatenate([output_weight.T, inner_weight, outer_weight.T], axis=1)
    if by_permutes(size):
        ring = spread_ring(late, size)
        fours = [spread_first(ring[k : k + 2], size) for k in (0, 2)]
        far = go(fours[0], "second")
    else:
        wqkv = gather_whole(early)

    small = jnp.concatenate(
        [query_up, value_up]
        + [b.astype(F32).reshape(-1, half) for b in (query_bias, value_bias, inner_bias)],
        axis=0,
    )
    other = lax.ppermute(small, "head", SWAP)
    both = jnp.where(me == 0, jnp.stack([small, other]), jnp.stack([other, small]))
    bi = both[:, 2 * rank + 2 :].reshape(1, 2 * hid)
    zero = jnp.zeros((model,), F32)
    vec = jnp.stack(
        [
            a.astype(F32)
            for a in (output_bias, outer_bias, first_scale, first_bias, second_scale, second_bias, zero, zero)
        ]
    )

    place_of = jnp.sum(bucket[None, :] > bucket[:, None], axis=1)
    wanted = jnp.where(me == 0, jnp.array([0, 3, 1, 2]), jnp.array([1, 2, 0, 3]))
    chosen = jnp.sum(jnp.where(place_of[None, :] == wanted[:, None], jnp.arange(micro)[None, :], 0), axis=1)
    live = live.reshape(micro, 1, slots)
    here = jnp.stack([lax.axis_index("dp"), me]).astype(jnp.int32)
    info = jnp.concatenate([chosen.astype(jnp.int32), bucket.astype(jnp.int32), here])

    first = run_fwd(0, info, tokens, wqkv, both, query_down, value_down, live)
    if by_permutes(size):
        last = go(then(fours[1], first[2]), "second")
        wrest = spread_core(fours[0], then(far, first[2]), size)
    else:
        wrest = gather_whole(late)
    second = run_fwd(1, then(info, first[2]), tokens, wqkv, both, query_down, value_down, live)
    if by_permutes(size):
        wrest += spread_core(fours[1], then(last, second[2]), size)
    acts = grads = None
    ctx = then(first[2], second[2])
    acts, a0, g1, gctx = run_mid(0, info, tokens, ctx, cotangent, live, wrest, bi, vec, acts)
    p_a0 = lax.ppermute(a0, "head", SWAP)
    grads, g0, lora0 = run_bwd(0, info, *first, gctx, g1, wqkv, both, query_down, value_down, grads)
    p_g0 = lax.ppermute(g0, "head", SWAP)
    ctx = then(second[2], (p_a0, g0))
    acts, a1, g1, gctx = run_mid(1, info, tokens, ctx, cotangent, live, wrest, bi, vec, acts)
    p_a1 = lax.ppermute(a1, "head", SWAP)
    grads, g1, lora1 = run_bwd(1, info, *second, then(gctx, p_g0), g1, wqkv, both, query_down, value_down, grads)
    p_g1 = lax.ppermute(then(g1, p_a1), "head", SWAP)
    lora = lora0 + lora1
    lora = jnp.concatenate([lora[:, :rank, :half], lora[:, rank:, 2 * half :]], axis=2)
    mine, other = jnp.where(me == 0, lora, lora[::-1])
    lora = sum_over_dp(mine + lax.ppermute(other, "head", SWAP))
    acts = place(0, info, acts, [p_a0, p_a1])
    grads = place(0, info, grads, [p_g0])
    grads = place(1, info, grads, [p_g1])
    return acts, grads, lora[:, :half], lora[:, half:]


def solution(mesh):
    return jax.shard_map(
        shards,
        mesh=mesh,
        in_specs=(
            P(None, "dp", None), P(None, "dp"), P(),
            P("dp", "head"), P("dp", "head"), P("dp", "head"), P("head", "dp"), P("dp", "head"), P("head", "dp"),
            P("head"), P("head"), P(), P("head"), P(), P(), P(), P(), P(),
            P(), P(), P(None, "head"), P(None, "head"), P(None, "dp", None),
        ),
        out_specs=(P(None, "dp", None), P(None, "dp", None), P(None, "head"), P(None, "head")),
        check_vma=False,
    )
```

```python
import functools
import math

import jax
import jax.numpy as jnp
from jax import lax
from jax.experimental import pallas as pl
from jax.experimental.pallas import tpu as pltpu
from jax.sharding import PartitionSpec as P

F32, BF16 = jnp.float32, jnp.bfloat16
EPS = 1e-5
MASKED = -1e9
NT = (((1,), (1,)), ((), ()))
TN = (((0,), (0,)), ((), ()))
NN = (((1,), (0,)), ((), ()))
SWAP = [(0, 1), (1, 0)]
RSQRT2 = 1.0 / math.sqrt(2.0)
PHI0 = 1.0 / math.sqrt(2.0 * math.pi)
ONCE = pl.Buffered(1)
VMEM = 60 << 20


def work(flops):
    return pl.CostEstimate(flops=int(flops), bytes_accessed=8 << 20, transcendentals=0)


def chip_table(size, move):
    deep = size // 4

    def index(z, x, c, y):
        return ((z % deep) * 4 + x * 2 + c) * 2 + y

    return [
        (index(z, x, c, y), index(*move(z, x, c, y)))
        for z in range(deep)
        for x in range(2)
        for c in range(2)
        for y in range(2)
    ]


def by_permutes(size):
    return size == 16


def permuter(size):
    tables = {
        "first": chip_table(size, lambda z, x, c, y: (z, x, c, 1 - y) if c else (z, 1 - x, c, y)),
        "second": chip_table(size, lambda z, x, c, y: (z, 1 - x, c, y) if c else (z, x, c, 1 - y)),
        "ring": chip_table(size, lambda z, x, c, y: (z + 1, x, c, y)),
        "core": chip_table(size, lambda z, x, c, y: (z, x, 1 - c, y)),
    }
    return lambda a, which: lax.ppermute(a, ("dp", "head"), tables[which])


def then(value, done):
    return lax.optimization_barrier((value, done))[0]


def spread_ring(shard, size):
    go, blocks = permuter(size), [shard]
    for _ in range(3):
        blocks.append(go(blocks[-1], "ring"))
    return blocks


def gather_whole(shard):
    whole = lax.all_gather(shard, ("head", "dp"), axis=0, tiled=True)
    return [whole.reshape(2, -1, shard.shape[1])]


def sub_pieces(refs, info):
    dp, y = info[8], info[9]
    if len(refs) == 1:
        return [(refs[0].at[h], h, 0) for h in range(2)]
    rows = refs[0].shape[1]
    z, x, core = dp >> 2, (dp >> 1) & 1, dp & 1
    out = []
    for k in range(4):
        deep = ((z + 4 - k) & 3) << 2
        for side in range(2):
            c = core ^ side
            for j in range(4):
                dx, dy = ((0, 0), (1 - c, c), (c, 1 - c), (1, 1))[j]
                row = (deep + ((x ^ dx) << 1) + c) * rows
                view = refs[(k // 2) * 8 + side * 4 + j].at[k % 2]
                out.append((view, y ^ dy, pl.multiple_of(row, rows)))
    return out


def fetch(refs, info, parts, sems):
    subs = sub_pieces(refs, info)
    result = []
    for p, (start, count, dest) in enumerate(parts):
        result.append(
            [
                pltpu.make_async_copy(
                    ref.at[:, pl.ds(start, count)], dest(h, row, ref.shape[0]), sems.at[p * len(subs) + n]
                )
                for n, (ref, h, row) in enumerate(subs)
            ]
        )
    return result


def side_by_side(buf, count):
    return lambda h, row, rows: buf.at[pl.ds(row, rows), pl.ds(pl.multiple_of(h * count, 128), count)]


def stacked(buf):
    return lambda h, row, rows: buf.at[h, pl.ds(row, rows)]


def mm(a, b, dims=NN):
    return lax.dot_general(a, b, dims, preferred_element_type=F32)


def lane_masks():
    lane = lax.broadcasted_iota(jnp.int32, (1, 128), 1)
    one, zero = jnp.ones((1, 128), F32), jnp.zeros((1, 128), F32)
    low = jnp.where(lane < 64, one, zero)
    return low.astype(BF16), (one - low).astype(BF16)


def pack_kernel(*refs):
    out_ref, cols = refs[-1], refs[0].shape[1]
    for k, ref in enumerate(refs[:-1]):
        out_ref[:, k * cols : (k + 1) * cols] = ref[...]


def pack(parts):
    rows, cols = parts[0].shape
    return pl.pallas_call(
        pack_kernel,
        out_shape=jax.ShapeDtypeStruct((rows, len(parts) * cols), parts[0].dtype),
        name="pack",
    )(*parts)


def prepare_kernel(
    bucket, here, wo_ref, wi_ref, wt_ref, uq_ref, uv_ref, qb_ref, vb_ref, ib_ref,
    b0, b1, b2, b3, b4, b5, late_ref, small_ref, vec_ref, info_ref,
):
    half, hid = wo_ref.shape[0], wi_ref.shape[1]
    late_ref[:, :half] = wo_ref[...].T
    late_ref[:, half : half + hid] = wi_ref[...]
    late_ref[:, half + hid :] = wt_ref[...].T
    rank = uq_ref.shape[0]
    small_ref[:rank] = uq_ref[...]
    small_ref[rank : 2 * rank] = uv_ref[...]
    small_ref[2 * rank : 2 * rank + 1] = qb_ref[...].astype(F32).reshape(1, half)
    small_ref[2 * rank + 1 : 2 * rank + 2] = vb_ref[...].astype(F32).reshape(1, half)
    inner = ib_ref[...].astype(F32).reshape(1, hid)
    for k in range(hid // half):
        small_ref[2 * rank + 2 + k : 2 * rank + 3 + k] = inner[:, k * half : (k + 1) * half]
    for k, ref in enumerate((b0, b1, b2, b3, b4, b5)):
        vec_ref[k : k + 1] = ref[...].astype(F32).reshape(1, -1)
    count = bucket.shape[0]
    for m in range(count):
        place_of = 0
        for other in range(count):
            place_of += jnp.where(bucket[other] > bucket[m], 1, 0)
        outside = jnp.where((place_of == 0) | (place_of == count - 1), 0, 1)
        second = jnp.where(place_of >= count // 2, 1, 0)
        info_ref[(outside ^ here[1]) * 2 + second] = m
        info_ref[count + m] = bucket[m]
    info_ref[2 * count] = here[0]
    info_ref[2 * count + 1] = here[1]


def prepare(bucket, here, *arrays):
    wo, wi, wt, uq = arrays[:4]
    rows, half = wo.shape[1], wo.shape[0]
    smem = pl.BlockSpec(memory_space=pltpu.SMEM)
    vmem = pl.BlockSpec(memory_space=pltpu.VMEM)
    return pl.pallas_call(
        prepare_kernel,
        out_shape=(
            jax.ShapeDtypeStruct((rows, half + 2 * wi.shape[1]), BF16),
            jax.ShapeDtypeStruct((2 * uq.shape[0] + 2 + wi.shape[1] // half, half), F32),
            jax.ShapeDtypeStruct((8, arrays[8].shape[0]), F32),
            jax.ShapeDtypeStruct((2 * bucket.shape[0] + 2,), jnp.int32),
        ),
        in_specs=[smem, smem] + [vmem] * len(arrays),
        out_specs=(vmem, vmem, vmem, smem),
        cost_estimate=work(2e9),
        name="prepare",
    )(bucket, here, *arrays)


def split(a):
    high = a.astype(BF16)
    return high, (a - high.astype(F32)).astype(BF16)


def fwd_kernel(pos, count, info, x_ref, own_ref, peer_ref, qd_ref, vd_ref, live_ref, *rest):
    pieces, (qkv_ref, p_ref, ctx_ref, z_ref, w, bias, sems) = rest[:count], rest[count:]
    slots, width = x_ref.shape[1], ctx_ref.shape[2]
    span, half = info[4 + info[pos]], pl.program_id(1)

    @pl.when(half == 0)
    def _():
        (copies,) = fetch(pieces, info, [(0, 3 * width, stacked(w))], sems)
        for copy in copies:
            copy.start()
        t = lax.broadcasted_iota(jnp.int32, (slots, slots), 0)
        s = lax.broadcasted_iota(jnp.int32, (slots, slots), 1)
        ok = ((t ^ s) < span) & (live_ref[pl.ds(info[pos], 1), :] == 1)
        bias[...] = jnp.where(ok, 0.0, MASKED)
        down = jnp.concatenate([qd_ref[...], vd_ref[...]], axis=0)
        z_ref[0] = mm(x_ref[0], down, NT).astype(BF16)
        for copy in copies:
            copy.wait()

    x, z, r = x_ref[0], z_ref[0], qd_ref.shape[0]
    small = jnp.where(half == info[9], own_ref[...], peer_ref[...])
    uq, uv = split(2.0 * small[:r]), split(2.0 * small[r : 2 * r])
    addq = mm(z[:, :r], uq[0]) + mm(z[:, :r], uq[1]) + small[2 * r : 2 * r + 1]
    addv = mm(z[:, r:], uv[0]) + mm(z[:, r:], uv[1]) + small[2 * r + 1 : 2 * r + 2]
    qkv_ref[0, :, :width] = (mm(x, w[half, :, :width]) + addq).astype(BF16)
    qkv_ref[0, :, width : 2 * width] = mm(x, w[half, :, width : 2 * width]).astype(BF16)
    qkv_ref[0, :, 2 * width :] = (mm(x, w[half, :, 2 * width :]) + addv).astype(BF16)
    masks = lane_masks()

    def attend(size):
        def pair(j, _):
            col = pl.multiple_of(j * 128, 128)
            for b in range(slots // size):
                rows = slice(b * size, (b + 1) * size)
                q2 = qkv_ref[0, rows, pl.ds(col, 128)]
                k2 = qkv_ref[0, rows, pl.ds(width + col, 128)] * jnp.asarray(0.125, BF16)
                v2 = qkv_ref[0, rows, pl.ds(2 * width + col, 128)]
                acc = None
                for e in range(2):
                    s = mm(q2, k2 * masks[e], NT) + bias[rows, rows]
                    s = jnp.exp(s - jnp.max(s, axis=1, keepdims=True))
                    probs = (s * (1.0 / jnp.sum(s, axis=1, keepdims=True))).astype(BF16)
                    p_ref[0, 2 * j + e, rows, :size] = probs
                    part = mm(probs, v2 * masks[e])
                    acc = part if acc is None else acc + part
                ctx_ref[0, rows, pl.ds(col, 128)] = acc.astype(BF16)
            return 0

        lax.fori_loop(0, width // 128, pair, 0)

    by_span(pos, span, slots, attend)


def by_span(pos, span, slots, attend):
    if pos == 0:
        pl.when(span == slots)(lambda: attend(slots))
        pl.when(span != slots)(lambda: attend(slots // 2))
    else:
        attend(slots // 2)


def any_spec():
    return pl.BlockSpec(memory_space=pl.ANY)


def sub_count(pieces):
    return sum(p.shape[0] for p in pieces)


def run_fwd(pos, info, tokens, pieces, small, peer_small, query_down, value_down, live):
    micro, slots, model = tokens.shape
    half = small.shape[1]
    heads, wide = half // 64, slots if pos == 0 else slots // 2
    return pl.pallas_call(
        functools.partial(fwd_kernel, pos, len(pieces)),
        out_shape=(
            jax.ShapeDtypeStruct((2, slots, 3 * half), BF16),
            jax.ShapeDtypeStruct((2, heads, slots, wide), BF16),
            jax.ShapeDtypeStruct((1, slots, model), BF16),
            jax.ShapeDtypeStruct((1, slots, 2 * query_down.shape[0]), BF16),
        ),
        grid_spec=pltpu.PrefetchScalarGridSpec(
            num_scalar_prefetch=1,
            grid=(1, 2),
            in_specs=[
                pl.BlockSpec((1, slots, model), lambda i, h, info: (info[pos], 0, 0)),
                pl.BlockSpec(small.shape, lambda i, h, info: (0, 0)),
                pl.BlockSpec(small.shape, lambda i, h, info: (0, 0)),
                pl.BlockSpec(query_down.shape, lambda i, h, info: (0, 0)),
                pl.BlockSpec(value_down.shape, lambda i, h, info: (0, 0)),
                pl.BlockSpec(live.shape, lambda i, h, info: (0, 0)),
            ]
            + [any_spec() for _ in pieces],
            out_specs=[
                pl.BlockSpec((1, slots, 3 * half), lambda i, h, info: (h, 0, 0)),
                pl.BlockSpec((1, heads, slots, wide), lambda i, h, info: (h, 0, 0, 0)),
                pl.BlockSpec((1, slots, half), lambda i, h, info: (0, 0, h)),
                pl.BlockSpec((1, slots, 2 * query_down.shape[0]), lambda i, h, info: (0, 0, 0)),
            ],
            scratch_shapes=[
                pltpu.VMEM((2, model, 3 * half), BF16),
                pltpu.VMEM((slots, slots), F32),
                pltpu.SemaphoreType.DMA((sub_count(pieces),)),
            ],
        ),
        compiler_params=pltpu.CompilerParams(vmem_limit_bytes=VMEM),
        cost_estimate=work(12e9),
        name="attention_forward",
    )(info, tokens, small, peer_small, query_down, value_down, live, *pieces)


def gelu_parts(u):
    cdf = 0.5 * (1.0 + lax.erf(u * RSQRT2))
    pdf = jnp.exp(-0.5 * u * u) * PHI0
    return u * cdf, cdf + u * pdf


def norm(rows):
    c = rows - jnp.mean(rows, axis=1, keepdims=True)
    rstd = lax.rsqrt(jnp.mean(c * c, axis=1, keepdims=True) + EPS)
    return c * rstd, rstd


def norm_back(e, xhat, rstd):
    return rstd * (
        e - jnp.mean(e, axis=1, keepdims=True) - xhat * jnp.mean(e * xhat, axis=1, keepdims=True)
    )


def mid_kernel(pos, count, info, x_ref, ctx_ref, cot_ref, live_ref, own_ref, peer_ref, vec_ref, *rest):
    pieces = rest[:count]
    full_ref, act_ref, g1_ref, gctx_ref, wo, wi, wt, slope, xhat, acc, low, hidden, bi_ref, sems = rest[-14:]
    model = x_ref.shape[2]
    half, units = model // 2, wi.shape[1]
    hid, step = units // 2, 768
    parts = [
        (0, half, side_by_side(wo, half)),
        (half, hid, side_by_side(wi, hid)),
        (half + hid, hid, side_by_side(wt, hid)),
    ]
    copies = fetch(pieces, info, parts, sems)
    for copy in copies[0] + copies[1] + copies[2]:
        copy.start()
    first = own_ref.shape[0] - hid // half
    for h in range(2):
        small = jnp.where(info[9] == h, own_ref[...], peer_ref[...])
        for k in range(hid // half):
            cols = h * hid + k * half
            bi_ref[:, cols : cols + half] = small[first + k : first + k + 1]
    bo, b2 = vec_ref[0:1], vec_ref[1:2]
    s1, t1, s2, t2 = vec_ref[2:3], vec_ref[3:4], vec_ref[4:5], vec_ref[5:6]
    for copy in copies[0]:
        copy.wait()
    xh, rstd1 = norm(x_ref[0].astype(F32) + bo + mm(ctx_ref[0], wo[...], NT))
    xhat[...] = xh
    low[...] = (xh * s1 + t1).astype(BF16)
    for copy in copies[1]:
        copy.wait()

    def up(j, _):
        cols = pl.ds(pl.multiple_of(j * step, step), step)
        a, d = gelu_parts(mm(low[...], wi[:, cols]) + bi_ref[:, cols])
        slope[:, cols] = d
        hidden[:, cols] = a.astype(BF16)
        return 0

    lax.fori_loop(0, units // step, up, 0)
    for copy in copies[2]:
        copy.wait()
    xh2, rstd2 = norm(mm(hidden[...], wt[...], NT) + (xhat[...] * s1 + t1) + b2)
    act_ref[0] = (xh2 * s2 + t2).astype(BF16)
    full_ref[0] = act_ref[0]
    live = jnp.broadcast_to(live_ref[pl.ds(info[pos], 1), :].astype(F32), (8, live_ref.shape[1])).T[:, :1]
    g2 = norm_back(cot_ref[0].astype(F32) * live * s2, xh2, rstd2)
    low[...] = g2.astype(BF16)
    acc[...] = g2

    def down(j, _):
        cols = pl.ds(pl.multiple_of(j * step, step), step)
        hidden[:, cols] = (mm(low[...], wt[:, cols]) * slope[:, cols]).astype(BF16)
        return 0

    lax.fori_loop(0, units // step, down, 0)
    g1 = norm_back((acc[...] + mm(hidden[...], wi[...], NT)) * s1, xhat[...], rstd1)
    g1_ref[0] = g1
    gctx_ref[0] = mm(g1.astype(BF16), wo[...]).astype(BF16)


def run_mid(pos, info, tokens, ctx, cot, live, pieces, small, peer_small, vec, full):
    micro, slots, model = tokens.shape
    units = pieces[0].shape[-1] - model // 2
    own = lambda i, info: (info[pos], 0, 0)
    same = lambda i, info: (0, 0)
    in_specs = [
        pl.BlockSpec((1, slots, model), own),
        pl.BlockSpec((1, slots, model), lambda i, info: (0, 0, 0)),
        pl.BlockSpec((1, slots, model), own),
        pl.BlockSpec(live.shape, same, pipeline_mode=ONCE),
        pl.BlockSpec(small.shape, same, pipeline_mode=ONCE),
        pl.BlockSpec(small.shape, same, pipeline_mode=ONCE),
        pl.BlockSpec((8, model), same, pipeline_mode=ONCE),
    ] + [any_spec() for _ in pieces]
    args = [info, tokens, ctx, cot, live, small, peer_small, vec, *pieces]
    aliases = {}
    if full is not None:
        in_specs.append(any_spec())
        args.append(full)
        aliases = {len(args) - 1: 0}
    first = pl.BlockSpec((1, slots, model), lambda i, info: (0, 0, 0))
    return pl.pallas_call(
        functools.partial(mid_kernel, pos, len(pieces)),
        out_shape=(
            jax.ShapeDtypeStruct(tokens.shape, BF16),
            jax.ShapeDtypeStruct((1, slots, model), BF16),
            jax.ShapeDtypeStruct((1, slots, model), F32),
            jax.ShapeDtypeStruct((1, slots, model), BF16),
        ),
        grid_spec=pltpu.PrefetchScalarGridSpec(
            num_scalar_prefetch=1,
            grid=(1,),
            in_specs=in_specs,
            out_specs=[pl.BlockSpec((1, slots, model), own), first, first, first],
            scratch_shapes=[
                pltpu.VMEM((model, model), BF16),
                pltpu.VMEM((model, units), BF16),
                pltpu.VMEM((model, units), BF16),
                pltpu.VMEM((slots, units), F32),
                pltpu.VMEM((slots, model), F32),
                pltpu.VMEM((slots, model), F32),
                pltpu.VMEM((slots, model), BF16),
                pltpu.VMEM((slots, units), BF16),
                pltpu.VMEM((1, units), F32),
                pltpu.SemaphoreType.DMA((3 * sub_count(pieces),)),
            ],
        ),
        input_output_aliases=aliases,
        compiler_params=pltpu.CompilerParams(vmem_limit_bytes=VMEM),
        cost_estimate=work(24e9),
        name="feed_forward",
    )(*args)


def bwd_kernel(pos, count, info, qkv_ref, p_ref, z_ref, gctx_ref, g1_ref, own_ref, peer_ref, qd_ref, vd_ref, *rest):
    pieces = rest[:count]
    full_ref, grad_ref, lora_ref, w, dqkv, total, sems = rest[-7:]
    slots, width = gctx_ref.shape[1], gctx_ref.shape[2]
    span, half = info[4 + info[pos]], pl.program_id(1)
    masks = lane_masks()
    (copies,) = fetch(pieces, info, [(0, 3 * width, stacked(w))], sems)

    @pl.when(half == 0)
    def _():
        for copy in copies:
            copy.start()

    def attend(size):
        def pair(j, _):
            col = pl.multiple_of(j * 128, 128)
            for b in range(slots // size):
                rows = slice(b * size, (b + 1) * size)
                q2 = qkv_ref[0, rows, pl.ds(col, 128)] * jnp.asarray(0.125, BF16)
                k2 = qkv_ref[0, rows, pl.ds(width + col, 128)] * jnp.asarray(0.125, BF16)
                v2 = qkv_ref[0, rows, pl.ds(2 * width + col, 128)]
                g2 = gctx_ref[0, rows, pl.ds(col, 128)]
                dq = dk = dv = jnp.zeros((size, 128), F32)
                for e in range(2):
                    probs = p_ref[0, 2 * j + e, rows, :size]
                    dp = mm(g2, v2 * masks[e], NT)
                    dv = dv + mm(probs, g2 * masks[e], TN)
                    p32 = probs.astype(F32)
                    pd = p32 * dp
                    ds = (pd - p32 * jnp.sum(pd, axis=1, keepdims=True)).astype(BF16)
                    dq = dq + mm(ds, k2 * masks[e])
                    dk = dk + mm(ds, q2 * masks[e], TN)
                dqkv[rows, pl.ds(col, 128)] = dq.astype(BF16)
                dqkv[rows, pl.ds(width + col, 128)] = dk.astype(BF16)
                dqkv[rows, pl.ds(2 * width + col, 128)] = dv.astype(BF16)
            return 0

        lax.fori_loop(0, width // 128, pair, 0)

    by_span(pos, span, slots, attend)

    @pl.when(half == 0)
    def _():
        for copy in copies:
            copy.wait()

    part = mm(dqkv[...], w[half], NT)
    r = qd_ref.shape[0]
    small = jnp.where(half == info[9], own_ref[...], peer_ref[...])
    uq, uv = split(2.0 * small[:r]), split(2.0 * small[r : 2 * r])
    dq, dv = dqkv[:, :width], dqkv[:, 2 * width :]
    tq = split(mm(dq, uq[0], NT) + mm(dq, uq[1], NT))
    tv = split(mm(dv, uv[0], NT) + mm(dv, uv[1], NT))
    down = jnp.concatenate([qd_ref[...], vd_ref[...]] * 2, axis=0)
    part = part + mm(jnp.concatenate([tq[0], tv[0], tq[1], tv[1]], axis=1), down)
    lora_ref[0, :, :width] = 2.0 * mm(z_ref[0, :, :r], dq, TN)
    lora_ref[0, :, width:] = 2.0 * mm(z_ref[0, :, r:], dv, TN)

    @pl.when(half == 0)
    def _():
        total[...] = g1_ref[0] + part

    @pl.when(half == 1)
    def _():
        grad_ref[0] = (total[...] + part).astype(BF16)
        full_ref[0] = grad_ref[0]


def run_bwd(pos, info, qkv, probs, ctx, z, gctx, g1, pieces, small, peer_small, query_down, value_down, full):
    _, slots, width3 = qkv.shape
    half, model = width3 // 3, g1.shape[2]
    heads, wide = probs.shape[1], probs.shape[3]
    in_specs = [
        pl.BlockSpec((1, slots, width3), lambda i, h, info: (h, 0, 0)),
        pl.BlockSpec((1, heads, slots, wide), lambda i, h, info: (h, 0, 0, 0)),
        pl.BlockSpec(z.shape, lambda i, h, info: (0, 0, 0)),
        pl.BlockSpec((1, slots, half), lambda i, h, info: (0, 0, h)),
        pl.BlockSpec((1, slots, model), lambda i, h, info: (0, 0, 0)),
        pl.BlockSpec(small.shape, lambda i, h, info: (0, 0)),
        pl.BlockSpec(small.shape, lambda i, h, info: (0, 0)),
        pl.BlockSpec(query_down.shape, lambda i, h, info: (0, 0)),
        pl.BlockSpec(value_down.shape, lambda i, h, info: (0, 0)),
    ] + [any_spec() for _ in pieces]
    args = [info, qkv, probs, z, gctx, g1, small, peer_small, query_down, value_down, *pieces]
    aliases = {}
    if full is not None:
        in_specs.append(any_spec())
        args.append(full)
        aliases = {len(args) - 1: 0}
    return pl.pallas_call(
        functools.partial(bwd_kernel, pos, len(pieces)),
        out_shape=(
            jax.ShapeDtypeStruct((4, slots, model), BF16),
            jax.ShapeDtypeStruct((1, slots, model), BF16),
            jax.ShapeDtypeStruct((2, query_down.shape[0], 2 * half), F32),
        ),
        grid_spec=pltpu.PrefetchScalarGridSpec(
            num_scalar_prefetch=1,
            grid=(1, 2),
            in_specs=in_specs,
            out_specs=[
                pl.BlockSpec((1, slots, model), lambda i, h, info: (info[pos], 0, 0)),
                pl.BlockSpec((1, slots, model), lambda i, h, info: (0, 0, 0)),
                pl.BlockSpec((1, query_down.shape[0], 2 * half), lambda i, h, info: (h, 0, 0)),
            ],
            scratch_shapes=[
                pltpu.VMEM((2, model, width3), BF16),
                pltpu.VMEM((slots, width3), BF16),
                pltpu.VMEM((slots, model), F32),
                pltpu.SemaphoreType.DMA((sub_count(pieces),)),
            ],
        ),
        input_output_aliases=aliases,
        compiler_params=pltpu.CompilerParams(vmem_limit_bytes=VMEM),
        cost_estimate=work(16e9),
        name="attention_backward",
    )(*args)


def place_kernel(pos, info, full_ref, *rest):
    pieces, (out_ref, sems) = rest[:-2], rest[-2:]
    copies = [
        pltpu.make_async_copy(piece.at[0], out_ref.at[info[2 + pos + n]], sems.at[n])
        for n, piece in enumerate(pieces)
    ]
    for copy in copies:
        copy.start()
    for copy in copies:
        copy.wait()


def place(pos, info, full, pieces):
    return pl.pallas_call(
        functools.partial(place_kernel, pos),
        out_shape=jax.ShapeDtypeStruct(full.shape, full.dtype),
        grid_spec=pltpu.PrefetchScalarGridSpec(
            num_scalar_prefetch=1,
            grid=(),
            in_specs=[any_spec()] + [pl.BlockSpec(memory_space=pltpu.VMEM) for _ in pieces],
            out_specs=any_spec(),
            scratch_shapes=[pltpu.SemaphoreType.DMA((len(pieces),))],
        ),
        input_output_aliases={1: 0},
        compiler_params=pltpu.CompilerParams(vmem_limit_bytes=8 << 20),
        cost_estimate=work(1e9),
        name="place",
    )(info, full, *pieces)


def sum_over_dp(a):
    size = lax.axis_size("dp")
    if size & (size - 1):
        return lax.psum(a, "dp")
    bit = 1
    while bit < size:
        a = a + lax.ppermute(a, "dp", [(i, i ^ bit) for i in range(size)])
        bit *= 2
    return a


def shards(
    tokens, live, bucket, query_weight, key_weight, value_weight, output_weight, inner_weight,
    outer_weight, query_bias, value_bias, output_bias, inner_bias, outer_bias, first_scale,
    first_bias, second_scale, second_bias, query_down, value_down, query_up, value_up, cotangent,
):
    micro, slots, model = tokens.shape
    half, hid = query_weight.shape[1], inner_weight.shape[1]
    rank = query_up.shape[0]
    me = lax.axis_index("head")
    size = lax.axis_size("dp")
    query_down, value_down = query_down.T, value_down.T
    here = jnp.stack([lax.axis_index("dp"), me]).astype(jnp.int32)
    early = pack([query_weight, key_weight, value_weight])
    late, small, vec, info = prepare(
        bucket, here, output_weight, inner_weight, outer_weight, query_up, value_up, query_bias, value_bias,
        inner_bias, output_bias, outer_bias, first_scale, first_bias, second_scale, second_bias,
    )
    peer_small = lax.ppermute(small, "head", SWAP)

    if by_permutes(size):
        go = permuter(size)

        def plane(pair, hold=None):
            across = go(pair, "first")
            return [pair, across, go(pair, "second"), go(across if hold is None else then(across, hold), "second")]

        def both_cores(blocks):
            return blocks + [go(block, "core") for block in blocks]

        ring = spread_ring(early, size)
        wqkv = []
        for k in (0, 2):
            wqkv += both_cores(plane(jnp.stack(ring[k : k + 2])))
        ring = spread_ring(then(late, ring[1]), size)
        near = plane(jnp.stack(ring[:2]))
        distant = jnp.stack(ring[2:])
    else:
        wqkv = gather_whole(early)
    first = run_fwd(0, info, tokens, wqkv, small, peer_small, query_down, value_down, live)
    if by_permutes(size):
        distant = plane(distant, first[2])
        wrest = both_cores(then(near, first[2]))
    else:
        wrest = gather_whole(late)
    second = run_fwd(1, then(info, first[2]), tokens, wqkv, small, peer_small, query_down, value_down, live)
    if by_permutes(size):
        wrest += both_cores(then(distant[:3], first[2]) + [then(distant[3], second[2])])
    acts = grads = None
    shared = (wqkv, small, peer_small, query_down, value_down)
    ctx = then(first[2], second[2])
    acts, a0, g1, gctx = run_mid(0, info, tokens, ctx, cotangent, live, wrest, small, peer_small, vec, acts)
    p_a0 = lax.ppermute(a0, "head", SWAP)
    grads, g0, lora0 = run_bwd(0, info, *first, gctx, g1, *shared, grads)
    p_g0 = lax.ppermute(g0, "head", SWAP)
    ctx = then(second[2], (p_a0, g0))
    acts, a1, g1, gctx = run_mid(1, info, tokens, ctx, cotangent, live, wrest, small, peer_small, vec, acts)
    p_a1 = lax.ppermute(a1, "head", SWAP)
    grads, g1, lora1 = run_bwd(1, info, *second, then(gctx, p_g0), g1, *shared, grads)
    p_g1 = lax.ppermute(then(g1, p_a1), "head", SWAP)
    lora = sum_over_dp(lora0 + lora1)
    mine, other = jnp.where(me == 0, lora, lora[::-1])
    acts = place(0, info, acts, [p_a0, p_a1])
    grads = place(0, info, grads, [p_g0])
    p_g1, other = then(p_g1, (acts, grads, lora)), then(other, p_g1)
    lora = mine + lax.ppermute(other, "head", SWAP)
    grads = place(1, info, grads, [p_g1])
    return acts, grads, lora[:, :half], lora[:, half:]


def solution(mesh):
    return jax.shard_map(
        shards,
        mesh=mesh,
        in_specs=(
            P(None, "dp", None), P(None, "dp"), P(),
            P("dp", "head"), P("dp", "head"), P("dp", "head"), P("head", "dp"), P("dp", "head"), P("head", "dp"),
            P("head"), P("head"), P(), P("head"), P(), P(), P(), P(), P(),
            P(), P(), P(None, "head"), P(None, "head"), P(None, "dp", None),
        ),
        out_specs=(P(None, "dp", None), P(None, "dp", None), P(None, "head"), P(None, "head")),
        check_vma=False,
    )
```

```python
import functools
import math

import jax
import jax.numpy as jnp
from jax import lax
from jax.experimental import pallas as pl
from jax.experimental.pallas import tpu as pltpu
from jax.sharding import PartitionSpec as P

F32, BF16 = jnp.float32, jnp.bfloat16
EPS = 1e-5
MASKED = -1e9
NT = (((1,), (1,)), ((), ()))
TN = (((0,), (0,)), ((), ()))
NN = (((1,), (0,)), ((), ()))
SWAP = [(0, 1), (1, 0)]
RSQRT2 = 1.0 / math.sqrt(2.0)
PHI0 = 1.0 / math.sqrt(2.0 * math.pi)
ONCE = pl.Buffered(1)
VMEM = 60 << 20


def work(flops):
    return pl.CostEstimate(flops=int(flops), bytes_accessed=8 << 20, transcendentals=0)


def chip_table(size, move):
    deep = size // 4

    def index(z, x, c, y):
        return ((z % deep) * 4 + x * 2 + c) * 2 + y

    return [
        (index(z, x, c, y), index(*move(z, x, c, y)))
        for z in range(deep)
        for x in range(2)
        for c in range(2)
        for y in range(2)
    ]


def by_permutes(size):
    return size == 16


def permuter(size):
    tables = {
        "first": chip_table(size, lambda z, x, c, y: (z, x, c, 1 - y) if c else (z, 1 - x, c, y)),
        "second": chip_table(size, lambda z, x, c, y: (z, 1 - x, c, y) if c else (z, x, c, 1 - y)),
        "ring": chip_table(size, lambda z, x, c, y: (z + 1, x, c, y)),
        "core": chip_table(size, lambda z, x, c, y: (z, x, 1 - c, y)),
    }
    return lambda a, which: lax.ppermute(a, ("dp", "head"), tables[which])


def then(value, done):
    return lax.optimization_barrier((value, done))[0]


def spread_ring(shard, size):
    go, blocks = permuter(size), [shard]
    for _ in range(3):
        blocks.append(go(blocks[-1], "ring"))
    return blocks


def gather_whole(shard):
    whole = lax.all_gather(shard, ("head", "dp"), axis=0, tiled=True)
    return [whole.reshape(2, -1, shard.shape[1])]


def sub_pieces(refs, info):
    dp, y = info[8], info[9]
    if len(refs) == 1:
        return [(refs[0].at[y ^ h], y ^ h, 0, h) for h in range(2)]
    rows = refs[0].shape[1]
    z, x, core = dp >> 2, (dp >> 1) & 1, dp & 1
    out = []
    for k in range(4):
        deep = ((z + 4 - k) & 3) << 2
        for side in range(2):
            c = core ^ side
            for j in range(4):
                dx, dy = ((0, 0), (1 - c, c), (c, 1 - c), (1, 1))[j]
                row = (deep + ((x ^ dx) << 1) + c) * rows
                view = refs[(k // 2) * 8 + side * 4 + j].at[k % 2]
                slot = dy * 16 + (k * 2 + side) * 2 + (1 if j in (1, 2) else 0)
                out.append((view, y ^ dy, pl.multiple_of(row, rows), slot))
    return out


def fetch(refs, info, parts, sems):
    subs = sub_pieces(refs, info)
    count = len(subs)
    result = []
    for p, (start, cols, dest) in enumerate(parts):
        copies = [
            pltpu.make_async_copy(
                ref.at[:, pl.ds(start, cols)], dest(h, row, ref.shape[0]), sems.at[p * count + slot]
            )
            for ref, h, row, slot in subs
        ]
        ref, h, row, _ = subs[0]
        waits = [
            pltpu.make_async_copy(
                ref.at[:, pl.ds(start, cols)], dest(h, row, ref.shape[0]), sems.at[p * count + slot]
            )
            for slot in range(count)
        ]
        result.append((copies, waits[: count // 2], waits[count // 2 :]))
    return result


def start_all(copies):
    for copy in copies:
        copy.start()


def wait_all(copies):
    for copy in copies:
        copy.wait()


def side_by_side(buf, count):
    return lambda h, row, rows: buf.at[pl.ds(row, rows), pl.ds(pl.multiple_of(h * count, 128), count)]


def stacked(buf):
    return lambda h, row, rows: buf.at[h, pl.ds(row, rows)]


def adapter_rows(own_ref, peer_ref, turn, rank):
    small = jnp.where(turn == 0, own_ref[: 2 * rank + 2], peer_ref[: 2 * rank + 2])
    uq, uv = split(2.0 * small[:rank]), split(2.0 * small[rank : 2 * rank])
    none = jnp.zeros((2 * rank, small.shape[1]), BF16)
    query = jnp.concatenate([uq[0], uq[1], none], axis=0)
    value = jnp.concatenate([none, uv[0], uv[1]], axis=0)
    rows = jnp.concatenate([query, jnp.zeros_like(query), value], axis=1)
    return rows, small[2 * rank : 2 * rank + 1], small[2 * rank + 1 : 2 * rank + 2]


def mm(a, b, dims=NN):
    return lax.dot_general(a, b, dims, preferred_element_type=F32)


def lane_masks():
    lane = lax.broadcasted_iota(jnp.int32, (1, 128), 1)
    one, zero = jnp.ones((1, 128), F32), jnp.zeros((1, 128), F32)
    low = jnp.where(lane < 64, one, zero)
    return low.astype(BF16), (one - low).astype(BF16)


def pack_kernel(*refs):
    out_ref, cols = refs[-1], refs[0].shape[1]
    for k, ref in enumerate(refs[:-1]):
        out_ref[:, k * cols : (k + 1) * cols] = ref[...]


def pack(parts):
    rows, cols = parts[0].shape
    return pl.pallas_call(
        pack_kernel,
        out_shape=jax.ShapeDtypeStruct((rows, len(parts) * cols), parts[0].dtype),
        name="pack",
    )(*parts)


def prepare_kernel(
    bucket, here, wo_ref, wi_ref, wt_ref, uq_ref, uv_ref, qb_ref, vb_ref, ib_ref,
    b0, b1, b2, b3, b4, b5, late_ref, small_ref, vec_ref, info_ref,
):
    half, hid = wo_ref.shape[0], wi_ref.shape[1]
    late_ref[:, :half] = wo_ref[...].T
    late_ref[:, half : half + hid] = wi_ref[...]
    late_ref[:, half + hid :] = wt_ref[...].T
    rank = uq_ref.shape[0]
    small_ref[:rank] = uq_ref[...]
    small_ref[rank : 2 * rank] = uv_ref[...]
    small_ref[2 * rank : 2 * rank + 1] = qb_ref[...].astype(F32).reshape(1, half)
    small_ref[2 * rank + 1 : 2 * rank + 2] = vb_ref[...].astype(F32).reshape(1, half)
    inner = ib_ref[...].astype(F32).reshape(1, hid)
    for k in range(hid // half):
        small_ref[2 * rank + 2 + k : 2 * rank + 3 + k] = inner[:, k * half : (k + 1) * half]
    for k, ref in enumerate((b0, b1, b2, b3, b4, b5)):
        vec_ref[k : k + 1] = ref[...].astype(F32).reshape(1, -1)
    count = bucket.shape[0]
    for m in range(count):
        place_of = 0
        for other in range(count):
            place_of += jnp.where(bucket[other] > bucket[m], 1, 0)
        outside = jnp.where((place_of == 0) | (place_of == count - 1), 0, 1)
        second = jnp.where(place_of >= count // 2, 1, 0)
        info_ref[(outside ^ here[1]) * 2 + second] = m
        info_ref[count + m] = bucket[m]
    info_ref[2 * count] = here[0]
    info_ref[2 * count + 1] = here[1]


def prepare(bucket, here, *arrays):
    wo, wi, wt, uq = arrays[:4]
    rows, half = wo.shape[1], wo.shape[0]
    smem = pl.BlockSpec(memory_space=pltpu.SMEM)
    vmem = pl.BlockSpec(memory_space=pltpu.VMEM)
    return pl.pallas_call(
        prepare_kernel,
        out_shape=(
            jax.ShapeDtypeStruct((rows, half + 2 * wi.shape[1]), BF16),
            jax.ShapeDtypeStruct((2 * uq.shape[0] + 2 + wi.shape[1] // half, half), F32),
            jax.ShapeDtypeStruct((8, arrays[8].shape[0]), F32),
            jax.ShapeDtypeStruct((2 * bucket.shape[0] + 2,), jnp.int32),
        ),
        in_specs=[smem, smem] + [vmem] * len(arrays),
        out_specs=(vmem, vmem, vmem, smem),
        cost_estimate=work(2e9),
        name="prepare",
    )(bucket, here, *arrays)


def split(a):
    high = a.astype(BF16)
    return high, (a - high.astype(F32)).astype(BF16)


def fwd_kernel(pos, count, info, x_ref, own_ref, peer_ref, qd_ref, vd_ref, live_ref, *rest):
    pieces, (qkv_ref, p_ref, ctx_ref, z_ref, w, wide_x, bias, sems) = rest[:count], rest[count:]
    slots, model, width = x_ref.shape[1], x_ref.shape[2], own_ref.shape[1]
    rank = qd_ref.shape[0]
    span, turn, pair = info[4 + info[pos]], pl.program_id(0), pl.program_id(1)
    half = info[9] ^ turn
    ((copies, early, late),) = fetch(pieces, info, [(0, 3 * width, stacked(w))], sems)

    @pl.when((turn == 0) & (pair == 0))
    def _():
        start_all(copies)
        t = lax.broadcasted_iota(jnp.int32, (slots, slots), 0)
        s = lax.broadcasted_iota(jnp.int32, (slots, slots), 1)
        ok = ((t ^ s) < span) & (live_ref[pl.ds(info[pos], 1), :] == 1)
        bias[...] = jnp.where(ok, 0.0, MASKED)
        down = jnp.concatenate([qd_ref[...], vd_ref[...]], axis=0)
        z = mm(x_ref[0], down, NT).astype(BF16)
        z_ref[0] = z
        wide_x[:, :model] = x_ref[0]
        wide_x[:, model:] = jnp.concatenate([z[:, :rank], z[:, :rank], z[:, rank:], z[:, rank:]], axis=1)
        wait_all(early)

    @pl.when((turn == 1) & (pair == 0))
    def _():
        wait_all(late)

    @pl.when(pair == 0)
    def _():
        rows, bq, bv = adapter_rows(own_ref, peer_ref, turn, rank)
        w[half, model:] = rows
        for k, shift in enumerate((bq, 0.0, bv)):
            cols = slice(k * width, (k + 1) * width)
            qkv_ref[0, :, cols] = (mm(wide_x[...], w[half, :, cols]) + shift).astype(BF16)

    masks = lane_masks()
    col = pl.multiple_of(pair * 128, 128)

    def attend(size):
        for b in range(slots // size):
            rows = slice(b * size, (b + 1) * size)
            q2 = qkv_ref[0, rows, pl.ds(col, 128)]
            k2 = qkv_ref[0, rows, pl.ds(width + col, 128)] * jnp.asarray(0.125, BF16)
            v2 = qkv_ref[0, rows, pl.ds(2 * width + col, 128)]
            acc = None
            for e in range(2):
                s = mm(q2, k2 * masks[e], NT) + bias[rows, rows]
                s = jnp.exp(s - jnp.max(s, axis=1, keepdims=True))
                probs = (s * (1.0 / jnp.sum(s, axis=1, keepdims=True))).astype(BF16)
                p_ref[0, e, rows, :size] = probs
                part = mm(probs, v2 * masks[e])
                acc = part if acc is None else acc + part
            ctx_ref[0, rows] = acc.astype(BF16)

    attend(block_size(pos, slots))


def block_size(pos, slots):
    return slots if pos == 0 else slots // 2


def any_spec():
    return pl.BlockSpec(memory_space=pl.ANY)


def sub_count(pieces):
    return sum(p.shape[0] for p in pieces)


def run_fwd(pos, info, tokens, pieces, small, peer_small, query_down, value_down, live):
    micro, slots, model = tokens.shape
    half = small.shape[1]
    pairs, wide = half // 128, slots if pos == 0 else slots // 2
    whole = lambda i, j, info: (0, 0)
    return pl.pallas_call(
        functools.partial(fwd_kernel, pos, len(pieces)),
        out_shape=(
            jax.ShapeDtypeStruct((2, slots, 3 * half), BF16),
            jax.ShapeDtypeStruct((2, 2 * pairs, slots, wide), BF16),
            jax.ShapeDtypeStruct((1, slots, model), BF16),
            jax.ShapeDtypeStruct((1, slots, 2 * query_down.shape[0]), BF16),
        ),
        grid_spec=pltpu.PrefetchScalarGridSpec(
            num_scalar_prefetch=1,
            grid=(2, pairs),
            in_specs=[
                pl.BlockSpec((1, slots, model), lambda i, j, info: (info[pos], 0, 0)),
                pl.BlockSpec(small.shape, whole),
                pl.BlockSpec(small.shape, whole),
                pl.BlockSpec(query_down.shape, whole),
                pl.BlockSpec(value_down.shape, whole),
                pl.BlockSpec(live.shape, whole),
            ]
            + [any_spec() for _ in pieces],
            out_specs=[
                pl.BlockSpec((1, slots, 3 * half), lambda i, j, info: (i ^ info[9], 0, 0)),
                pl.BlockSpec((1, 2, slots, wide), lambda i, j, info: (i ^ info[9], j, 0, 0)),
                pl.BlockSpec((1, slots, 128), lambda i, j, info: (0, 0, (i ^ info[9]) * pairs + j)),
                pl.BlockSpec((1, slots, 2 * query_down.shape[0]), lambda i, j, info: (0, 0, 0)),
            ],
            scratch_shapes=[
                pltpu.VMEM((2, model + 4 * query_down.shape[0], 3 * half), BF16),
                pltpu.VMEM((slots, model + 4 * query_down.shape[0]), BF16),
                pltpu.VMEM((slots, slots), F32),
                pltpu.SemaphoreType.DMA((sub_count(pieces),)),
            ],
        ),
        compiler_params=pltpu.CompilerParams(vmem_limit_bytes=VMEM),
        cost_estimate=work(12e9),
        name="attention_forward",
    )(info, tokens, small, peer_small, query_down, value_down, live, *pieces)


def gelu_parts(u):
    cdf = 0.5 * (1.0 + lax.erf(u * RSQRT2))
    pdf = jnp.exp(-0.5 * u * u) * PHI0
    return u * cdf, cdf + u * pdf


def norm(rows):
    c = rows - jnp.mean(rows, axis=1, keepdims=True)
    rstd = lax.rsqrt(jnp.mean(c * c, axis=1, keepdims=True) + EPS)
    return c * rstd, rstd


def norm_back(e, xhat, rstd):
    return rstd * (
        e - jnp.mean(e, axis=1, keepdims=True) - xhat * jnp.mean(e * xhat, axis=1, keepdims=True)
    )


def mid_kernel(pos, count, info, x_ref, ctx_ref, cot_ref, live_ref, own_ref, peer_ref, vec_ref, *rest):
    pieces = rest[:count]
    full_ref, act_ref, g1_ref, gctx_ref, wo, wi, wt, slope, xhat, acc, low, hidden, bi_ref, sems = rest[-14:]
    model = x_ref.shape[2]
    half, units = model // 2, wi.shape[1]
    hid, step = units // 2, 512
    parts = [
        (0, half, side_by_side(wo, half)),
        (half, hid, side_by_side(wi, hid)),
        (half + hid, hid, side_by_side(wt, hid)),
    ]
    fetched = fetch(pieces, info, parts, sems)
    for copies, _, _ in fetched:
        start_all(copies)
    first = own_ref.shape[0] - hid // half
    for h in range(2):
        small = jnp.where(info[9] == h, own_ref[...], peer_ref[...])
        for k in range(hid // half):
            cols = h * hid + k * half
            bi_ref[:, cols : cols + half] = small[first + k : first + k + 1]
    bo, b2 = vec_ref[0:1], vec_ref[1:2]
    s1, t1, s2, t2 = vec_ref[2:3], vec_ref[3:4], vec_ref[4:5], vec_ref[5:6]
    wait_all(fetched[0][1] + fetched[0][2])
    xh, rstd1 = norm(x_ref[0].astype(F32) + bo + mm(ctx_ref[0], wo[...], NT))
    xhat[...] = xh
    low[...] = (xh * s1 + t1).astype(BF16)
    wait_all(fetched[1][1] + fetched[1][2])

    def up(j, _):
        cols = pl.ds(pl.multiple_of(j * step, step), step)
        a, d = gelu_parts(mm(low[...], wi[:, cols]) + bi_ref[:, cols])
        slope[:, cols] = d
        hidden[:, cols] = a.astype(BF16)
        return 0

    lax.fori_loop(0, units // step, up, 0)
    wait_all(fetched[2][1] + fetched[2][2])
    xh2, rstd2 = norm(mm(hidden[...], wt[...], NT) + (xhat[...] * s1 + t1) + b2)
    act_ref[0] = (xh2 * s2 + t2).astype(BF16)
    full_ref[0] = act_ref[0]
    live = jnp.broadcast_to(live_ref[pl.ds(info[pos], 1), :].astype(F32), (8, live_ref.shape[1])).T[:, :1]
    g2 = norm_back(cot_ref[0].astype(F32) * live * s2, xh2, rstd2)
    low[...] = g2.astype(BF16)
    acc[...] = g2

    def down(j, _):
        cols = pl.ds(pl.multiple_of(j * step, step), step)
        hidden[:, cols] = (mm(low[...], wt[:, cols]) * slope[:, cols]).astype(BF16)
        return 0

    lax.fori_loop(0, units // step, down, 0)
    g1 = norm_back((acc[...] + mm(hidden[...], wi[...], NT)) * s1, xhat[...], rstd1)
    g1_ref[0] = g1
    gctx_ref[0] = mm(g1.astype(BF16), wo[...]).astype(BF16)


def run_mid(pos, info, tokens, ctx, cot, live, pieces, small, peer_small, vec, full):
    micro, slots, model = tokens.shape
    units = pieces[0].shape[-1] - model // 2
    own = lambda i, info: (info[pos], 0, 0)
    same = lambda i, info: (0, 0)
    in_specs = [
        pl.BlockSpec((1, slots, model), own),
        pl.BlockSpec((1, slots, model), lambda i, info: (0, 0, 0)),
        pl.BlockSpec((1, slots, model), own),
        pl.BlockSpec(live.shape, same, pipeline_mode=ONCE),
        pl.BlockSpec(small.shape, same, pipeline_mode=ONCE),
        pl.BlockSpec(small.shape, same, pipeline_mode=ONCE),
        pl.BlockSpec((8, model), same, pipeline_mode=ONCE),
    ] + [any_spec() for _ in pieces]
    args = [info, tokens, ctx, cot, live, small, peer_small, vec, *pieces]
    aliases = {}
    if full is not None:
        in_specs.append(any_spec())
        args.append(full)
        aliases = {len(args) - 1: 0}
    first = pl.BlockSpec((1, slots, model), lambda i, info: (0, 0, 0))
    return pl.pallas_call(
        functools.partial(mid_kernel, pos, len(pieces)),
        out_shape=(
            jax.ShapeDtypeStruct(tokens.shape, BF16),
            jax.ShapeDtypeStruct((1, slots, model), BF16),
            jax.ShapeDtypeStruct((1, slots, model), F32),
            jax.ShapeDtypeStruct((1, slots, model), BF16),
        ),
        grid_spec=pltpu.PrefetchScalarGridSpec(
            num_scalar_prefetch=1,
            grid=(1,),
            in_specs=in_specs,
            out_specs=[pl.BlockSpec((1, slots, model), own), first, first, first],
            scratch_shapes=[
                pltpu.VMEM((model, model), BF16),
                pltpu.VMEM((model, units), BF16),
                pltpu.VMEM((model, units), BF16),
                pltpu.VMEM((slots, units), F32),
                pltpu.VMEM((slots, model), F32),
                pltpu.VMEM((slots, model), F32),
                pltpu.VMEM((slots, model), BF16),
                pltpu.VMEM((slots, units), BF16),
                pltpu.VMEM((1, units), F32),
                pltpu.SemaphoreType.DMA((3 * sub_count(pieces),)),
            ],
        ),
        input_output_aliases=aliases,
        compiler_params=pltpu.CompilerParams(vmem_limit_bytes=VMEM),
        cost_estimate=work(24e9),
        name="feed_forward",
    )(*args)


def bwd_kernel(
    pos, count, info, qkv_ref, p_ref, z_ref, gctx_ref, g1_ref, own_ref, peer_ref, qd_ref, vd_ref, *rest
):
    pieces = rest[:count]
    full_ref, grad_ref, lora_ref, w, dqkv, total, sems = rest[-7:]
    slots, width = qkv_ref.shape[1], own_ref.shape[1]
    turn, pair = pl.program_id(0), pl.program_id(1)
    half = info[9] ^ turn
    masks = lane_masks()
    ((copies, early, late),) = fetch(pieces, info, [(0, 3 * width, stacked(w))], sems)

    @pl.when((turn == 0) & (pair == 0))
    def _():
        start_all(copies)

    col = pl.multiple_of(pair * 128, 128)

    def attend(size):
        for b in range(slots // size):
            rows = slice(b * size, (b + 1) * size)
            q2 = qkv_ref[0, rows, pl.ds(col, 128)] * jnp.asarray(0.125, BF16)
            k2 = qkv_ref[0, rows, pl.ds(width + col, 128)] * jnp.asarray(0.125, BF16)
            v2 = qkv_ref[0, rows, pl.ds(2 * width + col, 128)]
            g2 = gctx_ref[0, rows]
            dq = dk = dv = jnp.zeros((size, 128), F32)
            for e in range(2):
                probs = p_ref[0, e, rows, :size]
                dp = mm(g2, v2 * masks[e], NT)
                dv = dv + mm(probs, g2 * masks[e], TN)
                p32 = probs.astype(F32)
                pd = p32 * dp
                ds = (pd - p32 * jnp.sum(pd, axis=1, keepdims=True)).astype(BF16)
                dq = dq + mm(ds, k2 * masks[e])
                dk = dk + mm(ds, q2 * masks[e], TN)
            dqkv[rows, pl.ds(col, 128)] = dq.astype(BF16)
            dqkv[rows, pl.ds(width + col, 128)] = dk.astype(BF16)
            dqkv[rows, pl.ds(2 * width + col, 128)] = dv.astype(BF16)

    attend(block_size(pos, slots))

    @pl.when((turn == 0) & (pair == width // 128 - 1))
    def _():
        wait_all(early)

    @pl.when((turn == 1) & (pair == width // 128 - 1))
    def _():
        wait_all(late)

    @pl.when(pair == width // 128 - 1)
    def _():
        rank, model = qd_ref.shape[0], g1_ref.shape[2]
        w[half, model:] = adapter_rows(own_ref, peer_ref, turn, rank)[0]
        part = mm(dqkv[...], w[half], NT)
        t = part[:, model:]
        tq, tv = split(t[:, :rank] + t[:, rank : 2 * rank]), split(t[:, 2 * rank : 3 * rank] + t[:, 3 * rank :])
        down = jnp.concatenate([qd_ref[...], vd_ref[...]] * 2, axis=0)
        part = part[:, :model] + mm(jnp.concatenate([tq[0], tv[0], tq[1], tv[1]], axis=1), down)
        lora = 2.0 * mm(z_ref[0], dqkv[...], TN)
        lora_ref[0, :, :width] = lora[:rank, :width]
        lora_ref[0, :, width:] = lora[rank:, 2 * width :]

        @pl.when(turn == 0)
        def _():
            total[...] = g1_ref[0] + part

        @pl.when(turn == 1)
        def _():
            grad_ref[0] = (total[...] + part).astype(BF16)
            full_ref[0] = grad_ref[0]


def run_bwd(pos, info, qkv, probs, ctx, z, gctx, g1, pieces, small, peer_small, query_down, value_down, full):
    _, slots, width3 = qkv.shape
    half, model = width3 // 3, g1.shape[2]
    pairs, wide = half // 128, probs.shape[3]
    whole = lambda i, j, info: (0, 0)
    in_specs = [
        pl.BlockSpec((1, slots, width3), lambda i, j, info: (i ^ info[9], 0, 0)),
        pl.BlockSpec((1, 2, slots, wide), lambda i, j, info: (i ^ info[9], j, 0, 0)),
        pl.BlockSpec(z.shape, lambda i, j, info: (0, 0, 0)),
        pl.BlockSpec((1, slots, 128), lambda i, j, info: (0, 0, (i ^ info[9]) * pairs + j)),
        pl.BlockSpec((1, slots, model), lambda i, j, info: (0, 0, 0)),
        pl.BlockSpec(small.shape, whole),
        pl.BlockSpec(small.shape, whole),
        pl.BlockSpec(query_down.shape, whole),
        pl.BlockSpec(value_down.shape, whole),
    ] + [any_spec() for _ in pieces]
    args = [info, qkv, probs, z, gctx, g1, small, peer_small, query_down, value_down, *pieces]
    aliases = {}
    if full is not None:
        in_specs.append(any_spec())
        args.append(full)
        aliases = {len(args) - 1: 0}
    return pl.pallas_call(
        functools.partial(bwd_kernel, pos, len(pieces)),
        out_shape=(
            jax.ShapeDtypeStruct((4, slots, model), BF16),
            jax.ShapeDtypeStruct((1, slots, model), BF16),
            jax.ShapeDtypeStruct((2, query_down.shape[0], 2 * half), F32),
        ),
        grid_spec=pltpu.PrefetchScalarGridSpec(
            num_scalar_prefetch=1,
            grid=(2, pairs),
            in_specs=in_specs,
            out_specs=[
                pl.BlockSpec((1, slots, model), lambda i, j, info: (info[pos], 0, 0)),
                pl.BlockSpec((1, slots, model), lambda i, j, info: (0, 0, 0)),
                pl.BlockSpec((1, query_down.shape[0], 2 * half), lambda i, j, info: (i ^ info[9], 0, 0)),
            ],
            scratch_shapes=[
                pltpu.VMEM((2, model + 4 * query_down.shape[0], width3), BF16),
                pltpu.VMEM((slots, width3), BF16),
                pltpu.VMEM((slots, model), F32),
                pltpu.SemaphoreType.DMA((sub_count(pieces),)),
            ],
        ),
        input_output_aliases=aliases,
        compiler_params=pltpu.CompilerParams(vmem_limit_bytes=VMEM),
        cost_estimate=work(16e9),
        name="attention_backward",
    )(*args)


def place_kernel(pos, info, full_ref, *rest):
    pieces, (out_ref, sems) = rest[:-2], rest[-2:]
    copies = [
        pltpu.make_async_copy(piece.at[0], out_ref.at[info[2 + pos + n]], sems.at[n])
        for n, piece in enumerate(pieces)
    ]
    for copy in copies:
        copy.start()
    for copy in copies:
        copy.wait()


def place(pos, info, full, pieces):
    return pl.pallas_call(
        functools.partial(place_kernel, pos),
        out_shape=jax.ShapeDtypeStruct(full.shape, full.dtype),
        grid_spec=pltpu.PrefetchScalarGridSpec(
            num_scalar_prefetch=1,
            grid=(),
            in_specs=[any_spec()] + [pl.BlockSpec(memory_space=pltpu.VMEM) for _ in pieces],
            out_specs=any_spec(),
            scratch_shapes=[pltpu.SemaphoreType.DMA((len(pieces),))],
        ),
        input_output_aliases={1: 0},
        compiler_params=pltpu.CompilerParams(vmem_limit_bytes=8 << 20),
        cost_estimate=work(1e9),
        name="place",
    )(info, full, *pieces)


def sum_over_dp(a):
    size = lax.axis_size("dp")
    if size & (size - 1):
        return lax.psum(a, "dp")
    bit = 1
    while bit < size:
        a = a + lax.ppermute(a, "dp", [(i, i ^ bit) for i in range(size)])
        bit *= 2
    return a


def shards(
    tokens, live, bucket, query_weight, key_weight, value_weight, output_weight, inner_weight,
    outer_weight, query_bias, value_bias, output_bias, inner_bias, outer_bias, first_scale,
    first_bias, second_scale, second_bias, query_down, value_down, query_up, value_up, cotangent,
):
    micro, slots, model = tokens.shape
    half, hid = query_weight.shape[1], inner_weight.shape[1]
    rank = query_up.shape[0]
    me = lax.axis_index("head")
    size = lax.axis_size("dp")
    query_down, value_down = query_down.T, value_down.T
    here = jnp.stack([lax.axis_index("dp"), me]).astype(jnp.int32)
    early = pack([query_weight, key_weight, value_weight])
    late, small, vec, info = prepare(
        bucket, here, output_weight, inner_weight, outer_weight, query_up, value_up, query_bias, value_bias,
        inner_bias, output_bias, outer_bias, first_scale, first_bias, second_scale, second_bias,
    )
    peer_small = lax.ppermute(small, "head", SWAP)

    if by_permutes(size):
        go = permuter(size)

        def plane(pair, hold=None):
            across = go(pair, "first")
            return [pair, across, go(pair, "second"), go(across if hold is None else then(across, hold), "second")]

        def both_cores(blocks):
            return blocks + [go(block, "core") for block in blocks]

        ring = spread_ring(early, size)
        wqkv = []
        for k in (0, 2):
            wqkv += both_cores(plane(jnp.stack(ring[k : k + 2])))
        ring = spread_ring(then(late, ring[1]), size)
        near = plane(jnp.stack(ring[:2]))
        distant = jnp.stack(ring[2:])
    else:
        wqkv = gather_whole(early)
    first = run_fwd(0, info, tokens, wqkv, small, peer_small, query_down, value_down, live)
    if by_permutes(size):
        distant = plane(distant, first[2])
        wrest = both_cores(then(near, first[2]))
    else:
        wrest = gather_whole(late)
    second = run_fwd(1, then(info, first[2]), tokens, wqkv, small, peer_small, query_down, value_down, live)
    if by_permutes(size):
        wrest += both_cores(then(distant[:3], first[2]) + [then(distant[3], second[2])])
    acts = grads = None
    shared = (wqkv, small, peer_small, query_down, value_down)
    ctx = then(first[2], second[2])
    acts, a0, g1, gctx = run_mid(0, info, tokens, ctx, cotangent, live, wrest, small, peer_small, vec, acts)
    p_a0 = lax.ppermute(a0, "head", SWAP)
    grads, g0, lora0 = run_bwd(0, info, *first, gctx, g1, *shared, grads)
    p_g0 = lax.ppermute(g0, "head", SWAP)
    ctx = then(second[2], (p_a0, g0))
    acts, a1, g1, gctx = run_mid(1, info, tokens, ctx, cotangent, live, wrest, small, peer_small, vec, acts)
    p_a1 = lax.ppermute(a1, "head", SWAP)
    grads, g1, lora1 = run_bwd(1, info, *second, then(gctx, p_g0), g1, *shared, grads)
    p_g1 = lax.ppermute(then(g1, p_a1), "head", SWAP)
    lora = sum_over_dp(lora0 + lora1)
    mine, other = jnp.where(me == 0, lora, lora[::-1])
    acts = place(0, info, acts, [p_a0, p_a1])
    grads = place(0, info, grads, [p_g0])
    p_g1, other = then(p_g1, (acts, grads, lora)), then(other, p_g1)
    lora = mine + lax.ppermute(other, "head", SWAP)
    grads = place(1, info, grads, [p_g1])
    return acts, grads, lora[:, :half], lora[:, half:]


def solution(mesh):
    return jax.shard_map(
        shards,
        mesh=mesh,
        in_specs=(
            P(None, "dp", None), P(None, "dp"), P(),
            P("dp", "head"), P("dp", "head"), P("dp", "head"), P("head", "dp"), P("dp", "head"), P("head", "dp"),
            P("head"), P("head"), P(), P("head"), P(), P(), P(), P(), P(),
            P(), P(), P(None, "head"), P(None, "head"), P(None, "dp", None),
        ),
        out_specs=(P(None, "dp", None), P(None, "dp", None), P(None, "head"), P(None, "head")),
        check_vma=False,
    )
```

```python
import functools
import math

import jax
import jax.numpy as jnp
from jax import lax
from jax.experimental import pallas as pl
from jax.experimental.pallas import tpu as pltpu
from jax.sharding import PartitionSpec as P

F32, BF16 = jnp.float32, jnp.bfloat16
EPS = 1e-5
MASKED = -1e9
NT = (((1,), (1,)), ((), ()))
TN = (((0,), (0,)), ((), ()))
NN = (((1,), (0,)), ((), ()))
SWAP = [(0, 1), (1, 0)]
RSQRT2 = 1.0 / math.sqrt(2.0)
PHI0 = 1.0 / math.sqrt(2.0 * math.pi)
ONCE = pl.Buffered(1)
VMEM = 60 << 20


def work(flops):
    return pl.CostEstimate(flops=int(flops), bytes_accessed=8 << 20, transcendentals=0)


def chip_table(size, move):
    deep = size // 4

    def index(z, x, c, y):
        return ((z % deep) * 4 + x * 2 + c) * 2 + y

    return [
        (index(z, x, c, y), index(*move(z, x, c, y)))
        for z in range(deep)
        for x in range(2)
        for c in range(2)
        for y in range(2)
    ]


def by_permutes(size):
    return size == 16


def permuter(size):
    tables = {
        "first": chip_table(size, lambda z, x, c, y: (z, x, c, 1 - y) if c else (z, 1 - x, c, y)),
        "second": chip_table(size, lambda z, x, c, y: (z, 1 - x, c, y) if c else (z, x, c, 1 - y)),
        "ring": chip_table(size, lambda z, x, c, y: (z + 1, x, c, y)),
        "core": chip_table(size, lambda z, x, c, y: (z, x, 1 - c, y)),
    }
    return lambda a, which: lax.ppermute(a, ("dp", "head"), tables[which])


def then(value, done):
    return lax.optimization_barrier((value, done))[0]


def spread_ring(shard, size):
    go, blocks = permuter(size), [shard]
    for _ in range(3):
        blocks.append(go(blocks[-1], "ring"))
    return blocks


def gather_whole(shard):
    whole = lax.all_gather(shard, ("head", "dp"), axis=0, tiled=True)
    return [whole.reshape(2, -1, shard.shape[1])]


def sub_pieces(refs, info):
    dp, y = info[8], info[9]
    if len(refs) == 1:
        return [(refs[0].at[y ^ h], h, 0) for h in range(2)]
    rows = refs[0].shape[1]
    z, x, core = dp >> 2, (dp >> 1) & 1, dp & 1
    out = []
    for k in range(4):
        deep = ((z + 4 - k) & 3) << 2
        for side in range(2):
            c = core ^ side
            for j in range(4):
                dx, dy = ((0, 0), (1 - c, c), (c, 1 - c), (1, 1))[j]
                row = (deep + ((x ^ dx) << 1) + c) * rows
                out.append((refs[(k // 2) * 8 + side * 4 + j].at[k % 2], dy, pl.multiple_of(row, rows)))
    return out


def fetch(refs, info, parts, sems):
    for p, (start, cols, dest) in enumerate(parts):
        for ref, dy, row in sub_pieces(refs, info):
            view = ref.at[:, pl.ds(start, cols)]
            pltpu.make_async_copy(view, dest(info[9] ^ dy, row, ref.shape[0]), sems.at[2 * p + dy]).start()


def wait_for(buf, sem):
    pltpu.make_async_copy(buf, buf, sem).wait()


def side_by_side(buf, count):
    return lambda h, row, rows: buf.at[pl.ds(row, rows), pl.ds(pl.multiple_of(h * count, 128), count)]


def stacked(buf):
    return lambda h, row, rows: buf.at[h, pl.ds(row, rows)]


def adapter_rows(own_ref, peer_ref, turn, rank):
    small = jnp.where(turn == 0, own_ref[: 2 * rank + 2], peer_ref[: 2 * rank + 2])
    uq, uv = split(2.0 * small[:rank]), split(2.0 * small[rank : 2 * rank])
    none = jnp.zeros((2 * rank, small.shape[1]), BF16)
    query = jnp.concatenate([uq[0], uq[1], none], axis=0)
    value = jnp.concatenate([none, uv[0], uv[1]], axis=0)
    rows = jnp.concatenate([query, jnp.zeros_like(query), value], axis=1)
    return rows, small[2 * rank : 2 * rank + 1], small[2 * rank + 1 : 2 * rank + 2]


def mm(a, b, dims=NN):
    return lax.dot_general(a, b, dims, preferred_element_type=F32)


def lane_masks():
    lane = lax.broadcasted_iota(jnp.int32, (1, 128), 1)
    one, zero = jnp.ones((1, 128), F32), jnp.zeros((1, 128), F32)
    low = jnp.where(lane < 64, one, zero)
    return low.astype(BF16), (one - low).astype(BF16)


def pack_kernel(*refs):
    out_ref, cols = refs[-1], refs[0].shape[1]
    for k, ref in enumerate(refs[:-1]):
        out_ref[:, k * cols : (k + 1) * cols] = ref[...]


def pack(parts):
    rows, cols = parts[0].shape
    return pl.pallas_call(
        pack_kernel,
        out_shape=jax.ShapeDtypeStruct((rows, len(parts) * cols), parts[0].dtype),
        name="pack",
    )(*parts)


def prepare_kernel(
    bucket, here, wo_ref, wi_ref, wt_ref, uq_ref, uv_ref, qb_ref, vb_ref, ib_ref,
    b0, b1, b2, b3, b4, b5, late_ref, small_ref, vec_ref, info_ref,
):
    half, hid = wo_ref.shape[1], wi_ref.shape[1]
    late_ref[:, :half] = wo_ref[...]
    late_ref[:, half : half + hid] = wi_ref[...]
    late_ref[:, half + hid :] = wt_ref[...]
    rank = uq_ref.shape[0]
    small_ref[:rank] = uq_ref[...]
    small_ref[rank : 2 * rank] = uv_ref[...]
    small_ref[2 * rank : 2 * rank + 1] = qb_ref[...].astype(F32).reshape(1, half)
    small_ref[2 * rank + 1 : 2 * rank + 2] = vb_ref[...].astype(F32).reshape(1, half)
    inner = ib_ref[...].astype(F32).reshape(1, hid)
    for k in range(hid // half):
        small_ref[2 * rank + 2 + k : 2 * rank + 3 + k] = inner[:, k * half : (k + 1) * half]
    for k, ref in enumerate((b0, b1, b2, b3, b4, b5)):
        vec_ref[k : k + 1] = ref[...].astype(F32).reshape(1, -1)
    count = bucket.shape[0]
    for m in range(count):
        place_of = 0
        for other in range(count):
            place_of += jnp.where(bucket[other] > bucket[m], 1, 0)
        outside = jnp.where((place_of == 0) | (place_of == count - 1), 0, 1)
        second = jnp.where(place_of >= count // 2, 1, 0)
        info_ref[(outside ^ here[1]) * 2 + second] = m
        info_ref[count + m] = bucket[m]
    info_ref[2 * count] = here[0]
    info_ref[2 * count + 1] = here[1]


def prepare(bucket, here, *arrays):
    wo, wi, wt, uq = arrays[:4]
    rows, half = wo.shape
    smem = pl.BlockSpec(memory_space=pltpu.SMEM)
    vmem = pl.BlockSpec(memory_space=pltpu.VMEM)
    return pl.pallas_call(
        prepare_kernel,
        out_shape=(
            jax.ShapeDtypeStruct((rows, half + 2 * wi.shape[1]), BF16),
            jax.ShapeDtypeStruct((2 * uq.shape[0] + 2 + wi.shape[1] // half, half), F32),
            jax.ShapeDtypeStruct((8, arrays[8].shape[0]), F32),
            jax.ShapeDtypeStruct((2 * bucket.shape[0] + 2,), jnp.int32),
        ),
        in_specs=[smem, smem] + [vmem] * len(arrays),
        out_specs=(vmem, vmem, vmem, smem),
        cost_estimate=work(2e9),
        name="prepare",
    )(bucket, here, *arrays)


def split(a):
    high = a.astype(BF16)
    return high, (a - high.astype(F32)).astype(BF16)


def fwd_kernel(pos, count, info, x_ref, own_ref, peer_ref, qd_ref, vd_ref, live_ref, *rest):
    pieces, (qkv_ref, p_ref, ctx_ref, z_ref, w, wide_x, bias, sems) = rest[:count], rest[count:]
    slots, model, width = x_ref.shape[1], x_ref.shape[2], own_ref.shape[1]
    rank = qd_ref.shape[0]
    span, turn, pair = info[4 + info[pos]], pl.program_id(0), pl.program_id(1)
    half = info[9] ^ turn

    @pl.when((turn == 0) & (pair == 0))
    def _():
        fetch(pieces, info, [(0, 3 * width, stacked(w))], sems)
        t = lax.broadcasted_iota(jnp.int32, (slots, slots), 0)
        s = lax.broadcasted_iota(jnp.int32, (slots, slots), 1)
        ok = ((t ^ s) < span) & (live_ref[pl.ds(info[pos], 1), :] == 1)
        bias[...] = jnp.where(ok, 0.0, MASKED)
        down = jnp.concatenate([qd_ref[...], vd_ref[...]], axis=0)
        z = mm(x_ref[0], down, NT).astype(BF16)
        z_ref[0] = z
        wide_x[:, :model] = x_ref[0]
        wide_x[:, model:] = jnp.concatenate([z[:, :rank], z[:, :rank], z[:, rank:], z[:, rank:]], axis=1)

    @pl.when(pair == 0)
    def _():
        wait_for(w.at[half, :model], sems.at[turn])
        rows, bq, bv = adapter_rows(own_ref, peer_ref, turn, rank)
        w[half, model:] = rows
        for k, shift in enumerate((bq, 0.0, bv)):
            cols = slice(k * width, (k + 1) * width)
            qkv_ref[0, :, cols] = (mm(wide_x[...], w[half, :, cols]) + shift).astype(BF16)

    masks = lane_masks()
    col = pl.multiple_of(pair * 128, 128)

    def attend(size):
        for b in range(slots // size):
            rows = slice(b * size, (b + 1) * size)
            q2 = qkv_ref[0, rows, pl.ds(col, 128)]
            k2 = qkv_ref[0, rows, pl.ds(width + col, 128)] * jnp.asarray(0.125, BF16)
            v2 = qkv_ref[0, rows, pl.ds(2 * width + col, 128)]
            acc = None
            for e in range(2):
                s = mm(q2, k2 * masks[e], NT) + bias[rows, rows]
                s = jnp.exp(s - jnp.max(s, axis=1, keepdims=True))
                probs = (s * (1.0 / jnp.sum(s, axis=1, keepdims=True))).astype(BF16)
                p_ref[0, e, rows, :size] = probs
                part = mm(probs, v2 * masks[e])
                acc = part if acc is None else acc + part
            ctx_ref[0, rows] = acc.astype(BF16)

    attend(block_size(pos, slots))


def block_size(pos, slots):
    return slots if pos == 0 else slots // 2


def any_spec():
    return pl.BlockSpec(memory_space=pl.ANY)


def run_fwd(pos, info, tokens, pieces, small, peer_small, query_down, value_down, live):
    micro, slots, model = tokens.shape
    half = small.shape[1]
    pairs, wide = half // 128, slots if pos == 0 else slots // 2
    whole = lambda i, j, info: (0, 0)
    return pl.pallas_call(
        functools.partial(fwd_kernel, pos, len(pieces)),
        out_shape=(
            jax.ShapeDtypeStruct((2, slots, 3 * half), BF16),
            jax.ShapeDtypeStruct((2, 2 * pairs, slots, wide), BF16),
            jax.ShapeDtypeStruct((1, slots, model), BF16),
            jax.ShapeDtypeStruct((1, slots, 2 * query_down.shape[0]), BF16),
        ),
        grid_spec=pltpu.PrefetchScalarGridSpec(
            num_scalar_prefetch=1,
            grid=(2, pairs),
            in_specs=[
                pl.BlockSpec((1, slots, model), lambda i, j, info: (info[pos], 0, 0)),
                pl.BlockSpec(small.shape, whole),
                pl.BlockSpec(small.shape, whole),
                pl.BlockSpec(query_down.shape, whole),
                pl.BlockSpec(value_down.shape, whole),
                pl.BlockSpec(live.shape, whole),
            ]
            + [any_spec() for _ in pieces],
            out_specs=[
                pl.BlockSpec((1, slots, 3 * half), lambda i, j, info: (i ^ info[9], 0, 0)),
                pl.BlockSpec((1, 2, slots, wide), lambda i, j, info: (i ^ info[9], j, 0, 0)),
                pl.BlockSpec((1, slots, 128), lambda i, j, info: (0, 0, (i ^ info[9]) * pairs + j)),
                pl.BlockSpec((1, slots, 2 * query_down.shape[0]), lambda i, j, info: (0, 0, 0)),
            ],
            scratch_shapes=[
                pltpu.VMEM((2, model + 4 * query_down.shape[0], 3 * half), BF16),
                pltpu.VMEM((slots, model + 4 * query_down.shape[0]), BF16),
                pltpu.VMEM((slots, slots), F32),
                pltpu.SemaphoreType.DMA((2,)),
            ],
        ),
        compiler_params=pltpu.CompilerParams(vmem_limit_bytes=VMEM),
        cost_estimate=work(12e9),
        name="attention_forward",
    )(info, tokens, small, peer_small, query_down, value_down, live, *pieces)


def gelu_parts(u):
    cdf = 0.5 * (1.0 + lax.erf(u * RSQRT2))
    pdf = jnp.exp(-0.5 * u * u) * PHI0
    return u * cdf, cdf + u * pdf


def norm(rows):
    c = rows - jnp.mean(rows, axis=1, keepdims=True)
    rstd = lax.rsqrt(jnp.mean(c * c, axis=1, keepdims=True) + EPS)
    return c * rstd, rstd


def norm_back(e, xhat, rstd):
    return rstd * (
        e - jnp.mean(e, axis=1, keepdims=True) - xhat * jnp.mean(e * xhat, axis=1, keepdims=True)
    )


def mid_kernel(pos, count, info, x_ref, ctx_ref, cot_ref, live_ref, own_ref, peer_ref, vec_ref, *rest):
    pieces = rest[:count]
    full_ref, act_ref, g1_ref, gctx_ref, wo, wi, wt, slope, xhat, acc, low, hidden, bi_ref, sems = rest[-14:]
    model = x_ref.shape[2]
    half, units = model // 2, wi.shape[1]
    hid, step = units // 2, 768
    parts = [
        (0, half, side_by_side(wo, half)),
        (half, hid, side_by_side(wi, hid)),
        (half + hid, hid, side_by_side(wt, hid)),
    ]
    fetch(pieces, info, parts, sems)
    first = own_ref.shape[0] - hid // half
    for h in range(2):
        small = jnp.where(info[9] == h, own_ref[...], peer_ref[...])
        for k in range(hid // half):
            cols = h * hid + k * half
            bi_ref[:, cols : cols + half] = small[first + k : first + k + 1]
    bo, b2 = vec_ref[0:1], vec_ref[1:2]
    s1, t1, s2, t2 = vec_ref[2:3], vec_ref[3:4], vec_ref[4:5], vec_ref[5:6]
    for h in range(2):
        wait_for(wo.at[:, h * half : (h + 1) * half], sems.at[0 + h])
    xh, rstd1 = norm(x_ref[0].astype(F32) + bo + mm(ctx_ref[0], wo[...], NT))
    xhat[...] = xh
    low[...] = (xh * s1 + t1).astype(BF16)
    for h in range(2):
        wait_for(wi.at[:, h * hid : (h + 1) * hid], sems.at[2 + h])

    def up(j, _):
        cols = pl.ds(pl.multiple_of(j * step, step), step)
        a, d = gelu_parts(mm(low[...], wi[:, cols]) + bi_ref[:, cols])
        slope[:, cols] = d
        hidden[:, cols] = a.astype(BF16)
        return 0

    lax.fori_loop(0, units // step, up, 0)
    for h in range(2):
        wait_for(wt.at[:, h * hid : (h + 1) * hid], sems.at[4 + h])
    xh2, rstd2 = norm(mm(hidden[...], wt[...], NT) + (xhat[...] * s1 + t1) + b2)
    act_ref[0] = (xh2 * s2 + t2).astype(BF16)
    full_ref[0] = act_ref[0]
    live = jnp.broadcast_to(live_ref[pl.ds(info[pos], 1), :].astype(F32), (8, live_ref.shape[1])).T[:, :1]
    g2 = norm_back(cot_ref[0].astype(F32) * live * s2, xh2, rstd2)
    low[...] = g2.astype(BF16)
    acc[...] = g2

    def down(j, _):
        cols = pl.ds(pl.multiple_of(j * step, step), step)
        hidden[:, cols] = (mm(low[...], wt[:, cols]) * slope[:, cols]).astype(BF16)
        return 0

    lax.fori_loop(0, units // step, down, 0)
    g1 = norm_back((acc[...] + mm(hidden[...], wi[...], NT)) * s1, xhat[...], rstd1)
    g1_ref[0] = g1
    gctx_ref[0] = mm(g1.astype(BF16), wo[...]).astype(BF16)


def run_mid(pos, info, tokens, ctx, cot, live, pieces, small, peer_small, vec, full):
    micro, slots, model = tokens.shape
    units = pieces[0].shape[-1] - model // 2
    own = lambda i, info: (info[pos], 0, 0)
    same = lambda i, info: (0, 0)
    in_specs = [
        pl.BlockSpec((1, slots, model), own),
        pl.BlockSpec((1, slots, model), lambda i, info: (0, 0, 0)),
        pl.BlockSpec((1, slots, model), own),
        pl.BlockSpec(live.shape, same, pipeline_mode=ONCE),
        pl.BlockSpec(small.shape, same, pipeline_mode=ONCE),
        pl.BlockSpec(small.shape, same, pipeline_mode=ONCE),
        pl.BlockSpec((8, model), same, pipeline_mode=ONCE),
    ] + [any_spec() for _ in pieces]
    args = [info, tokens, ctx, cot, live, small, peer_small, vec, *pieces]
    aliases = {}
    if full is not None:
        in_specs.append(any_spec())
        args.append(full)
        aliases = {len(args) - 1: 0}
    first = pl.BlockSpec((1, slots, model), lambda i, info: (0, 0, 0))
    return pl.pallas_call(
        functools.partial(mid_kernel, pos, len(pieces)),
        out_shape=(
            jax.ShapeDtypeStruct(tokens.shape, BF16),
            jax.ShapeDtypeStruct((1, slots, model), BF16),
            jax.ShapeDtypeStruct((1, slots, model), F32),
            jax.ShapeDtypeStruct((1, slots, model), BF16),
        ),
        grid_spec=pltpu.PrefetchScalarGridSpec(
            num_scalar_prefetch=1,
            grid=(1,),
            in_specs=in_specs,
            out_specs=[pl.BlockSpec((1, slots, model), own), first, first, first],
            scratch_shapes=[
                pltpu.VMEM((model, model), BF16),
                pltpu.VMEM((model, units), BF16),
                pltpu.VMEM((model, units), BF16),
                pltpu.VMEM((slots, units), F32),
                pltpu.VMEM((slots, model), F32),
                pltpu.VMEM((slots, model), F32),
                pltpu.VMEM((slots, model), BF16),
                pltpu.VMEM((slots, units), BF16),
                pltpu.VMEM((1, units), F32),
                pltpu.SemaphoreType.DMA((6,)),
            ],
        ),
        input_output_aliases=aliases,
        compiler_params=pltpu.CompilerParams(vmem_limit_bytes=VMEM),
        cost_estimate=work(24e9),
        name="feed_forward",
    )(*args)


def bwd_kernel(
    pos, count, info, qkv_ref, p_ref, z_ref, gctx_ref, g1_ref, own_ref, peer_ref, qd_ref, vd_ref, *rest
):
    pieces = rest[:count]
    full_ref, grad_ref, lora_ref, w, dqkv, total, sems = rest[-7:]
    slots, width = qkv_ref.shape[1], own_ref.shape[1]
    turn, pair = pl.program_id(0), pl.program_id(1)
    half = info[9] ^ turn
    masks = lane_masks()

    @pl.when((turn == 0) & (pair == 0))
    def _():
        fetch(pieces, info, [(0, 3 * width, stacked(w))], sems)

    col = pl.multiple_of(pair * 128, 128)

    def attend(size):
        for b in range(slots // size):
            rows = slice(b * size, (b + 1) * size)
            q2 = qkv_ref[0, rows, pl.ds(col, 128)] * jnp.asarray(0.125, BF16)
            k2 = qkv_ref[0, rows, pl.ds(width + col, 128)] * jnp.asarray(0.125, BF16)
            v2 = qkv_ref[0, rows, pl.ds(2 * width + col, 128)]
            g2 = gctx_ref[0, rows]
            dq = dk = dv = jnp.zeros((size, 128), F32)
            for e in range(2):
                probs = p_ref[0, e, rows, :size]
                dp = mm(g2, v2 * masks[e], NT)
                dv = dv + mm(probs, g2 * masks[e], TN)
                p32 = probs.astype(F32)
                pd = p32 * dp
                ds = (pd - p32 * jnp.sum(pd, axis=1, keepdims=True)).astype(BF16)
                dq = dq + mm(ds, k2 * masks[e])
                dk = dk + mm(ds, q2 * masks[e], TN)
            dqkv[rows, pl.ds(col, 128)] = dq.astype(BF16)
            dqkv[rows, pl.ds(width + col, 128)] = dk.astype(BF16)
            dqkv[rows, pl.ds(2 * width + col, 128)] = dv.astype(BF16)

    attend(block_size(pos, slots))

    @pl.when(pair == width // 128 - 1)
    def _():
        rank, model = qd_ref.shape[0], g1_ref.shape[2]
        wait_for(w.at[half, :model], sems.at[turn])
        w[half, model:] = adapter_rows(own_ref, peer_ref, turn, rank)[0]
        part = mm(dqkv[...], w[half], NT)
        lora = 2.0 * mm(z_ref[0], dqkv[...], TN)
        lora_ref[0, :, :width] = lora[:rank, :width]
        lora_ref[0, :, width:] = lora[rank:, 2 * width :]

        @pl.when(turn == 0)
        def _():
            total[:, :model] = g1_ref[0] + part[:, :model]
            total[:, model:] = part[:, model:]

        @pl.when(turn == 1)
        def _():
            t = total[:, model:] + part[:, model:]
            tq, tv = split(t[:, :rank] + t[:, rank : 2 * rank]), split(t[:, 2 * rank : 3 * rank] + t[:, 3 * rank :])
            down = jnp.concatenate([qd_ref[...], vd_ref[...]] * 2, axis=0)
            sums = total[:, :model] + part[:, :model]
            sums = sums + mm(jnp.concatenate([tq[0], tv[0], tq[1], tv[1]], axis=1), down)
            grad_ref[0] = sums.astype(BF16)
            full_ref[0] = grad_ref[0]


def run_bwd(pos, info, qkv, probs, ctx, z, gctx, g1, pieces, small, peer_small, query_down, value_down, full):
    _, slots, width3 = qkv.shape
    half, model = width3 // 3, g1.shape[2]
    pairs, wide = half // 128, probs.shape[3]
    whole = lambda i, j, info: (0, 0)
    in_specs = [
        pl.BlockSpec((1, slots, width3), lambda i, j, info: (i ^ info[9], 0, 0)),
        pl.BlockSpec((1, 2, slots, wide), lambda i, j, info: (i ^ info[9], j, 0, 0)),
        pl.BlockSpec(z.shape, lambda i, j, info: (0, 0, 0)),
        pl.BlockSpec((1, slots, 128), lambda i, j, info: (0, 0, (i ^ info[9]) * pairs + j)),
        pl.BlockSpec((1, slots, model), lambda i, j, info: (0, 0, 0)),
        pl.BlockSpec(small.shape, whole),
        pl.BlockSpec(small.shape, whole),
        pl.BlockSpec(query_down.shape, whole),
        pl.BlockSpec(value_down.shape, whole),
    ] + [any_spec() for _ in pieces]
    args = [info, qkv, probs, z, gctx, g1, small, peer_small, query_down, value_down, *pieces]
    aliases = {}
    if full is not None:
        in_specs.append(any_spec())
        args.append(full)
        aliases = {len(args) - 1: 0}
    return pl.pallas_call(
        functools.partial(bwd_kernel, pos, len(pieces)),
        out_shape=(
            jax.ShapeDtypeStruct((4, slots, model), BF16),
            jax.ShapeDtypeStruct((1, slots, model), BF16),
            jax.ShapeDtypeStruct((2, query_down.shape[0], 2 * half), F32),
        ),
        grid_spec=pltpu.PrefetchScalarGridSpec(
            num_scalar_prefetch=1,
            grid=(2, pairs),
            in_specs=in_specs,
            out_specs=[
                pl.BlockSpec((1, slots, model), lambda i, j, info: (info[pos], 0, 0)),
                pl.BlockSpec((1, slots, model), lambda i, j, info: (0, 0, 0)),
                pl.BlockSpec((1, query_down.shape[0], 2 * half), lambda i, j, info: (i ^ info[9], 0, 0)),
            ],
            scratch_shapes=[
                pltpu.VMEM((2, model + 4 * query_down.shape[0], width3), BF16),
                pltpu.VMEM((slots, width3), BF16),
                pltpu.VMEM((slots, model + 4 * query_down.shape[0]), F32),
                pltpu.SemaphoreType.DMA((2,)),
            ],
        ),
        input_output_aliases=aliases,
        compiler_params=pltpu.CompilerParams(vmem_limit_bytes=VMEM),
        cost_estimate=work(16e9),
        name="attention_backward",
    )(*args)


def place_kernel(pos, info, full_ref, *rest):
    pieces, (out_ref, sems) = rest[:-2], rest[-2:]
    copies = [
        pltpu.make_async_copy(piece.at[0], out_ref.at[info[2 + pos + n]], sems.at[n])
        for n, piece in enumerate(pieces)
    ]
    for copy in copies:
        copy.start()
    for copy in copies:
        copy.wait()


def place(pos, info, full, pieces):
    return pl.pallas_call(
        functools.partial(place_kernel, pos),
        out_shape=jax.ShapeDtypeStruct(full.shape, full.dtype),
        grid_spec=pltpu.PrefetchScalarGridSpec(
            num_scalar_prefetch=1,
            grid=(),
            in_specs=[any_spec()] + [pl.BlockSpec(memory_space=pltpu.VMEM) for _ in pieces],
            out_specs=any_spec(),
            scratch_shapes=[pltpu.SemaphoreType.DMA((len(pieces),))],
        ),
        input_output_aliases={1: 0},
        compiler_params=pltpu.CompilerParams(vmem_limit_bytes=8 << 20),
        cost_estimate=work(1e9),
        name="place",
    )(info, full, *pieces)


def sum_over_dp(a):
    size = lax.axis_size("dp")
    if size & (size - 1):
        return lax.psum(a, "dp")
    bit = 1
    while bit < size:
        a = a + lax.ppermute(a, "dp", [(i, i ^ bit) for i in range(size)])
        bit *= 2
    return a


def shards(
    tokens, live, bucket, query_weight, key_weight, value_weight, output_weight, inner_weight,
    outer_weight, query_bias, value_bias, output_bias, inner_bias, outer_bias, first_scale,
    first_bias, second_scale, second_bias, query_down, value_down, query_up, value_up, cotangent,
):
    micro, slots, model = tokens.shape
    half, hid = query_weight.shape[1], inner_weight.shape[1]
    rank = query_up.shape[0]
    me = lax.axis_index("head")
    size = lax.axis_size("dp")
    query_down, value_down = query_down.T, value_down.T
    here = jnp.stack([lax.axis_index("dp"), me]).astype(jnp.int32)
    early = pack([query_weight, key_weight, value_weight])
    late, small, vec, info = prepare(
        bucket, here, output_weight.T, inner_weight, outer_weight.T, query_up, value_up, query_bias, value_bias,
        inner_bias, output_bias, outer_bias, first_scale, first_bias, second_scale, second_bias,
    )
    peer_small = lax.ppermute(small, "head", SWAP)

    if by_permutes(size):
        go = permuter(size)

        def plane(pair, flip, hold=None):
            one, two = go(pair, "first"), go(pair, "second")
            via, last = (two, "first") if flip else (one, "second")
            return [pair, one, two, go(via if hold is None else then(via, hold), last)]

        def both_cores(blocks):
            return blocks + [go(block, "core") for block in blocks]

        ring = spread_ring(early, size)
        wqkv = []
        for k in (0, 2):
            wqkv += both_cores(plane(jnp.stack(ring[k : k + 2]), k == 2))
        ring = spread_ring(then(late, ring[1]), size)
        near = plane(jnp.stack(ring[:2]), False)
        distant = jnp.stack(ring[2:])
    else:
        wqkv = gather_whole(early)
    first = run_fwd(0, info, tokens, wqkv, small, peer_small, query_down, value_down, live)
    if by_permutes(size):
        distant = plane(distant, True, first[2])
        wrest = both_cores(then(near, first[2]))
    else:
        wrest = gather_whole(late)
    second = run_fwd(1, then(info, first[2]), tokens, wqkv, small, peer_small, query_down, value_down, live)
    if by_permutes(size):
        wrest += both_cores(then(distant[:3], first[2]) + [then(distant[3], second[2])])
    acts = grads = None
    shared = (wqkv, small, peer_small, query_down, value_down)
    ctx = then(first[2], second[2])
    acts, a0, g1_0, gctx0 = run_mid(0, info, tokens, ctx, cotangent, live, wrest, small, peer_small, vec, acts)
    p_a0 = lax.ppermute(a0, "head", SWAP)
    ctx = then(second[2], a0)
    acts, a1, g1_1, gctx1 = run_mid(1, info, tokens, ctx, cotangent, live, wrest, small, peer_small, vec, acts)
    p_a1 = lax.ppermute(a1, "head", SWAP)
    gctx0 = then(gctx0, (p_a0, a1))
    grads, g0, lora0 = run_bwd(0, info, *first, gctx0, g1_0, *shared, grads)
    p_g0 = lax.ppermute(g0, "head", SWAP)
    gctx1 = then(gctx1, (p_a1, g0))
    grads, g1, lora1 = run_bwd(1, info, *second, gctx1, g1_1, *shared, grads)
    p_g1 = lax.ppermute(then(g1, p_g0), "head", SWAP)
    lora = sum_over_dp(lora0 + lora1)
    mine, other = jnp.where(me == 0, lora, lora[::-1])
    acts = place(0, info, acts, [p_a0, p_a1])
    grads = place(0, info, grads, [p_g0])
    p_g1, other = then(p_g1, (acts, grads, lora)), then(other, p_g1)
    lora = mine + lax.ppermute(other, "head", SWAP)
    grads = place(1, info, grads, [p_g1])
    return acts, grads, lora[:, :half], lora[:, half:]


def solution(mesh):
    return jax.shard_map(
        shards,
        mesh=mesh,
        in_specs=(
            P(None, "dp", None), P(None, "dp"), P(),
            P("dp", "head"), P("dp", "head"), P("dp", "head"), P("head", "dp"), P("dp", "head"), P("head", "dp"),
            P("head"), P("head"), P(), P("head"), P(), P(), P(), P(), P(),
            P(), P(), P(None, "head"), P(None, "head"), P(None, "dp", None),
        ),
        out_specs=(P(None, "dp", None), P(None, "dp", None), P(None, "head"), P(None, "head")),
        check_vma=False,
    )
```

```python
import functools
import math

import jax
import jax.numpy as jnp
from jax import lax
from jax.experimental import pallas as pl
from jax.experimental.pallas import tpu as pltpu
from jax.sharding import PartitionSpec as P

F32, BF16 = jnp.float32, jnp.bfloat16
EPS = 1e-5
MASKED = -1e9
NT = (((1,), (1,)), ((), ()))
TN = (((0,), (0,)), ((), ()))
NN = (((1,), (0,)), ((), ()))
SWAP = [(0, 1), (1, 0)]
RSQRT2 = 1.0 / math.sqrt(2.0)
PHI0 = 1.0 / math.sqrt(2.0 * math.pi)
ONCE = pl.Buffered(1)
VMEM = 60 << 20


def work(flops):
    return pl.CostEstimate(flops=int(flops), bytes_accessed=8 << 20, transcendentals=0)


def chip_table(size, move):
    deep = size // 4

    def index(z, x, c, y):
        return ((z % deep) * 4 + x * 2 + c) * 2 + y

    return [
        (index(z, x, c, y), index(*move(z, x, c, y)))
        for z in range(deep)
        for x in range(2)
        for c in range(2)
        for y in range(2)
    ]


def by_permutes(size):
    return size == 16


def permuter(size):
    tables = {
        "first": chip_table(size, lambda z, x, c, y: (z, x, c, 1 - y) if c else (z, 1 - x, c, y)),
        "second": chip_table(size, lambda z, x, c, y: (z, 1 - x, c, y) if c else (z, x, c, 1 - y)),
        "ring": chip_table(size, lambda z, x, c, y: (z + 1, x, c, y)),
        "core": chip_table(size, lambda z, x, c, y: (z, x, 1 - c, y)),
    }
    return lambda a, which: lax.ppermute(a, ("dp", "head"), tables[which])


def then(value, done):
    return lax.optimization_barrier((value, done))[0]


def spread_ring(shard, size):
    go, blocks = permuter(size), [shard]
    for _ in range(3):
        blocks.append(go(blocks[-1], "ring"))
    return blocks


def gather_whole(shard):
    whole = lax.all_gather(shard, ("head", "dp"), axis=0, tiled=True)
    return [whole.reshape(2, -1, shard.shape[1])]


def sub_pieces(refs, info):
    dp, y = info[8], info[9]
    if len(refs) == 1:
        return [(refs[0].at[y ^ h], h, 0) for h in range(2)]
    rows = refs[0].shape[1]
    z, x, core = dp >> 2, (dp >> 1) & 1, dp & 1
    out = []
    for k in range(4):
        deep = ((z + 4 - k) & 3) << 2
        for side in range(2):
            c = core ^ side
            for j in range(4):
                dx, dy = ((0, 0), (1 - c, c), (c, 1 - c), (1, 1))[j]
                row = (deep + ((x ^ dx) << 1) + c) * rows
                out.append((refs[(k // 2) * 8 + side * 4 + j].at[k % 2], dy, pl.multiple_of(row, rows)))
    return out


def fetch(refs, info, parts, sems):
    for p, (start, cols, dest) in enumerate(parts):
        for ref, dy, row in sub_pieces(refs, info):
            view = ref.at[:, pl.ds(start, cols)]
            pltpu.make_async_copy(view, dest(info[9] ^ dy, row, ref.shape[0]), sems.at[2 * p + dy]).start()


def wait_for(buf, sem):
    pltpu.make_async_copy(buf, buf, sem).wait()


def side_by_side(buf, count):
    return lambda h, row, rows: buf.at[pl.ds(row, rows), pl.ds(pl.multiple_of(h * count, 128), count)]


def stacked(buf):
    return lambda h, row, rows: buf.at[h, pl.ds(row, rows)]


def adapter_rows(own_ref, peer_ref, turn, rank):
    small = jnp.where(turn == 0, own_ref[: 2 * rank + 2], peer_ref[: 2 * rank + 2])
    uq, uv = split(2.0 * small[:rank]), split(2.0 * small[rank : 2 * rank])
    none = jnp.zeros((2 * rank, small.shape[1]), BF16)
    query = jnp.concatenate([uq[0], uq[1], none], axis=0)
    value = jnp.concatenate([none, uv[0], uv[1]], axis=0)
    rows = jnp.concatenate([query, jnp.zeros_like(query), value], axis=1)
    return rows, small[2 * rank : 2 * rank + 1], small[2 * rank + 1 : 2 * rank + 2]


def mm(a, b, dims=NN):
    return lax.dot_general(a, b, dims, preferred_element_type=F32)


def lane_masks():
    lane = lax.broadcasted_iota(jnp.int32, (1, 128), 1)
    one, zero = jnp.ones((1, 128), F32), jnp.zeros((1, 128), F32)
    low = jnp.where(lane < 64, one, zero)
    return low.astype(BF16), (one - low).astype(BF16)


def pack_kernel(*refs):
    out_ref, cols = refs[-1], refs[0].shape[1]
    for k, ref in enumerate(refs[:-1]):
        out_ref[:, k * cols : (k + 1) * cols] = ref[...]


def pack(parts):
    rows, cols = parts[0].shape
    return pl.pallas_call(
        pack_kernel,
        out_shape=jax.ShapeDtypeStruct((rows, len(parts) * cols), parts[0].dtype),
        name="pack",
    )(*parts)


def prepare_kernel(
    bucket, here, wo_ref, wi_ref, wt_ref, uq_ref, uv_ref, qb_ref, vb_ref, ib_ref,
    b0, b1, b2, b3, b4, b5, late_ref, small_ref, vec_ref, info_ref,
):
    half, hid = wo_ref.shape[1], wi_ref.shape[1]
    late_ref[:, :half] = wo_ref[...]
    late_ref[:, half : half + hid] = wi_ref[...]
    late_ref[:, half + hid :] = wt_ref[...]
    rank = uq_ref.shape[0]
    small_ref[:rank] = uq_ref[...]
    small_ref[rank : 2 * rank] = uv_ref[...]
    small_ref[2 * rank : 2 * rank + 1] = qb_ref[...].astype(F32).reshape(1, half)
    small_ref[2 * rank + 1 : 2 * rank + 2] = vb_ref[...].astype(F32).reshape(1, half)
    inner = ib_ref[...].astype(F32).reshape(1, hid)
    for k in range(hid // half):
        small_ref[2 * rank + 2 + k : 2 * rank + 3 + k] = inner[:, k * half : (k + 1) * half]
    for k, ref in enumerate((b0, b1, b2, b3, b4, b5)):
        vec_ref[k : k + 1] = ref[...].astype(F32).reshape(1, -1)
    count = bucket.shape[0]
    for m in range(count):
        place_of = 0
        for other in range(count):
            place_of += jnp.where(bucket[other] > bucket[m], 1, 0)
        outside = jnp.where((place_of == 0) | (place_of == count - 1), 0, 1)
        second = jnp.where(place_of >= count // 2, 1, 0)
        info_ref[(outside ^ here[1]) * 2 + second] = m
        info_ref[count + m] = bucket[m]
    info_ref[2 * count] = here[0]
    info_ref[2 * count + 1] = here[1]


def prepare(bucket, here, *arrays):
    wo, wi, wt, uq = arrays[:4]
    rows, half = wo.shape
    smem = pl.BlockSpec(memory_space=pltpu.SMEM)
    vmem = pl.BlockSpec(memory_space=pltpu.VMEM)
    return pl.pallas_call(
        prepare_kernel,
        out_shape=(
            jax.ShapeDtypeStruct((rows, half + 2 * wi.shape[1]), BF16),
            jax.ShapeDtypeStruct((2 * uq.shape[0] + 2 + wi.shape[1] // half, half), F32),
            jax.ShapeDtypeStruct((8, arrays[8].shape[0]), F32),
            jax.ShapeDtypeStruct((2 * bucket.shape[0] + 2,), jnp.int32),
        ),
        in_specs=[smem, smem] + [vmem] * len(arrays),
        out_specs=(vmem, vmem, vmem, smem),
        cost_estimate=work(2e9),
        name="prepare",
    )(bucket, here, *arrays)


def split(a):
    high = a.astype(BF16)
    return high, (a - high.astype(F32)).astype(BF16)


def fwd_kernel(pos, count, info, x_ref, own_ref, peer_ref, qd_ref, vd_ref, live_ref, *rest):
    pieces, (qkv_ref, p_ref, ctx_ref, z_ref, w, wide_x, bias, sems) = rest[:count], rest[count:]
    slots, model, width = x_ref.shape[1], x_ref.shape[2], own_ref.shape[1]
    rank = qd_ref.shape[0]
    span, turn, pair = info[4 + info[pos]], pl.program_id(0), pl.program_id(1)
    half = info[9] ^ turn

    @pl.when((turn == 0) & (pair == 0))
    def _():
        fetch(pieces, info, [(0, 3 * width, stacked(w))], sems)
        t = lax.broadcasted_iota(jnp.int32, (slots, slots), 0)
        s = lax.broadcasted_iota(jnp.int32, (slots, slots), 1)
        ok = ((t ^ s) < span) & (live_ref[pl.ds(info[pos], 1), :] == 1)
        bias[...] = jnp.where(ok, 0.0, MASKED)
        down = jnp.concatenate([qd_ref[...], vd_ref[...]], axis=0)
        z = mm(x_ref[0], down, NT).astype(BF16)
        z_ref[0] = z
        wide_x[:, :model] = x_ref[0]
        wide_x[:, model:] = jnp.concatenate([z[:, :rank], z[:, :rank], z[:, rank:], z[:, rank:]], axis=1)

    @pl.when(pair == 0)
    def _():
        wait_for(w.at[half, :model], sems.at[turn])
        rows, bq, bv = adapter_rows(own_ref, peer_ref, turn, rank)
        w[half, model:] = rows
        for k, shift in enumerate((bq, 0.0, bv)):
            cols = slice(k * width, (k + 1) * width)
            qkv_ref[0, :, cols] = (mm(wide_x[...], w[half, :, cols]) + shift).astype(BF16)

    masks = lane_masks()
    col = pl.multiple_of(pair * 128, 128)

    def attend(size):
        for b in range(slots // size):
            rows = slice(b * size, (b + 1) * size)
            q2 = qkv_ref[0, rows, pl.ds(col, 128)]
            k2 = qkv_ref[0, rows, pl.ds(width + col, 128)] * jnp.asarray(0.125, BF16)
            v2 = qkv_ref[0, rows, pl.ds(2 * width + col, 128)]
            acc = None
            for e in range(2):
                s = mm(q2, k2 * masks[e], NT) + bias[rows, rows]
                s = jnp.exp(s - jnp.max(s, axis=1, keepdims=True))
                probs = (s * (1.0 / jnp.sum(s, axis=1, keepdims=True))).astype(BF16)
                p_ref[0, e, rows, :size] = probs
                part = mm(probs, v2 * masks[e])
                acc = part if acc is None else acc + part
            ctx_ref[0, rows] = acc.astype(BF16)

    attend(block_size(pos, slots))


def block_size(pos, slots):
    return slots if pos == 0 else slots // 2


def any_spec():
    return pl.BlockSpec(memory_space=pl.ANY)


def run_fwd(pos, info, tokens, pieces, small, peer_small, query_down, value_down, live):
    micro, slots, model = tokens.shape
    half = small.shape[1]
    pairs, wide = half // 128, slots if pos == 0 else slots // 2
    whole = lambda i, j, info: (0, 0)
    return pl.pallas_call(
        functools.partial(fwd_kernel, pos, len(pieces)),
        out_shape=(
            jax.ShapeDtypeStruct((2, slots, 3 * half), BF16),
            jax.ShapeDtypeStruct((2, 2 * pairs, slots, wide), BF16),
            jax.ShapeDtypeStruct((1, slots, model), BF16),
            jax.ShapeDtypeStruct((1, slots, 2 * query_down.shape[0]), BF16),
        ),
        grid_spec=pltpu.PrefetchScalarGridSpec(
            num_scalar_prefetch=1,
            grid=(2, pairs),
            in_specs=[
                pl.BlockSpec((1, slots, model), lambda i, j, info: (info[pos], 0, 0)),
                pl.BlockSpec(small.shape, whole),
                pl.BlockSpec(small.shape, whole),
                pl.BlockSpec(query_down.shape, whole),
                pl.BlockSpec(value_down.shape, whole),
                pl.BlockSpec(live.shape, whole),
            ]
            + [any_spec() for _ in pieces],
            out_specs=[
                pl.BlockSpec((1, slots, 3 * half), lambda i, j, info: (i ^ info[9], 0, 0)),
                pl.BlockSpec((1, 2, slots, wide), lambda i, j, info: (i ^ info[9], j, 0, 0)),
                pl.BlockSpec((1, slots, 128), lambda i, j, info: (0, 0, (i ^ info[9]) * pairs + j)),
                pl.BlockSpec((1, slots, 2 * query_down.shape[0]), lambda i, j, info: (0, 0, 0)),
            ],
            scratch_shapes=[
                pltpu.VMEM((2, model + 4 * query_down.shape[0], 3 * half), BF16),
                pltpu.VMEM((slots, model + 4 * query_down.shape[0]), BF16),
                pltpu.VMEM((slots, slots), F32),
                pltpu.SemaphoreType.DMA((2,)),
            ],
        ),
        compiler_params=pltpu.CompilerParams(vmem_limit_bytes=VMEM),
        cost_estimate=work(12e9),
        name="attention_forward",
    )(info, tokens, small, peer_small, query_down, value_down, live, *pieces)


def gelu_parts(u):
    cdf = 0.5 * (1.0 + lax.erf(u * RSQRT2))
    pdf = jnp.exp(-0.5 * u * u) * PHI0
    return u * cdf, cdf + u * pdf


def norm(rows):
    c = rows - jnp.mean(rows, axis=1, keepdims=True)
    rstd = lax.rsqrt(jnp.mean(c * c, axis=1, keepdims=True) + EPS)
    return c * rstd, rstd


def norm_back(e, xhat, rstd):
    return rstd * (
        e - jnp.mean(e, axis=1, keepdims=True) - xhat * jnp.mean(e * xhat, axis=1, keepdims=True)
    )


def mid_kernel(pos, count, info, x_ref, ctx_ref, cot_ref, live_ref, own_ref, peer_ref, vec_ref, *rest):
    pieces = rest[:count]
    full_ref, act_ref, g1_ref, gctx_ref, wo, wi, wt, slope, xhat, acc, low, hidden, bi_ref, sems = rest[-14:]
    model = x_ref.shape[2]
    half, units = model // 2, wi.shape[1]
    hid, step = units // 2, 768
    parts = [
        (0, half, side_by_side(wo, half)),
        (half, hid, side_by_side(wi, hid)),
        (half + hid, hid, side_by_side(wt, hid)),
    ]
    fetch(pieces, info, parts, sems)
    first = own_ref.shape[0] - hid // half
    for h in range(2):
        small = jnp.where(info[9] == h, own_ref[...], peer_ref[...])
        for k in range(hid // half):
            cols = h * hid + k * half
            bi_ref[:, cols : cols + half] = small[first + k : first + k + 1]
    bo, b2 = vec_ref[0:1], vec_ref[1:2]
    s1, t1, s2, t2 = vec_ref[2:3], vec_ref[3:4], vec_ref[4:5], vec_ref[5:6]
    for h in range(2):
        wait_for(wo.at[:, h * half : (h + 1) * half], sems.at[0 + h])
    xh, rstd1 = norm(x_ref[0].astype(F32) + bo + mm(ctx_ref[0], wo[...], NT))
    xhat[...] = xh
    low[...] = (xh * s1 + t1).astype(BF16)
    for h in range(2):
        wait_for(wi.at[:, h * hid : (h + 1) * hid], sems.at[2 + h])

    def up(j, _):
        cols = pl.ds(pl.multiple_of(j * step, step), step)
        a, d = gelu_parts(mm(low[...], wi[:, cols]) + bi_ref[:, cols])
        slope[:, cols] = d
        hidden[:, cols] = a.astype(BF16)
        return 0

    lax.fori_loop(0, units // step, up, 0)
    for h in range(2):
        wait_for(wt.at[:, h * hid : (h + 1) * hid], sems.at[4 + h])
    xh2, rstd2 = norm(mm(hidden[...], wt[...], NT) + (xhat[...] * s1 + t1) + b2)
    act_ref[0] = (xh2 * s2 + t2).astype(BF16)
    full_ref[0] = act_ref[0]
    live = jnp.broadcast_to(live_ref[pl.ds(info[pos], 1), :].astype(F32), (8, live_ref.shape[1])).T[:, :1]
    g2 = norm_back(cot_ref[0].astype(F32) * live * s2, xh2, rstd2)
    low[...] = g2.astype(BF16)
    acc[...] = g2

    def down(j, _):
        cols = pl.ds(pl.multiple_of(j * step, step), step)
        hidden[:, cols] = (mm(low[...], wt[:, cols]) * slope[:, cols]).astype(BF16)
        return 0

    lax.fori_loop(0, units // step, down, 0)
    g1 = norm_back((acc[...] + mm(hidden[...], wi[...], NT)) * s1, xhat[...], rstd1)
    g1_ref[0] = g1
    gctx_ref[0] = mm(g1.astype(BF16), wo[...]).astype(BF16)


def run_mid(pos, info, tokens, ctx, cot, live, pieces, small, peer_small, vec, full):
    micro, slots, model = tokens.shape
    units = pieces[0].shape[-1] - model // 2
    own = lambda i, info: (info[pos], 0, 0)
    same = lambda i, info: (0, 0)
    in_specs = [
        pl.BlockSpec((1, slots, model), own),
        pl.BlockSpec((1, slots, model), lambda i, info: (0, 0, 0)),
        pl.BlockSpec((1, slots, model), own),
        pl.BlockSpec(live.shape, same, pipeline_mode=ONCE),
        pl.BlockSpec(small.shape, same, pipeline_mode=ONCE),
        pl.BlockSpec(small.shape, same, pipeline_mode=ONCE),
        pl.BlockSpec((8, model), same, pipeline_mode=ONCE),
    ] + [any_spec() for _ in pieces]
    args = [info, tokens, ctx, cot, live, small, peer_small, vec, *pieces]
    aliases = {}
    if full is not None:
        in_specs.append(any_spec())
        args.append(full)
        aliases = {len(args) - 1: 0}
    first = pl.BlockSpec((1, slots, model), lambda i, info: (0, 0, 0))
    return pl.pallas_call(
        functools.partial(mid_kernel, pos, len(pieces)),
        out_shape=(
            jax.ShapeDtypeStruct(tokens.shape, BF16),
            jax.ShapeDtypeStruct((1, slots, model), BF16),
            jax.ShapeDtypeStruct((1, slots, model), F32),
            jax.ShapeDtypeStruct((1, slots, model), BF16),
        ),
        grid_spec=pltpu.PrefetchScalarGridSpec(
            num_scalar_prefetch=1,
            grid=(1,),
            in_specs=in_specs,
            out_specs=[pl.BlockSpec((1, slots, model), own), first, first, first],
            scratch_shapes=[
                pltpu.VMEM((model, model), BF16),
                pltpu.VMEM((model, units), BF16),
                pltpu.VMEM((model, units), BF16),
                pltpu.VMEM((slots, units), F32),
                pltpu.VMEM((slots, model), F32),
                pltpu.VMEM((slots, model), F32),
                pltpu.VMEM((slots, model), BF16),
                pltpu.VMEM((slots, units), BF16),
                pltpu.VMEM((1, units), F32),
                pltpu.SemaphoreType.DMA((6,)),
            ],
        ),
        input_output_aliases=aliases,
        compiler_params=pltpu.CompilerParams(vmem_limit_bytes=VMEM),
        cost_estimate=work(24e9),
        name="feed_forward",
    )(*args)


def bwd_kernel(
    pos, count, info, qkv_ref, p_ref, z_ref, gctx_ref, g1_ref, own_ref, peer_ref, qd_ref, vd_ref, *rest
):
    pieces = rest[:count]
    full_ref, grad_ref, mine_ref, other_ref, w, dqkv, total, sems = rest[-8:]
    earlier = rest[count : count + 2]
    slots, width = qkv_ref.shape[1], own_ref.shape[1]
    turn, pair = pl.program_id(0), pl.program_id(1)
    half = info[9] ^ turn
    masks = lane_masks()

    @pl.when((turn == 0) & (pair == 0))
    def _():
        fetch(pieces, info, [(0, 3 * width, stacked(w))], sems)

    col = pl.multiple_of(pair * 128, 128)

    def attend(size):
        for b in range(slots // size):
            rows = slice(b * size, (b + 1) * size)
            q2 = qkv_ref[0, rows, pl.ds(col, 128)] * jnp.asarray(0.125, BF16)
            k2 = qkv_ref[0, rows, pl.ds(width + col, 128)] * jnp.asarray(0.125, BF16)
            v2 = qkv_ref[0, rows, pl.ds(2 * width + col, 128)]
            g2 = gctx_ref[0, rows]
            dq = dk = dv = jnp.zeros((size, 128), F32)
            joined = []
            for e in range(2):
                probs = p_ref[0, e, rows, :size]
                dp = mm(g2, v2 * masks[e], NT)
                dv = dv + mm(probs, g2 * masks[e], TN)
                p32 = probs.astype(F32)
                pd = p32 * dp
                ds = (pd - p32 * jnp.sum(pd, axis=1, keepdims=True)).astype(BF16)
                if size == slots:
                    joined.append(ds)
                else:
                    dq = dq + mm(ds, k2 * masks[e])
                    dk = dk + mm(ds, q2 * masks[e], TN)
            if joined:
                ds = jnp.concatenate(joined, axis=1)
                dq = mm(ds, jnp.concatenate([k2 * masks[0], k2 * masks[1]], axis=0))
                dk = mm(ds, q2, TN)
                dk = jnp.where(lax.broadcasted_iota(jnp.int32, (1, 128), 1) < 64, dk[:size], dk[size:])
            dqkv[rows, pl.ds(col, 128)] = dq.astype(BF16)
            dqkv[rows, pl.ds(width + col, 128)] = dk.astype(BF16)
            dqkv[rows, pl.ds(2 * width + col, 128)] = dv.astype(BF16)

    attend(block_size(pos, slots))

    @pl.when(pair == width // 128 - 1)
    def _():
        rank, model = qd_ref.shape[0], g1_ref.shape[2]
        wait_for(w.at[half, :model], sems.at[turn])
        w[half, model:] = adapter_rows(own_ref, peer_ref, turn, rank)[0]
        part = mm(dqkv[...], w[half], NT)
        lora = 2.0 * mm(z_ref[0], dqkv[...], TN)
        lora = jnp.concatenate([lora[:rank, :width], lora[rank:, 2 * width :]], axis=1)

        @pl.when(turn == 0)
        def _():
            mine_ref[...] = lora if pos == 0 else lora + earlier[0][...]
            total[:, :model] = g1_ref[0] + part[:, :model]
            total[:, model:] = part[:, model:]

        @pl.when(turn == 1)
        def _():
            other_ref[...] = lora if pos == 0 else lora + earlier[1][...]
            t = total[:, model:] + part[:, model:]
            tq, tv = split(t[:, :rank] + t[:, rank : 2 * rank]), split(t[:, 2 * rank : 3 * rank] + t[:, 3 * rank :])
            down = jnp.concatenate([qd_ref[...], vd_ref[...]] * 2, axis=0)
            sums = total[:, :model] + part[:, :model]
            sums = sums + mm(jnp.concatenate([tq[0], tv[0], tq[1], tv[1]], axis=1), down)
            grad_ref[0] = sums.astype(BF16)
            full_ref[0] = grad_ref[0]


def run_bwd(pos, info, qkv, probs, ctx, z, gctx, g1, pieces, small, peer_small, query_down, value_down, full, earlier=()):
    _, slots, width3 = qkv.shape
    half, model = width3 // 3, g1.shape[2]
    pairs, wide = half // 128, probs.shape[3]
    whole = lambda i, j, info: (0, 0)
    in_specs = [
        pl.BlockSpec((1, slots, width3), lambda i, j, info: (i ^ info[9], 0, 0)),
        pl.BlockSpec((1, 2, slots, wide), lambda i, j, info: (i ^ info[9], j, 0, 0)),
        pl.BlockSpec(z.shape, lambda i, j, info: (0, 0, 0)),
        pl.BlockSpec((1, slots, 128), lambda i, j, info: (0, 0, (i ^ info[9]) * pairs + j)),
        pl.BlockSpec((1, slots, model), lambda i, j, info: (0, 0, 0)),
        pl.BlockSpec(small.shape, whole),
        pl.BlockSpec(small.shape, whole),
        pl.BlockSpec(query_down.shape, whole),
        pl.BlockSpec(value_down.shape, whole),
    ] + [any_spec() for _ in pieces]
    args = [info, qkv, probs, z, gctx, g1, small, peer_small, query_down, value_down, *pieces]
    in_specs += [pl.BlockSpec(e.shape, whole) for e in earlier]
    args += earlier
    aliases = {}
    if full is not None:
        in_specs.append(any_spec())
        args.append(full)
        aliases = {len(args) - 1: 0}
    return pl.pallas_call(
        functools.partial(bwd_kernel, pos, len(pieces)),
        out_shape=(
            jax.ShapeDtypeStruct((4, slots, model), BF16),
            jax.ShapeDtypeStruct((1, slots, model), BF16),
            jax.ShapeDtypeStruct((query_down.shape[0], 2 * half), F32),
            jax.ShapeDtypeStruct((query_down.shape[0], 2 * half), F32),
        ),
        grid_spec=pltpu.PrefetchScalarGridSpec(
            num_scalar_prefetch=1,
            grid=(2, pairs),
            in_specs=in_specs,
            out_specs=[
                pl.BlockSpec((1, slots, model), lambda i, j, info: (info[pos], 0, 0)),
                pl.BlockSpec((1, slots, model), lambda i, j, info: (0, 0, 0)),
                pl.BlockSpec((query_down.shape[0], 2 * half), whole),
                pl.BlockSpec((query_down.shape[0], 2 * half), whole),
            ],
            scratch_shapes=[
                pltpu.VMEM((2, model + 4 * query_down.shape[0], width3), BF16),
                pltpu.VMEM((slots, width3), BF16),
                pltpu.VMEM((slots, model + 4 * query_down.shape[0]), F32),
                pltpu.SemaphoreType.DMA((2,)),
            ],
        ),
        input_output_aliases=aliases,
        compiler_params=pltpu.CompilerParams(vmem_limit_bytes=VMEM),
        cost_estimate=work(16e9),
        name="attention_backward",
    )(*args)


def place_kernel(pos, info, full_ref, *rest):
    pieces, (out_ref, sems) = rest[:-2], rest[-2:]
    copies = [
        pltpu.make_async_copy(piece.at[0], out_ref.at[info[2 + pos + n]], sems.at[n])
        for n, piece in enumerate(pieces)
    ]
    for copy in copies:
        copy.start()
    for copy in copies:
        copy.wait()


def place(pos, info, full, pieces):
    return pl.pallas_call(
        functools.partial(place_kernel, pos),
        out_shape=jax.ShapeDtypeStruct(full.shape, full.dtype),
        grid_spec=pltpu.PrefetchScalarGridSpec(
            num_scalar_prefetch=1,
            grid=(),
            in_specs=[any_spec()] + [pl.BlockSpec(memory_space=pltpu.VMEM) for _ in pieces],
            out_specs=any_spec(),
            scratch_shapes=[pltpu.SemaphoreType.DMA((len(pieces),))],
        ),
        input_output_aliases={1: 0},
        compiler_params=pltpu.CompilerParams(vmem_limit_bytes=8 << 20),
        cost_estimate=work(1e9),
        name="place",
    )(info, full, *pieces)


def sum_over_dp(a):
    size = lax.axis_size("dp")
    if size & (size - 1):
        return lax.psum(a, "dp")
    bit = 1
    while bit < size:
        a = a + lax.ppermute(a, "dp", [(i, i ^ bit) for i in range(size)])
        bit *= 2
    return a


def shards(
    tokens, live, bucket, query_weight, key_weight, value_weight, output_weight, inner_weight,
    outer_weight, query_bias, value_bias, output_bias, inner_bias, outer_bias, first_scale,
    first_bias, second_scale, second_bias, query_down, value_down, query_up, value_up, cotangent,
):
    micro, slots, model = tokens.shape
    half, hid = query_weight.shape[1], inner_weight.shape[1]
    rank = query_up.shape[0]
    me = lax.axis_index("head")
    size = lax.axis_size("dp")
    query_down, value_down = query_down.T, value_down.T
    here = jnp.stack([lax.axis_index("dp"), me]).astype(jnp.int32)
    early = pack([query_weight, key_weight, value_weight])
    late, small, vec, info = prepare(
        bucket, here, output_weight.T, inner_weight, outer_weight.T, query_up, value_up, query_bias, value_bias,
        inner_bias, output_bias, outer_bias, first_scale, first_bias, second_scale, second_bias,
    )
    peer_small = lax.ppermute(small, "head", SWAP)

    if by_permutes(size):
        go = permuter(size)

        def plane(pair, flip, hold=None):
            one, two = go(pair, "first"), go(pair, "second")
            via, last = (two, "first") if flip else (one, "second")
            return [pair, one, two, go(via if hold is None else then(via, hold), last)]

        def both_cores(blocks):
            return blocks + [go(block, "core") for block in blocks]

        ring = spread_ring(early, size)
        wqkv = []
        for k in (0, 2):
            wqkv += both_cores(plane(jnp.stack(ring[k : k + 2]), k == 2))
        ring = spread_ring(then(late, ring[1]), size)
        near = plane(jnp.stack(ring[:2]), False)
        distant = jnp.stack(ring[2:])
    else:
        wqkv = gather_whole(early)
    first = run_fwd(0, info, tokens, wqkv, small, peer_small, query_down, value_down, live)
    if by_permutes(size):
        distant = plane(distant, True, first[2])
        wrest = both_cores(then(near, first[2]))
    else:
        wrest = gather_whole(late)
    second = run_fwd(1, then(info, first[2]), tokens, wqkv, small, peer_small, query_down, value_down, live)
    if by_permutes(size):
        wrest += both_cores(then(distant[:3], first[2]) + [then(distant[3], second[2])])
    acts = grads = None
    shared = (wqkv, small, peer_small, query_down, value_down)
    ctx = then(first[2], second[2])
    acts, a0, g1_0, gctx0 = run_mid(0, info, tokens, ctx, cotangent, live, wrest, small, peer_small, vec, acts)
    p_a0 = lax.ppermute(a0, "head", SWAP)
    ctx = then(second[2], a0)
    acts, a1, g1_1, gctx1 = run_mid(1, info, tokens, ctx, cotangent, live, wrest, small, peer_small, vec, acts)
    p_a1 = lax.ppermute(a1, "head", SWAP)
    gctx0 = then(gctx0, (p_a0, a1))
    grads, g0, *lora = run_bwd(0, info, *first, gctx0, g1_0, *shared, grads)
    p_g0 = lax.ppermute(g0, "head", SWAP)
    gctx1 = then(gctx1, (p_a1, g0))
    grads, g1, mine, other = run_bwd(1, info, *second, gctx1, g1_1, *shared, grads, lora)
    received = lax.ppermute(other, "head", SWAP)
    p_g1 = lax.ppermute(then(g1, (received, p_g0)), "head", SWAP)
    lora = sum_over_dp(mine + received)
    acts = place(0, info, acts, [p_a0, p_a1])
    grads = place(0, info, grads, [p_g0])
    p_g1 = then(p_g1, (acts, grads, lora))
    grads = place(1, info, grads, [p_g1])
    return acts, grads, lora[:, :half], lora[:, half:]


def solution(mesh):
    return jax.shard_map(
        shards,
        mesh=mesh,
        in_specs=(
            P(None, "dp", None), P(None, "dp"), P(),
            P("dp", "head"), P("dp", "head"), P("dp", "head"), P("head", "dp"), P("dp", "head"), P("head", "dp"),
            P("head"), P("head"), P(), P("head"), P(), P(), P(), P(), P(),
            P(), P(), P(None, "head"), P(None, "head"), P(None, "dp", None),
        ),
        out_specs=(P(None, "dp", None), P(None, "dp", None), P(None, "head"), P(None, "head")),
        check_vma=False,
    )
```

```python
import functools
import math

import jax
import jax.numpy as jnp
from jax import lax
from jax.experimental import pallas as pl
from jax.experimental.pallas import tpu as pltpu
from jax.sharding import PartitionSpec as P

F32, BF16 = jnp.float32, jnp.bfloat16
EPS = 1e-5
MASKED = -1e9
NT = (((1,), (1,)), ((), ()))
TN = (((0,), (0,)), ((), ()))
NN = (((1,), (0,)), ((), ()))
SWAP = [(0, 1), (1, 0)]
RSQRT2 = 1.0 / math.sqrt(2.0)
PHI0 = 1.0 / math.sqrt(2.0 * math.pi)
ONCE = pl.Buffered(1)
VMEM = 60 << 20


def work(flops):
    return pl.CostEstimate(flops=int(flops), bytes_accessed=8 << 20, transcendentals=0)


def chip_table(size, move):
    deep = size // 4

    def index(z, x, c, y):
        return ((z % deep) * 4 + x * 2 + c) * 2 + y

    return [
        (index(z, x, c, y), index(*move(z, x, c, y)))
        for z in range(deep)
        for x in range(2)
        for c in range(2)
        for y in range(2)
    ]


def by_permutes(size):
    return size == 16


def permuter(size):
    tables = {
        "first": chip_table(size, lambda z, x, c, y: (z, x, c, 1 - y) if c else (z, 1 - x, c, y)),
        "second": chip_table(size, lambda z, x, c, y: (z, 1 - x, c, y) if c else (z, x, c, 1 - y)),
        "ring": chip_table(size, lambda z, x, c, y: (z + 1, x, c, y)),
        "core": chip_table(size, lambda z, x, c, y: (z, x, 1 - c, y)),
    }
    return lambda a, which: lax.ppermute(a, ("dp", "head"), tables[which])


def then(value, done):
    return lax.optimization_barrier((value, done))[0]


def spread_ring(shard, size):
    go, blocks = permuter(size), [shard]
    for _ in range(3):
        blocks.append(go(blocks[-1], "ring"))
    return blocks


def gather_whole(shard):
    whole = lax.all_gather(shard, ("head", "dp"), axis=0, tiled=True)
    return [whole.reshape(2, -1, shard.shape[1])]


def sub_pieces(refs, info):
    dp, y = info[8], info[9]
    if len(refs) == 1:
        return [(refs[0].at[y ^ h], h, 0) for h in range(2)]
    rows = refs[0].shape[1]
    z, x, core = dp >> 2, (dp >> 1) & 1, dp & 1
    out = []
    for k in range(4):
        deep = ((z + 4 - k) & 3) << 2
        for side in range(2):
            c = core ^ side
            for j in range(4):
                dx, dy = ((0, 0), (1 - c, c), (c, 1 - c), (1, 1))[j]
                row = (deep + ((x ^ dx) << 1) + c) * rows
                out.append((refs[(k // 2) * 8 + side * 4 + j].at[k % 2], dy, pl.multiple_of(row, rows)))
    return out


def fetch(refs, info, parts, sems):
    for p, (start, cols, dest) in enumerate(parts):
        for ref, dy, row in sub_pieces(refs, info):
            view = ref.at[:, pl.ds(start, cols)]
            pltpu.make_async_copy(view, dest(info[9] ^ dy, row, ref.shape[0]), sems.at[2 * p + dy]).start()


def wait_for(buf, sem):
    pltpu.make_async_copy(buf, buf, sem).wait()


def side_by_side(buf, count):
    return lambda h, row, rows: buf.at[pl.ds(row, rows), pl.ds(pl.multiple_of(h * count, 128), count)]


def stacked(buf):
    return lambda h, row, rows: buf.at[h, pl.ds(row, rows)]


def adapter_rows(own_ref, peer_ref, turn, rank):
    small = jnp.where(turn == 0, own_ref[: 2 * rank + 2], peer_ref[: 2 * rank + 2])
    uq, uv = split(2.0 * small[:rank]), split(2.0 * small[rank : 2 * rank])
    none = jnp.zeros((2 * rank, small.shape[1]), BF16)
    query = jnp.concatenate([uq[0], uq[1], none], axis=0)
    value = jnp.concatenate([none, uv[0], uv[1]], axis=0)
    rows = jnp.concatenate([query, jnp.zeros_like(query), value], axis=1)
    return rows, small[2 * rank : 2 * rank + 1], small[2 * rank + 1 : 2 * rank + 2]


def mm(a, b, dims=NN):
    return lax.dot_general(a, b, dims, preferred_element_type=F32)


def lane_masks():
    lane = lax.broadcasted_iota(jnp.int32, (1, 128), 1)
    one, zero = jnp.ones((1, 128), F32), jnp.zeros((1, 128), F32)
    low = jnp.where(lane < 64, one, zero)
    return low.astype(BF16), (one - low).astype(BF16)


def pack_kernel(*refs):
    out_ref, cols = refs[-1], refs[0].shape[1]
    for k, ref in enumerate(refs[:-1]):
        out_ref[:, k * cols : (k + 1) * cols] = ref[...]


def pack(parts):
    rows, cols = parts[0].shape
    return pl.pallas_call(
        pack_kernel,
        out_shape=jax.ShapeDtypeStruct((rows, len(parts) * cols), parts[0].dtype),
        name="pack",
    )(*parts)


def prepare_kernel(
    bucket, here, wo_ref, wi_ref, wt_ref, uq_ref, uv_ref, qb_ref, vb_ref, ib_ref,
    b0, b1, b2, b3, b4, b5, late_ref, small_ref, vec_ref, info_ref,
):
    half, hid = wo_ref.shape[1], wi_ref.shape[1]
    late_ref[:, :half] = wo_ref[...]
    late_ref[:, half : half + hid] = wi_ref[...]
    late_ref[:, half + hid :] = wt_ref[...]
    rank = uq_ref.shape[0]
    small_ref[:rank] = uq_ref[...]
    small_ref[rank : 2 * rank] = uv_ref[...]
    small_ref[2 * rank : 2 * rank + 1] = qb_ref[...].astype(F32).reshape(1, half)
    small_ref[2 * rank + 1 : 2 * rank + 2] = vb_ref[...].astype(F32).reshape(1, half)
    inner = ib_ref[...].astype(F32).reshape(1, hid)
    for k in range(hid // half):
        small_ref[2 * rank + 2 + k : 2 * rank + 3 + k] = inner[:, k * half : (k + 1) * half]
    for k, ref in enumerate((b0, b1, b2, b3, b4, b5)):
        vec_ref[k : k + 1] = ref[...].astype(F32).reshape(1, -1)
    count = bucket.shape[0]
    for m in range(count):
        place_of = 0
        for other in range(count):
            place_of += jnp.where(bucket[other] > bucket[m], 1, 0)
        outside = jnp.where((place_of == 0) | (place_of == count - 1), 0, 1)
        second = jnp.where(place_of >= count // 2, 1, 0)
        info_ref[(outside ^ here[1]) * 2 + second] = m
        info_ref[count + m] = bucket[m]
    info_ref[2 * count] = here[0]
    info_ref[2 * count + 1] = here[1]


def prepare(bucket, here, *arrays):
    wo, wi, wt, uq = arrays[:4]
    rows, half = wo.shape
    smem = pl.BlockSpec(memory_space=pltpu.SMEM)
    vmem = pl.BlockSpec(memory_space=pltpu.VMEM)
    return pl.pallas_call(
        prepare_kernel,
        out_shape=(
            jax.ShapeDtypeStruct((rows, half + 2 * wi.shape[1]), BF16),
            jax.ShapeDtypeStruct((2 * uq.shape[0] + 2 + wi.shape[1] // half, half), F32),
            jax.ShapeDtypeStruct((8, arrays[8].shape[0]), F32),
            jax.ShapeDtypeStruct((2 * bucket.shape[0] + 2,), jnp.int32),
        ),
        in_specs=[smem, smem] + [vmem] * len(arrays),
        out_specs=(vmem, vmem, vmem, smem),
        cost_estimate=work(2e9),
        name="prepare",
    )(bucket, here, *arrays)


def split(a):
    high = a.astype(BF16)
    return high, (a - high.astype(F32)).astype(BF16)


def fwd_kernel(pos, count, info, x_ref, own_ref, peer_ref, qd_ref, vd_ref, live_ref, *rest):
    pieces, (qkv_ref, p_ref, ctx_ref, z_ref, w, wide_x, bias, sems) = rest[:count], rest[count:]
    slots, model, width = x_ref.shape[1], x_ref.shape[2], own_ref.shape[1]
    rank = qd_ref.shape[0]
    span, turn, pair = info[4 + info[pos]], pl.program_id(0), pl.program_id(1)
    half = info[9] ^ turn

    @pl.when((turn == 0) & (pair == 0))
    def _():
        fetch(pieces, info, [(0, 3 * width, stacked(w))], sems)
        t = lax.broadcasted_iota(jnp.int32, (slots, slots), 0)
        s = lax.broadcasted_iota(jnp.int32, (slots, slots), 1)
        ok = ((t ^ s) < span) & (live_ref[pl.ds(info[pos], 1), :] == 1)
        bias[...] = jnp.where(ok, 0.0, MASKED)
        down = jnp.concatenate([qd_ref[...], vd_ref[...]], axis=0)
        z = mm(x_ref[0], down, NT).astype(BF16)
        z_ref[0] = z
        wide_x[:, :model] = x_ref[0]
        wide_x[:, model:] = jnp.concatenate([z[:, :rank], z[:, :rank], z[:, rank:], z[:, rank:]], axis=1)

    @pl.when(pair == 0)
    def _():
        wait_for(w.at[half, :model], sems.at[turn])
        rows, bq, bv = adapter_rows(own_ref, peer_ref, turn, rank)
        w[half, model:] = rows
        for k, shift in enumerate((bq, 0.0, bv)):
            cols = slice(k * width, (k + 1) * width)
            qkv_ref[0, :, cols] = (mm(wide_x[...], w[half, :, cols]) + shift).astype(BF16)

    masks = lane_masks()
    col = pl.multiple_of(pair * 128, 128)

    def attend(size):
        for b in range(slots // size):
            rows = slice(b * size, (b + 1) * size)
            q2 = qkv_ref[0, rows, pl.ds(col, 128)]
            k2 = qkv_ref[0, rows, pl.ds(width + col, 128)] * jnp.asarray(0.125, BF16)
            v2 = qkv_ref[0, rows, pl.ds(2 * width + col, 128)]
            acc = None
            for e in range(2):
                s = mm(q2, k2 * masks[e], NT) + bias[rows, rows]
                s = jnp.exp(s - jnp.max(s, axis=1, keepdims=True))
                probs = (s * (1.0 / jnp.sum(s, axis=1, keepdims=True))).astype(BF16)
                p_ref[0, e, rows, :size] = probs
                part = mm(probs, v2 * masks[e])
                acc = part if acc is None else acc + part
            ctx_ref[0, rows] = acc.astype(BF16)

    attend(block_size(pos, slots))


def block_size(pos, slots):
    return slots if pos == 0 else slots // 2


def any_spec():
    return pl.BlockSpec(memory_space=pl.ANY)


def run_fwd(pos, info, tokens, pieces, small, peer_small, query_down, value_down, live):
    micro, slots, model = tokens.shape
    half = small.shape[1]
    pairs, wide = half // 128, slots if pos == 0 else slots // 2
    whole = lambda i, j, info: (0, 0)
    return pl.pallas_call(
        functools.partial(fwd_kernel, pos, len(pieces)),
        out_shape=(
            jax.ShapeDtypeStruct((2, slots, 3 * half), BF16),
            jax.ShapeDtypeStruct((2, 2 * pairs, slots, wide), BF16),
            jax.ShapeDtypeStruct((1, slots, model), BF16),
            jax.ShapeDtypeStruct((1, slots, 2 * query_down.shape[0]), BF16),
        ),
        grid_spec=pltpu.PrefetchScalarGridSpec(
            num_scalar_prefetch=1,
            grid=(2, pairs),
            in_specs=[
                pl.BlockSpec((1, slots, model), lambda i, j, info: (info[pos], 0, 0)),
                pl.BlockSpec(small.shape, whole),
                pl.BlockSpec(small.shape, whole),
                pl.BlockSpec(query_down.shape, whole),
                pl.BlockSpec(value_down.shape, whole),
                pl.BlockSpec(live.shape, whole),
            ]
            + [any_spec() for _ in pieces],
            out_specs=[
                pl.BlockSpec((1, slots, 3 * half), lambda i, j, info: (i ^ info[9], 0, 0)),
                pl.BlockSpec((1, 2, slots, wide), lambda i, j, info: (i ^ info[9], j, 0, 0)),
                pl.BlockSpec((1, slots, 128), lambda i, j, info: (0, 0, (i ^ info[9]) * pairs + j)),
                pl.BlockSpec((1, slots, 2 * query_down.shape[0]), lambda i, j, info: (0, 0, 0)),
            ],
            scratch_shapes=[
                pltpu.VMEM((2, model + 4 * query_down.shape[0], 3 * half), BF16),
                pltpu.VMEM((slots, model + 4 * query_down.shape[0]), BF16),
                pltpu.VMEM((slots, slots), F32),
                pltpu.SemaphoreType.DMA((2,)),
            ],
        ),
        compiler_params=pltpu.CompilerParams(vmem_limit_bytes=VMEM),
        cost_estimate=work(12e9),
        name="attention_forward",
    )(info, tokens, small, peer_small, query_down, value_down, live, *pieces)


def gelu_parts(u):
    cdf = 0.5 * (1.0 + lax.erf(u * RSQRT2))
    pdf = jnp.exp(-0.5 * u * u) * PHI0
    return u * cdf, cdf + u * pdf


def norm(rows):
    c = rows - jnp.mean(rows, axis=1, keepdims=True)
    rstd = lax.rsqrt(jnp.mean(c * c, axis=1, keepdims=True) + EPS)
    return c * rstd, rstd


def norm_back(e, xhat, rstd):
    return rstd * (
        e - jnp.mean(e, axis=1, keepdims=True) - xhat * jnp.mean(e * xhat, axis=1, keepdims=True)
    )


def mid_kernel(pos, count, info, x_ref, ctx_ref, cot_ref, live_ref, own_ref, peer_ref, vec_ref, *rest):
    pieces = rest[:count]
    full_ref, act_ref, g1_ref, gctx_ref, wo, wi, wt, slope, xhat, acc, low, hidden, bi_ref, sems = rest[-14:]
    model = x_ref.shape[2]
    half, units = model // 2, wi.shape[1]
    hid, step = units // 2, 768
    parts = [
        (0, half, side_by_side(wo, half)),
        (half, hid, side_by_side(wi, hid)),
        (half + hid, hid, side_by_side(wt, hid)),
    ]
    fetch(pieces, info, parts, sems)
    first = own_ref.shape[0] - hid // half
    for h in range(2):
        small = jnp.where(info[9] == h, own_ref[...], peer_ref[...])
        for k in range(hid // half):
            cols = h * hid + k * half
            bi_ref[:, cols : cols + half] = small[first + k : first + k + 1]
    bo, b2 = vec_ref[0:1], vec_ref[1:2]
    s1, t1, s2, t2 = vec_ref[2:3], vec_ref[3:4], vec_ref[4:5], vec_ref[5:6]
    for h in range(2):
        wait_for(wo.at[:, h * half : (h + 1) * half], sems.at[0 + h])
    xh, rstd1 = norm(x_ref[0].astype(F32) + bo + mm(ctx_ref[0], wo[...], NT))
    xhat[...] = xh
    low[...] = (xh * s1 + t1).astype(BF16)
    for h in range(2):
        wait_for(wi.at[:, h * hid : (h + 1) * hid], sems.at[2 + h])

    def up(j, _):
        cols = pl.ds(pl.multiple_of(j * step, step), step)
        a, d = gelu_parts(mm(low[...], wi[:, cols]) + bi_ref[:, cols])
        slope[:, cols] = d
        hidden[:, cols] = a.astype(BF16)
        return 0

    lax.fori_loop(0, units // step, up, 0)
    for h in range(2):
        wait_for(wt.at[:, h * hid : (h + 1) * hid], sems.at[4 + h])
    xh2, rstd2 = norm(mm(hidden[...], wt[...], NT) + (xhat[...] * s1 + t1) + b2)
    act_ref[0] = (xh2 * s2 + t2).astype(BF16)
    full_ref[0] = act_ref[0]
    live = jnp.broadcast_to(live_ref[pl.ds(info[pos], 1), :].astype(F32), (8, live_ref.shape[1])).T[:, :1]
    g2 = norm_back(cot_ref[0].astype(F32) * live * s2, xh2, rstd2)
    low[...] = g2.astype(BF16)
    acc[...] = g2

    def down(j, _):
        cols = pl.ds(pl.multiple_of(j * step, step), step)
        hidden[:, cols] = (mm(low[...], wt[:, cols]) * slope[:, cols]).astype(BF16)
        return 0

    lax.fori_loop(0, units // step, down, 0)
    g1 = norm_back((acc[...] + mm(hidden[...], wi[...], NT)) * s1, xhat[...], rstd1)
    g1_ref[0] = g1
    gctx_ref[0] = mm(g1.astype(BF16), wo[...]).astype(BF16)


def run_mid(pos, info, tokens, ctx, cot, live, pieces, small, peer_small, vec, full):
    micro, slots, model = tokens.shape
    units = pieces[0].shape[-1] - model // 2
    own = lambda i, info: (info[pos], 0, 0)
    same = lambda i, info: (0, 0)
    in_specs = [
        pl.BlockSpec((1, slots, model), own),
        pl.BlockSpec((1, slots, model), lambda i, info: (0, 0, 0)),
        pl.BlockSpec((1, slots, model), own),
        pl.BlockSpec(live.shape, same, pipeline_mode=ONCE),
        pl.BlockSpec(small.shape, same, pipeline_mode=ONCE),
        pl.BlockSpec(small.shape, same, pipeline_mode=ONCE),
        pl.BlockSpec((8, model), same, pipeline_mode=ONCE),
    ] + [any_spec() for _ in pieces]
    args = [info, tokens, ctx, cot, live, small, peer_small, vec, *pieces]
    aliases = {}
    if full is not None:
        in_specs.append(any_spec())
        args.append(full)
        aliases = {len(args) - 1: 0}
    first = pl.BlockSpec((1, slots, model), lambda i, info: (0, 0, 0))
    return pl.pallas_call(
        functools.partial(mid_kernel, pos, len(pieces)),
        out_shape=(
            jax.ShapeDtypeStruct(tokens.shape, BF16),
            jax.ShapeDtypeStruct((1, slots, model), BF16),
            jax.ShapeDtypeStruct((1, slots, model), F32),
            jax.ShapeDtypeStruct((1, slots, model), BF16),
        ),
        grid_spec=pltpu.PrefetchScalarGridSpec(
            num_scalar_prefetch=1,
            grid=(1,),
            in_specs=in_specs,
            out_specs=[pl.BlockSpec((1, slots, model), own), first, first, first],
            scratch_shapes=[
                pltpu.VMEM((model, model), BF16),
                pltpu.VMEM((model, units), BF16),
                pltpu.VMEM((model, units), BF16),
                pltpu.VMEM((slots, units), F32),
                pltpu.VMEM((slots, model), F32),
                pltpu.VMEM((slots, model), F32),
                pltpu.VMEM((slots, model), BF16),
                pltpu.VMEM((slots, units), BF16),
                pltpu.VMEM((1, units), F32),
                pltpu.SemaphoreType.DMA((6,)),
            ],
        ),
        input_output_aliases=aliases,
        compiler_params=pltpu.CompilerParams(vmem_limit_bytes=VMEM),
        cost_estimate=work(24e9),
        name="feed_forward",
    )(*args)


def bwd_kernel(
    pos, count, info, qkv_ref, p_ref, z_ref, gctx_ref, g1_ref, own_ref, peer_ref, qd_ref, vd_ref, *rest
):
    pieces = rest[:count]
    full_ref, grad_ref, mine_ref, other_ref, w, dqkv, total, sems = rest[-8:]
    earlier = rest[count : count + 2]
    slots, width = qkv_ref.shape[1], own_ref.shape[1]
    turn, pair = pl.program_id(0), pl.program_id(1)
    half = info[9] ^ turn
    masks = lane_masks()

    @pl.when((turn == 0) & (pair == 0))
    def _():
        fetch(pieces, info, [(0, 3 * width, stacked(w))], sems)

    col = pl.multiple_of(pair * 128, 128)

    def attend(size):
        for b in range(slots // size):
            rows = slice(b * size, (b + 1) * size)
            q2 = qkv_ref[0, rows, pl.ds(col, 128)] * jnp.asarray(0.125, BF16)
            k2 = qkv_ref[0, rows, pl.ds(width + col, 128)] * jnp.asarray(0.125, BF16)
            v2 = qkv_ref[0, rows, pl.ds(2 * width + col, 128)]
            g2 = gctx_ref[0, rows]
            dq = dk = dv = jnp.zeros((size, 128), F32)
            joined = []
            for e in range(2):
                probs = p_ref[0, e, rows, :size]
                dp = mm(g2, v2 * masks[e], NT)
                dv = dv + mm(probs, g2 * masks[e], TN)
                p32 = probs.astype(F32)
                pd = p32 * dp
                ds = (pd - p32 * jnp.sum(pd, axis=1, keepdims=True)).astype(BF16)
                if size == slots:
                    joined.append(ds)
                else:
                    dq = dq + mm(ds, k2 * masks[e])
                    dk = dk + mm(ds, q2 * masks[e], TN)
            if joined:
                ds = jnp.concatenate(joined, axis=1)
                dq = mm(ds, jnp.concatenate([k2 * masks[0], k2 * masks[1]], axis=0))
                dk = mm(ds, q2, TN)
                dk = jnp.where(lax.broadcasted_iota(jnp.int32, (1, 128), 1) < 64, dk[:size], dk[size:])
            dqkv[rows, pl.ds(col, 128)] = dq.astype(BF16)
            dqkv[rows, pl.ds(width + col, 128)] = dk.astype(BF16)
            dqkv[rows, pl.ds(2 * width + col, 128)] = dv.astype(BF16)

    attend(block_size(pos, slots))

    @pl.when(pair == width // 128 - 1)
    def _():
        rank, model = qd_ref.shape[0], g1_ref.shape[2]
        wait_for(w.at[half, :model], sems.at[turn])
        w[half, model:] = adapter_rows(own_ref, peer_ref, turn, rank)[0]
        part = mm(dqkv[...], w[half], NT)
        lora = 2.0 * mm(z_ref[0], dqkv[...], TN)
        lora = jnp.concatenate([lora[:rank, :width], lora[rank:, 2 * width :]], axis=1)

        @pl.when(turn == 0)
        def _():
            mine_ref[...] = lora if pos == 0 else lora + earlier[0][...]
            total[:, :model] = g1_ref[0] + part[:, :model]
            total[:, model:] = part[:, model:]

        @pl.when(turn == 1)
        def _():
            other_ref[...] = lora if pos == 0 else lora + earlier[1][...]
            t = total[:, model:] + part[:, model:]
            tq, tv = split(t[:, :rank] + t[:, rank : 2 * rank]), split(t[:, 2 * rank : 3 * rank] + t[:, 3 * rank :])
            down = jnp.concatenate([qd_ref[...], vd_ref[...]] * 2, axis=0)
            sums = total[:, :model] + part[:, :model]
            sums = sums + mm(jnp.concatenate([tq[0], tv[0], tq[1], tv[1]], axis=1), down)
            grad_ref[0] = sums.astype(BF16)
            full_ref[0] = grad_ref[0]


def run_bwd(pos, info, qkv, probs, ctx, z, gctx, g1, pieces, small, peer_small, query_down, value_down, full, earlier=()):
    _, slots, width3 = qkv.shape
    half, model = width3 // 3, g1.shape[2]
    pairs, wide = half // 128, probs.shape[3]
    whole = lambda i, j, info: (0, 0)
    in_specs = [
        pl.BlockSpec((1, slots, width3), lambda i, j, info: (i ^ info[9], 0, 0)),
        pl.BlockSpec((1, 2, slots, wide), lambda i, j, info: (i ^ info[9], j, 0, 0)),
        pl.BlockSpec(z.shape, lambda i, j, info: (0, 0, 0)),
        pl.BlockSpec((1, slots, 128), lambda i, j, info: (0, 0, (i ^ info[9]) * pairs + j)),
        pl.BlockSpec((1, slots, model), lambda i, j, info: (0, 0, 0)),
        pl.BlockSpec(small.shape, whole),
        pl.BlockSpec(small.shape, whole),
        pl.BlockSpec(query_down.shape, whole),
        pl.BlockSpec(value_down.shape, whole),
    ] + [any_spec() for _ in pieces]
    args = [info, qkv, probs, z, gctx, g1, small, peer_small, query_down, value_down, *pieces]
    in_specs += [pl.BlockSpec(e.shape, whole) for e in earlier]
    args += earlier
    aliases = {}
    if full is not None:
        in_specs.append(any_spec())
        args.append(full)
        aliases = {len(args) - 1: 0}
    return pl.pallas_call(
        functools.partial(bwd_kernel, pos, len(pieces)),
        out_shape=(
            jax.ShapeDtypeStruct((4, slots, model), BF16),
            jax.ShapeDtypeStruct((1, slots, model), BF16),
            jax.ShapeDtypeStruct((query_down.shape[0], 2 * half), F32),
            jax.ShapeDtypeStruct((query_down.shape[0], 2 * half), F32),
        ),
        grid_spec=pltpu.PrefetchScalarGridSpec(
            num_scalar_prefetch=1,
            grid=(2, pairs),
            in_specs=in_specs,
            out_specs=[
                pl.BlockSpec((1, slots, model), lambda i, j, info: (info[pos], 0, 0)),
                pl.BlockSpec((1, slots, model), lambda i, j, info: (0, 0, 0)),
                pl.BlockSpec((query_down.shape[0], 2 * half), whole),
                pl.BlockSpec((query_down.shape[0], 2 * half), whole),
            ],
            scratch_shapes=[
                pltpu.VMEM((2, model + 4 * query_down.shape[0], width3), BF16),
                pltpu.VMEM((slots, width3), BF16),
                pltpu.VMEM((slots, model + 4 * query_down.shape[0]), F32),
                pltpu.SemaphoreType.DMA((2,)),
            ],
        ),
        input_output_aliases=aliases,
        compiler_params=pltpu.CompilerParams(vmem_limit_bytes=VMEM),
        cost_estimate=work(16e9),
        name="attention_backward",
    )(*args)


def place_kernel(pos, info, full_ref, *rest):
    pieces, (out_ref, sems) = rest[:-2], rest[-2:]
    copies = [
        pltpu.make_async_copy(piece.at[0], out_ref.at[info[2 + pos + n]], sems.at[n])
        for n, piece in enumerate(pieces)
    ]
    for copy in copies:
        copy.start()
    for copy in copies:
        copy.wait()


def place(pos, info, full, pieces):
    return pl.pallas_call(
        functools.partial(place_kernel, pos),
        out_shape=jax.ShapeDtypeStruct(full.shape, full.dtype),
        grid_spec=pltpu.PrefetchScalarGridSpec(
            num_scalar_prefetch=1,
            grid=(),
            in_specs=[any_spec()] + [pl.BlockSpec(memory_space=pltpu.VMEM) for _ in pieces],
            out_specs=any_spec(),
            scratch_shapes=[pltpu.SemaphoreType.DMA((len(pieces),))],
        ),
        input_output_aliases={1: 0},
        compiler_params=pltpu.CompilerParams(vmem_limit_bytes=8 << 20),
        cost_estimate=work(1e9),
        name="place",
    )(info, full, *pieces)


def sum_over_dp(a):
    size = lax.axis_size("dp")
    if size & (size - 1):
        return lax.psum(a, "dp")
    bit = 1
    while bit < size:
        a = a + lax.ppermute(a, "dp", [(i, i ^ bit) for i in range(size)])
        bit *= 2
    return a


def shards(
    tokens, live, bucket, query_weight, key_weight, value_weight, output_weight, inner_weight,
    outer_weight, query_bias, value_bias, output_bias, inner_bias, outer_bias, first_scale,
    first_bias, second_scale, second_bias, query_down, value_down, query_up, value_up, cotangent,
):
    micro, slots, model = tokens.shape
    half, hid = query_weight.shape[1], inner_weight.shape[1]
    rank = query_up.shape[0]
    me = lax.axis_index("head")
    size = lax.axis_size("dp")
    query_down, value_down = query_down.T, value_down.T
    here = jnp.stack([lax.axis_index("dp"), me]).astype(jnp.int32)
    early = pack([query_weight, key_weight, value_weight])
    late, small, vec, info = prepare(
        bucket, here, output_weight.T, inner_weight, outer_weight.T, query_up, value_up, query_bias, value_bias,
        inner_bias, output_bias, outer_bias, first_scale, first_bias, second_scale, second_bias,
    )
    peer_small = lax.ppermute(small, "head", SWAP)

    if by_permutes(size):
        go = permuter(size)

        def plane(pair, flip, hold=None):
            one, two = go(pair, "first"), go(pair, "second")
            via, last = (two, "first") if flip else (one, "second")
            return [pair, one, two, go(via if hold is None else then(via, hold), last)]

        def both_cores(blocks):
            return blocks + [go(block, "core") for block in blocks]

        ring = spread_ring(early, size)
        wqkv = []
        for k in (0, 2):
            wqkv += both_cores(plane(jnp.stack(ring[k : k + 2]), k == 2))
        ring = spread_ring(then(late, ring[1]), size)
        near = plane(jnp.stack(ring[:2]), False)
        distant = jnp.stack(ring[2:])
    else:
        wqkv = gather_whole(early)
    first = run_fwd(0, info, tokens, wqkv, small, peer_small, query_down, value_down, live)
    if by_permutes(size):
        distant = plane(distant, True, first[2])
        wrest = both_cores(then(near, first[2]))
    else:
        wrest = gather_whole(late)
    second = run_fwd(1, then(info, first[2]), tokens, wqkv, small, peer_small, query_down, value_down, live)
    if by_permutes(size):
        wrest += both_cores(then(distant[:3], first[2]) + [then(distant[3], second[2])])
    acts = grads = None
    shared = (wqkv, small, peer_small, query_down, value_down)
    ctx = then(first[2], second[2])
    acts, a0, g1_0, gctx0 = run_mid(0, info, tokens, ctx, cotangent, live, wrest, small, peer_small, vec, acts)
    p_a0 = lax.ppermute(a0, "head", SWAP)
    grads, g0, *lora = run_bwd(0, info, *first, gctx0, g1_0, *shared, grads)
    p_g0 = lax.ppermute(g0, "head", SWAP)
    ctx = then(second[2], (p_a0, g0))
    acts, a1, g1_1, gctx1 = run_mid(1, info, tokens, ctx, cotangent, live, wrest, small, peer_small, vec, acts)
    p_a1 = lax.ppermute(a1, "head", SWAP)
    gctx1 = then(gctx1, (p_g0, a1))
    grads, g1, mine, other = run_bwd(1, info, *second, gctx1, g1_1, *shared, grads, lora)
    received = lax.ppermute(other, "head", SWAP)
    p_g1 = lax.ppermute(then(g1, (received, p_a1)), "head", SWAP)
    lora = sum_over_dp(mine + received)
    acts = place(0, info, acts, [p_a0, p_a1])
    grads = place(0, info, grads, [p_g0])
    p_g1 = then(p_g1, (acts, grads, lora))
    grads = place(1, info, grads, [p_g1])
    return acts, grads, lora[:, :half], lora[:, half:]


def solution(mesh):
    return jax.shard_map(
        shards,
        mesh=mesh,
        in_specs=(
            P(None, "dp", None), P(None, "dp"), P(),
            P("dp", "head"), P("dp", "head"), P("dp", "head"), P("head", "dp"), P("dp", "head"), P("head", "dp"),
            P("head"), P("head"), P(), P("head"), P(), P(), P(), P(), P(),
            P(), P(), P(None, "head"), P(None, "head"), P(None, "dp", None),
        ),
        out_specs=(P(None, "dp", None), P(None, "dp", None), P(None, "head"), P(None, "head")),
        check_vma=False,
    )
```
